256 devices in a mesh: gx: 8 (over z_hi, core), gy: 8 (over y, z_lo), gz: 4 (over x).
Axes of the slice: x: 4, y: 4, z: 8 (z_hi: 4, z_lo: 2; z = z_hi * 2 + z_lo), core: 2. Of those that a mesh axis runs over, the one named last changes fastest.
Arguments:
- pressure_prev: float32 [128, 192, 1024], P('gx', 'gy', 'gz'), may hold values from -6 to 6
- pressure_now: float32 [128, 192, 1024], P('gx', 'gy', 'gz'), may hold values from -6 to 6
- material: int32 [128, 192, 1024], P('gx', 'gy', 'gz'), may hold values from 0 to 7
- speed_table: float32 [8], replicated, may hold values from 0.05 to 0.32
- anchors: int32 [8, 8, 512], P('gx', 'gy', 'gz'), may hold values from 0 to 53496, as said below
- counts: int32 [8, 8, 4], P('gx', 'gy', 'gz'), may hold values from 64 to 128, as said below
- w_in: bfloat16 [512, 1024], replicated, may hold values from -0.25 to 0.25
- w_out: bfloat16 [1024, 512], replicated, may hold values from -0.1875 to 0.1875
Outputs:
- final_pressure: float32 [128, 192, 1024], P('gx', 'gy', 'gz')
- grad_in: float32 [512, 1024], P('gx')
- grad_out: float32 [1024, 512], P('gx')
The draws below stay inside these ranges and needn't reach their ends.
Inputs may be any that keep to these rules, and one draw needn't show every extreme that they name: `anchors`: each entry is i * 24 * 256 + j * 256 + k with i <= 8, j <= 16, k <= 248, so every patch lies inside its brick; entries of a brick may repeat. The used slots of a brick are its first counts slots.
All inputs are finite; a program needn't handle non-finite values.
Results may differ from the reference program's by a relative error of at most 0.0017.
Values sent between devices are 32-bit elements; how exact they have to be, the bound alone decides.
A program may use at most 64 MiB of HBM per device.

```python
import jax
import jax.numpy as jnp
from jax import lax

CX = 16
CY = 24
CZ = 256
PB = 128
STEPS = 8
PATCH = 8
HID = 1024
NMAT = 8
D = 512
NX = 128
NY = 192
NZ = 1024
N_GX = 8
N_GY = 8
N_GZ = 4


def draw_anchors(key, part):
    key_x, key_y, key_z = jax.random.split(jax.random.fold_in(key, 11), 3)
    shape = (N_GX, N_GY, N_GZ * PB)
    first_x = jax.random.randint(key_x, shape, 0, CX - PATCH + 1)
    first_y = jax.random.randint(key_y, shape, 0, CY - PATCH + 1)
    first_z = jax.random.randint(key_z, shape, 0, CZ - PATCH + 1)
    index = first_x * CY * CZ + first_y * CZ + first_z
    corner = (CX - PATCH) * CY * CZ + (CY - PATCH) * CZ + CZ - PATCH
    leading = jnp.arange(N_GZ * PB) % PB == 0
    return jnp.where(leading[None, None, :], corner, index).astype(jnp.int32)


def draw_counts(key, part):
    key_a, key_b, key_c = jax.random.split(jax.random.fold_in(key, 23), 3)
    bricks = N_GX * N_GY * N_GZ
    first = jax.random.randint(key_a, (bricks,), 1, PB + 1)
    second = jax.random.randint(key_b, (bricks,), 1, PB + 1)
    number = jnp.maximum(1, PB // 2 + first * second // (2 * PB))
    number = jnp.minimum(number, PB)
    chosen = jax.random.randint(key_c, (), 0, bricks)
    number = jnp.where(jnp.arange(bricks) == chosen, PB, number)
    return number.reshape(N_GX, N_GY, N_GZ).astype(jnp.int32)


def set_ends(values, own_key, low, high):
    place = [jax.random.randint(jax.random.fold_in(own_key, axis), (), 0, length) for axis, length in enumerate(values.shape)]
    main_axis = values.shape.index(max(values.shape))
    next_to = place[:main_axis] + [(place[main_axis] + 1) % values.shape[main_axis]] + place[main_axis + 1:]
    return values.at[tuple(place)].set(low).at[tuple(next_to)].set(high)


def level_of(stream_key, shape, shards, low, top_value):
    loudness = 1.0
    for axis_at, blocks in shards:
        steps = jax.random.uniform(jax.random.fold_in(jax.random.fold_in(stream_key, 6), axis_at), (blocks,), jnp.float32, low / len(shards), top_value / len(shards))
        loudness = loudness * jnp.repeat(jnp.exp(steps), shape[axis_at] // blocks).reshape((-1,) + (1,) * (len(shape) - 1 - axis_at))
    return loudness


def scatter_about(rng, extent, spread, limit, cuts=(), kind=jnp.bfloat16):
    values = jax.random.normal(rng, extent, jnp.float32) * spread
    if len(cuts) > 0:
        values = level_of(rng, extent, cuts, -0.22, 0.18) * values
    return jnp.clip(values, min=-limit, max=limit).astype(kind)


def setup_inputs(seed: int = 0) -> dict:
    keys = jax.random.split(jax.random.key(seed), 9)
    return {
        "pressure_prev": scatter_about(keys[0], (NX, NY, NZ), 1.0, 6.0, ((0, 8), (1, 8), (2, 4)), jnp.float32),
        "pressure_now": scatter_about(keys[1], (NX, NY, NZ), 1.0, 6.0, ((0, 8), (1, 8), (2, 4)), jnp.float32),
        "material": set_ends(jax.random.randint(keys[2], (NX, NY, NZ), 0, NMAT), jax.random.fold_in(keys[2], 1), 0, NMAT - 1).astype(jnp.int32),
        "speed_table": jnp.clip(jax.random.uniform(keys[3], (NMAT,), jnp.float32, 0.05, 0.32), 0.05, 0.32),
        "anchors": draw_anchors(jax.random.fold_in(keys[8], 71), 0),
        "counts": draw_counts(jax.random.fold_in(keys[8], 71), 0),
        "w_in": scatter_about(keys[6], (D, HID), D ** -0.5, 0.25),
        "w_out": scatter_about(keys[7], (HID, D), HID ** -0.5, 0.1875),
    }


def coefficient(material, speed_table):
    coef = jnp.zeros(material.shape, jnp.float32)
    for number in range(speed_table.shape[0]):
        coef = jnp.where(material == number, speed_table[number], coef)
    return coef

def update(prev, now, coef, padded):
    beside = padded[2:, 1:-1, 1:-1] + padded[:-2, 1:-1, 1:-1]
    beside = beside + padded[1:-1, 2:, 1:-1] + padded[1:-1, :-2, 1:-1]
    beside = beside + padded[1:-1, 1:-1, 2:] + padded[1:-1, 1:-1, :-2]
    return 2.0 * now - prev + coef * (beside - 6.0 * now)

def outer_sum(left, right):
    return lax.dot_general(left, right, (((0,), (0,)), ((), ())), preferred_element_type=jnp.float32)

def mlp_parts(inputs, targets, valid, total, w_in, w_out):
    scale = lax.rsqrt(lax.optimization_barrier(jnp.mean(inputs * inputs, axis=-1, keepdims=True)) + 1e-06)
    normed = (inputs * scale).astype(jnp.bfloat16)
    pre = jnp.dot(normed, w_in, preferred_element_type=jnp.float32)
    act = jax.nn.gelu(pre).astype(jnp.bfloat16)
    err = inputs + jnp.dot(act, w_out, preferred_element_type=jnp.float32) - targets
    dout = (2.0 * err * valid[:, None] / total).astype(jnp.bfloat16)
    dact = lax.dot_general(dout, w_out, (((1,), (1,)), ((), ())), preferred_element_type=jnp.float32)
    dpre = jax.vjp(jax.nn.gelu, pre)[1](dact)[0].astype(jnp.bfloat16)
    return (normed, act, dout, dpre)

def reference(pressure_prev, pressure_now, material, speed_table, anchors, counts, w_in, w_out):
    coef = coefficient(material, speed_table)
    prev, now = (pressure_prev, pressure_now)
    for step in range(STEPS):
        padded = jnp.pad(now, 1)
        prev, now = (now, update(prev, now, coef, padded))
    stacked = jnp.stack([pressure_now, now])
    total = jnp.sum(counts.astype(jnp.float32))
    bricks = N_GX * N_GY * N_GZ
    flat_anchor = anchors.reshape(bricks, PB).astype(jnp.int32)
    flat_count = counts.reshape(bricks).astype(jnp.int32)
    numbers = jnp.arange(bricks, dtype=jnp.int32)
    zero_index = jnp.zeros((), jnp.int32)

    def brick_terms(carry, item):
        number, local, count = item
        brick_x = number // (N_GY * N_GZ)
        brick_y = number // N_GZ % N_GY
        brick_z = number % N_GZ
        first_x = (local // (CY * CZ) + brick_x * CX).astype(jnp.int32)
        first_y = (local // CZ % CY + brick_y * CY).astype(jnp.int32)
        first_z = (local % CZ + brick_z * CZ).astype(jnp.int32)

        def take(a, b, c):
            return lax.dynamic_slice(stacked, (zero_index, a, b, c), (2, PATCH, PATCH, PATCH))
        pieces = jax.vmap(take)(first_x, first_y, first_z)
        inputs = pieces[:, 0].reshape(PB, D)
        targets = pieces[:, 1].reshape(PB, D)
        valid = (jnp.arange(PB, dtype=jnp.int32) < count).astype(jnp.float32)
        normed, act, dout, dpre = mlp_parts(inputs, targets, valid, total, w_in, w_out)
        return ((carry[0] + outer_sum(normed, dpre), carry[1] + outer_sum(act, dout)), None)
    start = (jnp.zeros((D, HID), jnp.float32), jnp.zeros((HID, D), jnp.float32))
    (grad_in, grad_out), unused = lax.scan(brick_terms, start, (numbers, flat_anchor, flat_count))
    return (now, grad_in, grad_out)
```

```python
import functools

import jax
import jax.numpy as jnp
from jax import lax
from jax.experimental import pallas as pl
from jax.experimental.pallas import tpu as pltpu
from jax.sharding import PartitionSpec as P

STEPS = 8
PATCH = 8
LANES = 128
AXES = ("gx", "gy", "gz")
F32 = jnp.float32
BF16 = jnp.bfloat16


def remote(src, dst, send_sem, recv_sem, device):
    return pltpu.make_async_remote_copy(
        src_ref=src,
        dst_ref=dst,
        send_sem=send_sem,
        recv_sem=recv_sem,
        device_id=device,
        device_id_type=pl.DeviceIdType.MESH,
    )


def signal(sem, device):
    pl.semaphore_signal(
        sem, inc=1, device_id=device, device_id_type=pl.DeviceIdType.MESH
    )


def wave_kernel(
    sizes,
    prev_ref,
    now_ref,
    mat_ref,
    tab_ref,
    cnt_ref,
    out_ref,
    tot_ref,
    buf_a,
    buf_b,
    coef,
    ysend,
    yrecv,
    zsend,
    zrecv,
    csend,
    crecv,
    xs,
    xr,
    ys,
    yr,
    zs,
    zr,
    cs,
    cr,
):
    nx, ny, nz = sizes
    gx, gy, gz = [lax.axis_index(axis) for axis in AXES]
    X, Y, Z = now_ref.shape
    W = Z + LANES
    here = (gx, gy, gz)

    def line_peer(axis, step):
        size = sizes[axis]
        device = list(here)
        device[axis] = lax.rem(here[axis] + step, size)
        return tuple(device)

    zero_plane = jnp.zeros((Y, W), F32)
    for buf in (buf_a, buf_b):
        buf[0] = zero_plane
        buf[X + 1] = zero_plane
    yrecv[...] = jnp.zeros(yrecv.shape, F32)
    zrecv[...] = jnp.zeros(zrecv.shape, F32)

    barrier = pltpu.get_barrier_semaphore()
    peers = 0
    for axis in range(3):
        for step in range(1, sizes[axis]):
            signal(barrier, line_peer(axis, step))
            peers += 1

    lane = lax.broadcasted_iota(jnp.int32, (Y, LANES), 1)
    row = lax.broadcasted_iota(jnp.int32, (Y, W), 0)

    def pack(x, carry):
        material = mat_ref[x]
        c = jnp.zeros((Y, Z), F32)
        for number in range(tab_ref.shape[0]):
            c = jnp.where(material == number, tab_ref[number], c)
        n, p = now_ref[x], prev_ref[x]
        coef[x, :, 0:Z] = c
        buf_a[x + 1, :, 0:Z] = n
        buf_b[x + 1, :, 0:Z] = p
        mine = lax.shift_right_logical(lane, 3) == x
        up, down = [], []
        for field, held_up, held_down in zip((n, p, c), carry[0], carry[1]):
            last = pltpu.roll(field[:, Z - LANES :], lax.rem(x * 8 + 8, LANES), 1)
            first = pltpu.roll(field[:, :LANES], x * 8, 1)
            up.append(jnp.where(mine, last, held_up))
            down.append(jnp.where(mine, first, held_down))
        return tuple(up), tuple(down)

    empty = tuple(jnp.zeros((Y, LANES), F32) for _ in range(3))
    ups, downs = lax.fori_loop(0, X, pack, (empty, empty))
    for i in range(3):
        zsend[0, i] = ups[i]
        zsend[1, i] = downs[i]
    csend[0] = jnp.full((8, LANES), cnt_ref[0].astype(F32))

    pl.semaphore_wait(barrier, peers)

    def z_up():
        return remote(
            zsend.at[0], zrecv.at[0], zs.at[0], zr.at[0], (gx, gy, lax.rem(gz + 1, nz))
        )

    def z_down():
        return remote(
            zsend.at[1],
            zrecv.at[1],
            zs.at[1],
            zr.at[1],
            (gx, gy, lax.rem(gz + nz - 1, nz)),
        )

    @pl.when(gz < nz - 1)
    def _():
        z_up().start()

    @pl.when(gz > 0)
    def _():
        z_down().start()

    def count_copy(axis, step):
        return remote(
            csend.at[axis],
            crecv.at[axis, here[axis]],
            cs.at[axis, step],
            cr.at[axis, here[axis]],
            line_peer(axis, step),
        )

    def count_start(axis):
        for step in range(1, sizes[axis]):
            count_copy(axis, step).start()
        crecv[axis, here[axis]] = csend[axis]

    def count_finish(axis):
        size = sizes[axis]
        for step in range(1, size):
            count_copy(axis, step).wait_send()
            source = lax.rem(here[axis] + step, size)
            remote(
                csend.at[axis],
                crecv.at[axis, source],
                cs.at[axis, step],
                cr.at[axis, source],
                line_peer(axis, step),
            ).wait_recv()
        total = crecv[axis, 0]
        for i in range(1, size):
            total = total + crecv[axis, i]
        return total

    count_start(0)

    @pl.when(gz < nz - 1)
    def _():
        z_up().wait_send()
        z_down().wait_recv()

    @pl.when(gz > 0)
    def _():
        z_down().wait_send()
        z_up().wait_recv()

    def unpack(x, carry):
        outer = []
        for i in range(3):
            left = pltpu.roll(zrecv[0, i], lax.rem(120 + LANES - x * 8, LANES), 1)
            right = pltpu.roll(zrecv[1, i], lax.rem(LANES - x * 8, LANES), 1)
            outer.append(
                jnp.where(lane < 8, right, jnp.where(lane >= 120, left, 0.0))
            )
        buf_a[x + 1, :, Z:W] = outer[0]
        buf_b[x + 1, :, Z:W] = outer[1]
        coef[x, :, Z:W] = outer[2]
        ysend[0, 0, x, :, 0:Z] = now_ref[x, 0:1, :]
        ysend[0, 0, x, :, Z:W] = outer[0][0:1]
        ysend[0, 1, x, :, 0:Z] = now_ref[x, Y - 1 : Y, :]
        ysend[0, 1, x, :, Z:W] = outer[0][Y - 1 : Y]
        return carry

    lax.fori_loop(0, X, unpack, 0)

    bufs = (buf_a, buf_b)

    def face(which, par):
        buf = bufs[par]
        if which == 0:
            return remote(
                buf.at[1],
                buf.at[X + 1],
                xs.at[par, 0],
                xr.at[par, 1],
                (lax.rem(gx + nx - 1, nx), gy, gz),
            )
        if which == 1:
            return remote(
                buf.at[X],
                buf.at[0],
                xs.at[par, 1],
                xr.at[par, 0],
                (lax.rem(gx + 1, nx), gy, gz),
            )
        if which == 2:
            return remote(
                ysend.at[par, 0],
                yrecv.at[par, 1],
                ys.at[par, 0],
                yr.at[par, 1],
                (gx, lax.rem(gy + ny - 1, ny), gz),
            )
        return remote(
            ysend.at[par, 1],
            yrecv.at[par, 0],
            ys.at[par, 1],
            yr.at[par, 0],
            (gx, lax.rem(gy + 1, ny), gz),
        )

    has = (gx > 0, gx < nx - 1, gy > 0, gy < ny - 1)
    opposite = (1, 0, 3, 2)

    def faces_start(par):
        for which in range(4):

            @pl.when(has[which])
            def _():
                face(which, par).start()

    def faces_sent(par):
        for which in range(4):

            @pl.when(has[which])
            def _():
                face(which, par).wait_send()

    def faces_here(par):
        for which in range(4):

            @pl.when(has[which])
            def _():
                face(opposite[which], par).wait_recv()

    faces_start(0)
    for t in range(STEPS):
        par = t % 2
        cur, other = bufs[par], bufs[1 - par]
        faces_here(par)
        if t > 0:
            faces_sent(1 - par)
        last_step = t == STEPS - 1

        def plane(x, carry):
            n = cur[x + 1]
            beside = cur[x + 2] + cur[x]
            low = yrecv[par, 0, x]
            high = yrecv[par, 1, x]
            beside = beside + jnp.where(row == Y - 1, high, pltpu.roll(n, Y - 1, 0))
            beside = beside + jnp.where(row == 0, low, pltpu.roll(n, 1, 0))
            beside = beside + pltpu.roll(n, W - 1, 1) + pltpu.roll(n, 1, 1)
            after = 2.0 * n - other[x + 1] + coef[x] * (beside - 6.0 * n)
            if last_step:
                out_ref[x] = after[:, 0:Z]
            else:
                other[x + 1] = after
                ysend[1 - par, 0, x] = after[0:1]
                ysend[1 - par, 1, x] = after[Y - 1 : Y]
            return carry

        lax.fori_loop(0, X, plane, 0)
        if not last_step:
            faces_start(1 - par)
        if t == 1:
            csend[1] = count_finish(0)
            count_start(1)
        if t == 3:
            csend[2] = count_finish(1)
            count_start(2)
        if t == 5:
            tot_ref[...] = count_finish(2)
    faces_sent(1)


def wave(prev, now, material, table, used, sizes):
    X, Y, Z = now.shape
    W = Z + LANES
    vmem = pl.BlockSpec(memory_space=pltpu.VMEM)
    smem = pl.BlockSpec(memory_space=pltpu.SMEM)
    dma = pltpu.SemaphoreType.DMA
    most = max(sizes)
    return pl.pallas_call(
        functools.partial(wave_kernel, sizes),
        name="wave",
        out_shape=(
            jax.ShapeDtypeStruct((X, Y, Z), F32),
            jax.ShapeDtypeStruct((8, LANES), F32),
        ),
        in_specs=[vmem, vmem, vmem, smem, smem],
        out_specs=(vmem, vmem),
        scratch_shapes=[
            pltpu.VMEM((X + 2, Y, W), F32),
            pltpu.VMEM((X + 2, Y, W), F32),
            pltpu.VMEM((X, Y, W), F32),
            pltpu.VMEM((2, 2, X, 1, W), F32),
            pltpu.VMEM((2, 2, X, 1, W), F32),
            pltpu.VMEM((2, 3, Y, LANES), F32),
            pltpu.VMEM((2, 3, Y, LANES), F32),
            pltpu.VMEM((3, 8, LANES), F32),
            pltpu.VMEM((3, most, 8, LANES), F32),
            dma((2, 2)),
            dma((2, 2)),
            dma((2, 2)),
            dma((2, 2)),
            dma((2,)),
            dma((2,)),
            dma((3, most)),
            dma((3, most)),
        ],
        compiler_params=pltpu.CompilerParams(collective_id=0, has_side_effects=True),
    )(prev, now, material, table, used)


def matmul(a, b, dims):
    return lax.dot_general(a, b, (dims, ((), ())), preferred_element_type=F32)


def in_order(values, order):
    total = None
    rest = values
    for part in range(3):
        piece = rest.astype(BF16)
        if part < 2:
            rest = rest - piece.astype(F32)
        term = matmul(piece, order, ((1,), (0,)))
        total = term if total is None else total + term
    return total


def patch_kernel(
    blocks,
    now_ref,
    final_ref,
    anchor_ref,
    cnt_ref,
    tot_ref,
    win_ref,
    wout_ref,
    grad_ref,
    rows,
    turned,
    picked,
    order,
):
    X, Y, Z = now_ref.shape
    slots = anchor_ref.shape[0]
    wide = win_ref.shape[0]
    hidden = win_ref.shape[1]
    tiles = X * Y // LANES

    for which, field in enumerate((now_ref, final_ref)):
        for x in range(X):
            for half in range(Z // LANES):
                rows[half, pl.ds(x, Y, stride=X), :] = field[
                    x, :, half * LANES : (half + 1) * LANES
                ]
        for half in range(Z // LANES):
            for tile in range(tiles):
                turned[which, tile, half * LANES : (half + 1) * LANES, :] = rows[
                    half, tile * LANES : (tile + 1) * LANES, :
                ].T
        turned[which, tiles] = jnp.zeros((Z, LANES), F32)

    lane = lax.broadcasted_iota(jnp.int32, (8, LANES), 1)

    def pick(s, carry):
        anchor = anchor_ref[s]
        i = anchor // (Y * Z)
        j = lax.rem(anchor // Z, Y)
        k = lax.rem(anchor, Z)
        shift = j * X + i
        tile = shift // LANES
        by = lax.rem(shift, LANES)
        back = lax.rem(LANES - by, LANES)
        for which in range(2):
            first = turned[which, tile, pl.ds(k, 8), :]
            second = turned[which, tile + 1, pl.ds(k, 8), :]
            value = jnp.where(
                lane < LANES - by,
                pltpu.roll(first, back, 1),
                pltpu.roll(second, back, 1),
            )
            picked[which, pl.ds(pl.multiple_of(s * 8, 8), 8), :] = value
        return carry

    lax.fori_loop(0, slots, pick, 0, unroll=4)

    at = lax.broadcasted_iota(jnp.int32, (8 * LANES, wide), 0)
    feature = lax.broadcasted_iota(jnp.int32, (8 * LANES, wide), 1)
    a = jnp.bitwise_and(at, X - 1)
    b = jnp.bitwise_and(lax.shift_right_logical(at, 4), 7)
    c = lax.shift_right_logical(at, 7)
    order[...] = jnp.where(
        (a < PATCH) & (feature == a * 64 + b * 8 + c), 1.0, 0.0
    ).astype(BF16)

    taken = []
    for which in range(2):
        values = jnp.concatenate(
            [picked[which, pl.ds(c, slots, stride=8), :] for c in range(8)], axis=1
        )
        taken.append(in_order(values, order[...]))
    inputs, targets = taken

    mean = jnp.mean(inputs * inputs, axis=1, keepdims=True)
    normed = (inputs * lax.rsqrt(mean + 1e-06)).astype(BF16)
    pre = matmul(normed, win_ref[...], ((1,), (0,)))
    root = 0.7978845608028654
    tanh = jnp.tanh(root * (pre + 0.044715 * (pre * pre * pre)))
    cdf = 0.5 * (1.0 + tanh)
    act = (pre * cdf).astype(BF16)
    slope = cdf + 0.5 * pre * (1.0 - tanh * tanh) * (
        root * (1.0 + (3.0 * 0.044715) * (pre * pre))
    )
    err = inputs + matmul(act, wout_ref[...], ((1,), (0,))) - targets
    slot = lax.broadcasted_iota(jnp.int32, (slots, 1), 0)
    valid = (slot < cnt_ref[0]).astype(F32)
    dout = (2.0 * err * valid / tot_ref[0:1, 0:1]).astype(BF16)
    dact = matmul(dout, wout_ref[...], ((1,), (1,)))
    dpre = (dact * slope).astype(BF16)
    grad_in = matmul(normed, dpre, ((0,), (0,)))
    grad_out = matmul(act, dout, ((0,), (0,)))
    in_rows = wide // blocks
    out_rows = hidden // blocks
    for block in range(blocks):
        core, high = block % 2, block // 2
        grad_ref[core, high, 0:in_rows, :] = grad_in[
            block * in_rows : (block + 1) * in_rows
        ]
        for half in range(2):
            start = block * out_rows + half * in_rows
            grad_ref[
                core, high, in_rows : 2 * in_rows, half * wide : (half + 1) * wide
            ] = grad_out[start : start + in_rows]


def patches(now, final, anchors, used, total, w_in, w_out, blocks):
    X, Y, Z = now.shape
    slots = anchors.shape[0]
    wide, hidden = w_in.shape
    vmem = pl.BlockSpec(memory_space=pltpu.VMEM)
    smem = pl.BlockSpec(memory_space=pltpu.SMEM)
    return pl.pallas_call(
        functools.partial(patch_kernel, blocks),
        name="patches",
        out_shape=jax.ShapeDtypeStruct(
            (2, blocks // 2, 2 * wide // blocks, hidden), F32
        ),
        in_specs=[vmem, vmem, smem, smem, vmem, vmem, vmem],
        out_specs=vmem,
        scratch_shapes=[
            pltpu.VMEM((Z // LANES, X * Y, LANES), F32),
            pltpu.VMEM((2, X * Y // LANES + 1, Z, LANES), F32),
            pltpu.VMEM((2, 8 * slots, LANES), F32),
            pltpu.VMEM((8 * LANES, wide), BF16),
        ],
        compiler_params=pltpu.CompilerParams(vmem_limit_bytes=60 * 1024 * 1024),
    )(now, final, anchors, used, total, w_in, w_out)


def reduce_kernel(
    grad_ref,
    in_ref,
    out_ref,
    pair,
    relay1,
    fin1,
    send1,
    held1,
    relay2,
    fin2,
    send2,
    held2,
    zrecv,
    gathered,
    pair_sem,
    sems1,
    sems2,
    z_send,
    z_recv,
    g_send,
    g_recv,
):
    gx, gy, gz = [lax.axis_index(axis) for axis in AXES]
    core, high = lax.rem(gx, 2), gx // 2
    low, y = lax.rem(gy, 2), gy // 2
    x = gz

    def device(core=core, high=high, low=low, y=y, x=x):
        return (high * 2 + core, y * 2 + low, x)

    barrier = pltpu.get_barrier_semaphore()
    signal(barrier, device(core=1 - core))
    peers = 1
    z_steps = [(h, l) for h in range(4) for l in range(2) if h or l]
    g_steps = [
        (i, j, l) for i in range(4) for j in range(4) for l in range(2) if i or j or l
    ]
    for h, l in z_steps:
        if h:
            signal(
                barrier, device(high=lax.rem(high + h, 4), low=lax.rem(low + l, 2))
            )
            peers += 1
    for i, j, l in g_steps:
        signal(
            barrier,
            device(x=lax.rem(x + i, 4), y=lax.rem(y + j, 4), low=lax.rem(low + l, 2)),
        )
        peers += 1
    pl.semaphore_wait(barrier, peers)

    swap = remote(
        grad_ref.at[1 - core],
        pair,
        pair_sem.at[0],
        pair_sem.at[1],
        device(core=1 - core),
    )
    swap.start()
    swap.wait()
    for h in range(4):
        pair[h] = pair[h] + grad_ref[core, h]

    half = 512
    places = ((x, lambda v: device(x=v)), (y, lambda v: device(y=v)))

    def ring(stage, colour, source, rows, relay, fin, send, sems):
        along = colour if stage == 0 else 1 - colour
        me, to = places[along]
        plus, minus, across = [lax.rem(me + d, 4) for d in (1, 3, 2)]

        def chunk(owner):
            return pl.ds(pl.multiple_of(owner * rows, 8), rows)

        first, second = pl.ds(0, 2), pl.ds(2, 2)

        def piece(part, owner):
            return source(part, chunk(owner))

        def copy(src, dst, number, peer):
            return remote(
                src,
                dst,
                sems.at[colour, 0, number],
                sems.at[colour, 1, number],
                to(peer),
            )

        copies = [
            copy(piece(first, across), relay.at[colour, 0], 0, plus),
            copy(piece(second, across), relay.at[colour, 1], 1, minus),
            copy(piece(second, plus), fin.at[colour, 0, second], 2, plus),
            copy(piece(first, minus), fin.at[colour, 1, first], 3, minus),
            copy(send.at[colour, 0], fin.at[colour, 0, first], 4, plus),
            copy(send.at[colour, 1], fin.at[colour, 1, second], 5, minus),
        ]

        def start():
            for one in copies[:4]:
                one.start()

        def forward():
            copies[0].wait_recv()
            send[colour, 0] = relay[colour, 0] + piece(first, plus)[...]
            copies[4].start()
            copies[1].wait_recv()
            send[colour, 1] = relay[colour, 1] + piece(second, minus)[...]
            copies[5].start()

        def finish():
            for one in copies[2:]:
                one.wait_recv()
            own = piece(pl.ds(0, 4), me)[...]
            total = own + fin[colour, 0] + fin[colour, 1]
            for one in copies:
                one.wait_send()
            return total

        return start, forward, finish

    def source1(colour):
        def pick(part, rows):
            return pair.at[part, rows, pl.ds(colour * half, half)]

        return pick

    def source2(colour):
        def pick(part, rows):
            return held1.at[colour, part, rows, :]

        return pick

    stage1 = [
        ring(0, colour, source1(colour), 32, relay1, fin1, send1, sems1)
        for colour in range(2)
    ]
    stage2 = [
        ring(1, colour, source2(colour), 8, relay2, fin2, send2, sems2)
        for colour in range(2)
    ]
    for rings, held in ((stage1, held1), (stage2, held2)):
        for one in rings:
            one[0]()
        for one in rings:
            one[1]()
        for colour, one in enumerate(rings):
            held[colour] = one[2]()

    z_me = high * 2 + low
    quarter = half // 2

    def z_piece(h, l):
        return held2.at[:, h, :, pl.ds(pl.multiple_of(l * quarter, quarter), quarter)]

    z_copies = []
    for number, (h, l) in enumerate(z_steps):
        ph, pw = lax.rem(high + h, 4), lax.rem(low + l, 2)
        one = remote(
            z_piece(ph, pw),
            zrecv.at[z_me],
            z_send.at[number],
            z_recv.at[z_me],
            device(high=ph, low=pw),
        )
        one.start()
        z_copies.append((one, ph * 2 + pw, device(high=ph, low=pw)))
    zrecv[z_me] = z_piece(high, low)[...]
    for one, slot, peer in z_copies:
        remote(
            z_piece(high, low), zrecv.at[slot], z_send.at[0], z_recv.at[slot], peer
        ).wait_recv()
    total = zrecv[0]
    for slot in range(1, 8):
        total = total + zrecv[slot]
    g_me = (x * 4 + y) * 2 + low
    gathered[g_me] = total
    g_copies = []
    for number, (i, j, l) in enumerate(g_steps):
        px, py, pw = lax.rem(x + i, 4), lax.rem(y + j, 4), lax.rem(low + l, 2)
        peer = device(x=px, y=py, low=pw)
        one = remote(
            gathered.at[g_me],
            gathered.at[g_me],
            g_send.at[number],
            g_recv.at[g_me],
            peer,
        )
        one.start()
        g_copies.append((one, (px * 4 + py) * 2 + pw, peer))
    for one, slot, peer in z_copies:
        one.wait_send()
    for one, slot, peer in g_copies:
        remote(
            gathered.at[slot],
            gathered.at[slot],
            g_send.at[0],
            g_recv.at[slot],
            peer,
        ).wait_recv()
    for ix in range(4):
        for iy in range(4):
            for il in range(2):
                slot = (ix * 4 + iy) * 2 + il
                for colour in range(2):
                    row = ix * 32 + iy * 8 if colour == 0 else iy * 32 + ix * 8
                    at = colour * half + il * quarter
                    value = gathered[slot, colour]
                    if row < 64:
                        in_ref[row : row + 8, at : at + quarter] = value
                    else:
                        top = row - 64 + (64 if at >= 512 else 0)
                        left = at % 512
                        out_ref[top : top + 8, left : left + quarter] = value
    for one, slot, peer in g_copies:
        one.wait_send()


def reduce(grads):
    vmem = pl.BlockSpec(memory_space=pltpu.VMEM)
    dma = pltpu.SemaphoreType.DMA
    return pl.pallas_call(
        reduce_kernel,
        name="reduce",
        out_shape=(
            jax.ShapeDtypeStruct((64, 1024), F32),
            jax.ShapeDtypeStruct((128, 512), F32),
        ),
        in_specs=[vmem],
        out_specs=(vmem, vmem),
        scratch_shapes=[
            pltpu.VMEM((4, 128, 1024), F32),
            pltpu.VMEM((2, 2, 2, 32, 512), F32),
            pltpu.VMEM((2, 2, 4, 32, 512), F32),
            pltpu.VMEM((2, 2, 2, 32, 512), F32),
            pltpu.VMEM((2, 4, 32, 512), F32),
            pltpu.VMEM((2, 2, 2, 8, 512), F32),
            pltpu.VMEM((2, 2, 4, 8, 512), F32),
            pltpu.VMEM((2, 2, 2, 8, 512), F32),
            pltpu.VMEM((2, 4, 8, 512), F32),
            pltpu.VMEM((8, 2, 8, 256), F32),
            pltpu.VMEM((32, 2, 8, 256), F32),
            dma((2,)),
            dma((2, 2, 6)),
            dma((2, 2, 6)),
            dma((7,)),
            dma((8,)),
            dma((31,)),
            dma((32,)),
        ],
        compiler_params=pltpu.CompilerParams(
            collective_id=1,
            has_side_effects=True,
            vmem_limit_bytes=60 * 1024 * 1024,
        ),
    )(grads)


def body(pressure_prev, pressure_now, material, speed_table, anchors, counts, w_in, w_out):
    sizes = tuple(lax.axis_size(axis) for axis in AXES)
    used = counts.reshape(-1)
    final, total = wave(
        pressure_prev, pressure_now, material, speed_table, used, sizes
    )
    grads = patches(
        pressure_now, final, anchors.reshape(-1), used, total, w_in, w_out, sizes[0]
    )
    grad_in, grad_out = reduce(grads)
    return final, grad_in, grad_out


def solution(mesh):
    return jax.shard_map(
        body,
        mesh=mesh,
        in_specs=(
            P("gx", "gy", "gz"),
            P("gx", "gy", "gz"),
            P("gx", "gy", "gz"),
            P(),
            P("gx", "gy", "gz"),
            P("gx", "gy", "gz"),
            P(),
            P(),
        ),
        out_specs=(P("gx", "gy", "gz"), P("gx", None), P("gx", None)),
        check_vma=False,
    )
```

```python
import functools
import types

import jax
import jax.numpy as jnp
from jax import lax
from jax.experimental import pallas as pl
from jax.experimental.pallas import tpu as pltpu
from jax.sharding import PartitionSpec as P

STEPS = 8
PATCH = 8
LANES = 128
AXES = ("gx", "gy", "gz")
F32 = jnp.float32
BF16 = jnp.bfloat16


def remote(src, dst, send_sem, recv_sem, device):
    return pltpu.make_async_remote_copy(
        src_ref=src,
        dst_ref=dst,
        send_sem=send_sem,
        recv_sem=recv_sem,
        device_id=device,
        device_id_type=pl.DeviceIdType.MESH,
    )


def signal(sem, device):
    pl.semaphore_signal(
        sem, inc=1, device_id=device, device_id_type=pl.DeviceIdType.MESH
    )


def matmul(a, b, dims):
    return lax.dot_general(a, b, (dims, ((), ())), preferred_element_type=F32)


def in_order(values, order, parts):
    total = None
    rest = values
    for part in range(parts):
        piece = rest.astype(BF16)
        if part < parts - 1:
            rest = rest - piece.astype(F32)
        term = matmul(piece, order, ((1,), (0,)))
        total = term if total is None else total + term
    return total


def step_kernel(
    names,
    sizes,
    prev_ref,
    now_ref,
    mat_ref,
    tab_ref,
    cnt_ref,
    anchor_ref,
    win_hbm,
    wout_hbm,
    out_ref,
    sum_ref,
    *scratch,
):
    m = types.SimpleNamespace(**dict(zip(names, scratch)))
    nx, ny, nz = sizes
    gx, gy, gz = [lax.axis_index(axis) for axis in AXES]
    here = (gx, gy, gz)
    core, high = lax.rem(gx, 2), gx // 2
    low, y = lax.rem(gy, 2), gy // 2
    X, Y, Z = now_ref.shape
    W = Z + LANES
    T = W // LANES
    slots = anchor_ref.shape[0]
    wide, hidden = win_hbm.shape
    A, B, C = m.A, m.B, m.C

    def device(core=core, high=high, low=low, y=y, x=gz):
        return (high * 2 + core, y * 2 + low, x)

    def line_peer(axis, step):
        place = list(here)
        place[axis] = lax.rem(here[axis] + step, sizes[axis])
        return tuple(place)

    partner = device(core=1 - core)

    barrier = pltpu.get_barrier_semaphore()
    z_steps = [(h, l) for h in range(4) for l in range(2) if h or l]
    g_steps = [
        (i, j, l) for i in range(4) for j in range(4) for l in range(2) if i or j or l
    ]
    reached = []
    for axis in range(3):
        for step in range(1, sizes[axis]):
            reached.append(line_peer(axis, step))
    for dx in (nx - 1, 1):
        for dy in (ny - 1, 1):
            reached.append((lax.rem(gx + dx, nx), lax.rem(gy + dy, ny), gz))
    for h, l in z_steps:
        if h and l:
            reached.append(
                device(high=lax.rem(high + h, 4), low=lax.rem(low + l, 2))
            )
    for i, j, l in g_steps:
        if i and (j or l):
            reached.append(
                device(
                    x=lax.rem(gz + i, 4), y=lax.rem(y + j, 4), low=lax.rem(low + l, 2)
                )
            )

    load_in = pltpu.make_async_copy(win_hbm, m.w_in, m.load.at[0])
    load_out = pltpu.make_async_copy(wout_hbm, m.w_out, m.load.at[1])
    load_in.start()
    load_out.start()

    m.xrecv[...] = jnp.zeros(m.xrecv.shape, F32)
    m.yrecv[...] = jnp.zeros(m.yrecv.shape, F32)
    m.zrecv[...] = jnp.zeros(m.zrecv.shape, F32)
    m.crecv[...] = jnp.zeros(m.crecv.shape, F32)
    for place in reached:
        signal(barrier, place)

    lane = lax.broadcasted_iota(jnp.int32, (Y, LANES), 1)
    row = lax.broadcasted_iota(jnp.int32, (Y, W), 0)

    def put_rows(entry, x, value, tiles, first):
        for side, at in ((0, 0), (1, Y - 1)):
            for k, tile in enumerate(tiles):
                m.ysend[side, entry, tile, pl.ds(x, 1), :] = value[
                    at : at + 1, k * LANES : (k + 1) * LANES
                ]
                if first:
                    at2 = at + 1 - 2 * side
                    m.ysend[side, 1, tile, pl.ds(x, 1), :] = value[
                        at2 : at2 + 1, k * LANES : (k + 1) * LANES
                    ]

    inner_tiles = range(Z // LANES)
    last_tile = range(Z // LANES, T)

    def pack(x, carry):
        material = mat_ref[x]
        c = jnp.zeros((Y, Z), F32)
        for number in range(tab_ref.shape[0]):
            c = jnp.where(material == number, tab_ref[number], c)
        n, p = now_ref[x], prev_ref[x]
        C[x + 1, :, 0:Z] = c
        A[x + 2, :, 0:Z] = n
        B[x + 2, :, 0:Z] = p
        put_rows(0, x, n, inner_tiles, True)
        put_rows(2, x, p, inner_tiles, False)
        put_rows(3, x, c, inner_tiles, False)
        mine = lax.shift_right_logical(lane, 3) == x
        up, down = [], []
        for field, held_up, held_down in zip((n, p, c), carry[0], carry[1]):
            last = pltpu.roll(field[:, Z - LANES :], lax.rem(x * 8 + 8, LANES), 1)
            first = pltpu.roll(field[:, :LANES], x * 8, 1)
            up.append(jnp.where(mine, last, held_up))
            down.append(jnp.where(mine, first, held_down))
        return tuple(up), tuple(down)

    empty = tuple(jnp.zeros((Y, LANES), F32) for _ in range(3))
    ups, downs = lax.fori_loop(0, X, pack, (empty, empty))
    for i in range(3):
        m.zsend[0, i] = ups[i]
        m.zsend[1, i] = downs[i]

    def stage_planes(lanes):
        sources = (
            ((A, 2), (A, 3), (B, 2), (C, 1)),
            ((A, X), (A, X + 1), (B, X + 1), (C, X)),
        )
        for side in range(2):
            for entry, (field, plane) in enumerate(sources[side]):
                m.xsend[side, entry, :, lanes] = field[plane, :, lanes]

    main, edge = slice(0, Z), slice(Z, W)
    stage_planes(main)
    m.nsend[0] = jnp.full((8, LANES), cnt_ref[0].astype(F32))

    pl.semaphore_wait(barrier, len(reached))

    def z_copy(side):
        step = 1 if side == 0 else nz - 1
        return remote(
            m.zsend.at[side],
            m.zrecv.at[side],
            m.z_sem.at[0, side],
            m.z_sem.at[1, side],
            (gx, gy, lax.rem(gz + step, nz)),
        )

    @pl.when(gz < nz - 1)
    def _():
        z_copy(0).start()

    @pl.when(gz > 0)
    def _():
        z_copy(1).start()

    left, right = lax.rem(gx + nx - 1, nx), lax.rem(gx + 1, nx)
    below, above = lax.rem(gy + ny - 1, ny), lax.rem(gy + 1, ny)
    targets_of = (
        (left, gy, gz),
        (right, gy, gz),
        (gx, below, gz),
        (gx, above, gz),
        (left, below, gz),
        (left, above, gz),
        (right, below, gz),
        (right, above, gz),
    )
    sides = (gx > 0, gx < nx - 1, gy > 0, gy < ny - 1)
    has = sides + tuple(
        jnp.logical_and(sides[i], sides[j]) for i in (0, 1) for j in (2, 3)
    )
    opposite = (1, 0, 3, 2, 7, 6, 5, 4)

    def face(d, par, form):
        if d < 2:
            if form == 0:
                src = A.at[2:4] if d == 0 else A.at[X : X + 2]
                dst = m.xrecv.at[par, 1 - d, 0:2]
            else:
                lanes = pl.ds(0, Z) if form == 1 else pl.ds(Z, LANES)
                src = m.xsend.at[d, :, :, lanes]
                dst = m.xrecv.at[par, 1 - d, :, :, lanes]
        elif d < 4:
            side = d - 2
            if form == 0:
                src = m.ysend.at[side, 0:2]
                dst = m.yrecv.at[par, 1 - side, 0:2]
            else:
                tiles = pl.ds(0, T - 1) if form == 1 else pl.ds(T - 1, 1)
                src = m.ysend.at[side, :, tiles]
                dst = m.yrecv.at[par, 1 - side, :, tiles]
        else:
            src = m.csend.at[d - 4]
            dst = m.crecv.at[par, 7 - d]
        number = d + 8 if form == 2 else d
        arrives = opposite[d] + 8 if form == 2 else opposite[d]
        return remote(
            src, dst, m.f_send.at[number], m.f_recv.at[par, arrives], targets_of[d]
        )

    def each(ds, action):
        for d in ds:

            @pl.when(has[d])
            def _():
                action(d)

    def start(ds, par, form):
        each(ds, lambda d: face(d, par, form).start())

    def sent(ds, par, form):
        each(ds, lambda d: face(d, par, form).wait_send())

    def came(ds, par, form):
        each(ds, lambda d: face(opposite[d], par, form).wait_recv())

    start(range(4), 0, 1)

    def count_copy(axis, step):
        return remote(
            m.nsend.at[axis],
            m.nrecv.at[axis, here[axis]],
            m.n_send.at[axis, step],
            m.n_recv.at[axis, here[axis]],
            line_peer(axis, step),
        )

    def count_start(axis):
        for step in range(1, sizes[axis]):
            count_copy(axis, step).start()
        m.nrecv[axis, here[axis]] = m.nsend[axis]

    def count_finish(axis):
        size = sizes[axis]
        for step in range(1, size):
            count_copy(axis, step).wait_send()
            source = lax.rem(here[axis] + step, size)
            remote(
                m.nsend.at[axis],
                m.nrecv.at[axis, source],
                m.n_send.at[axis, step],
                m.n_recv.at[axis, source],
                line_peer(axis, step),
            ).wait_recv()
        total = m.nrecv[axis, 0]
        for i in range(1, size):
            total = total + m.nrecv[axis, i]
        return total

    count_start(0)

    tiles = X * Y // LANES
    narrow = lax.broadcasted_iota(jnp.int32, (8, LANES), 1)

    def turn(field):
        for x in range(X):
            for half in range(Z // LANES):
                m.rows[half, pl.ds(x, Y, stride=X), :] = field[
                    x, :, half * LANES : (half + 1) * LANES
                ]
        for half in range(Z // LANES):
            for tile in range(tiles):
                m.turned[tile, half * LANES : (half + 1) * LANES, :] = m.rows[
                    half, tile * LANES : (tile + 1) * LANES, :
                ].T

    def pick_one(s, tile, k, by):
        first = m.turned[tile, pl.ds(k, 8), :]
        second = m.turned[tile + 1, pl.ds(k, 8), :]
        back = lax.rem(LANES - by, LANES)
        m.picked[pl.ds(pl.multiple_of(s * 8, 8), 8), :] = jnp.where(
            narrow < LANES - by,
            pltpu.roll(first, back, 1),
            pltpu.roll(second, back, 1),
        )

    def pick_inputs(s, carry):
        anchor = anchor_ref[s]
        i = anchor // (Y * Z)
        j = lax.rem(anchor // Z, Y)
        k = lax.rem(anchor, Z)
        shift = j * X + i
        tile, by = shift // LANES, lax.rem(shift, LANES)
        m.where[0, s] = tile
        m.where[1, s] = k
        m.where[2, s] = by
        pick_one(s, tile, k, by)
        return carry

    def pick_targets(s, carry):
        pick_one(s, m.where[0, s], m.where[1, s], m.where[2, s])
        return carry

    def picked_values():
        return jnp.concatenate(
            [m.picked[pl.ds(c, slots, stride=8), :] for c in range(8)], axis=1
        )

    def swap(ref, number):
        return remote(
            ref.at[0:slots],
            ref.at[slots : 2 * slots],
            m.p_send.at[number],
            m.p_recv.at[number],
            partner,
        )

    m.turned[tiles] = jnp.zeros((Z, LANES), F32)
    turn(now_ref)

    @pl.when(gz < nz - 1)
    def _():
        z_copy(0).wait_send()
        z_copy(1).wait_recv()

    @pl.when(gz > 0)
    def _():
        z_copy(1).wait_send()
        z_copy(0).wait_recv()

    def unpack(x, carry):
        for i, (field, at) in enumerate(((A, 2), (B, 2), (C, 1))):
            before = pltpu.roll(m.zrecv[0, i], lax.rem(120 + LANES - x * 8, LANES), 1)
            after = pltpu.roll(m.zrecv[1, i], lax.rem(LANES - x * 8, LANES), 1)
            value = jnp.where(lane < 8, after, jnp.where(lane >= 120, before, 0.0))
            field[x + at, :, Z:W] = value
            put_rows((0, 2, 3)[i], x, value, last_tile, i == 0)
        return carry

    lax.fori_loop(0, X, unpack, 0)

    def put_lines():
        for i in range(4):
            plane = 2 if i < 2 else X + 1
            at = 0 if i % 2 == 0 else Y - 1
            m.csend[i] = A[plane, at : at + 1, :]

    stage_planes(edge)
    put_lines()
    start(range(4, 8), 0, 0)
    start(range(4), 0, 2)

    lax.fori_loop(0, slots, pick_inputs, 0, unroll=8)
    at = lax.broadcasted_iota(jnp.int32, (8 * LANES, wide), 0)
    feature = lax.broadcasted_iota(jnp.int32, (8 * LANES, wide), 1)
    pa = jnp.bitwise_and(at, X - 1)
    pb = jnp.bitwise_and(lax.shift_right_logical(at, 4), 7)
    pc = lax.shift_right_logical(at, 7)
    m.order[...] = jnp.where(
        (pa < PATCH) & (feature == pa * 64 + pb * 8 + pc), 1.0, 0.0
    ).astype(BF16)
    m.inputs[0:slots] = in_order(picked_values(), m.order[...], 3)
    swap(m.inputs, 0).start()

    root = 0.7978845608028654

    def forward(part):
        rows = slice(part * slots, (part + 1) * slots)
        inputs = m.inputs[rows]
        mean = jnp.mean(inputs * inputs, axis=1, keepdims=True)
        normed = (inputs * lax.rsqrt(mean + 1e-06)).astype(BF16)
        pre = matmul(normed, m.w_in[...], ((1,), (0,)))
        tanh = jnp.tanh(root * (pre + 0.044715 * (pre * pre * pre)))
        cdf = 0.5 * (1.0 + tanh)
        act = (pre * cdf).astype(BF16)
        m.act[rows] = act
        m.slope[rows] = cdf + 0.5 * pre * (1.0 - tanh * tanh) * (
            root * (1.0 + (3.0 * 0.044715) * (pre * pre))
        )
        m.base[rows] = inputs + matmul(act, m.w_out[...], ((1,), (0,)))
        source = lax.broadcasted_iota(jnp.int32, (wide, wide // 2), 0)
        column = lax.broadcasted_iota(jnp.int32, (wide, wide // 2), 1)
        block = lax.shift_right_logical(column, 6) * 2 + core
        chosen = jnp.where(
            source == block * 64 + jnp.bitwise_and(column, 63), 1.0, 0.0
        ).astype(BF16)
        m.normed[rows] = matmul(normed, chosen, ((1,), (0,))).astype(BF16)

    def backward(part, count):
        rows = slice(part * slots, (part + 1) * slots)
        err = m.base[rows] - m.targets[rows]
        slot = lax.broadcasted_iota(jnp.int32, (slots, 1), 0).astype(F32)
        valid = (slot < count).astype(F32)
        dout = (2.0 * err * valid / m.total[0:1, 0:1]).astype(BF16)
        m.dout[rows] = dout
        dact = matmul(dout, m.w_out[...], ((1,), (1,)))
        m.dpre[rows] = (dact * m.slope[rows]).astype(BF16)

    for r in range(STEPS // 2):
        par = r % 2
        if r == 0:
            came(range(4), 0, 1)
            came(range(4), 0, 2)
        else:
            came(range(4), par, 0)
        came(range(4, 8), par, 0)
        A[0:2] = m.xrecv[par, 0, 0:2]
        A[X + 2 : X + 4] = m.xrecv[par, 1, 0:2]
        if r == 0:
            B[1] = m.xrecv[0, 0, 2]
            B[X + 2] = m.xrecv[0, 1, 2]
            C[0] = m.xrecv[0, 0, 3]
            C[X + 1] = m.xrecv[0, 1, 3]
            m.yold[...] = m.yrecv[0, :, 2]
            m.ycoef[...] = m.yrecv[0, :, 3]

        def whole(parts):
            return jnp.concatenate(parts, axis=1)

        def update(field, plane, low_row, high_row, old, coef):
            n = field[plane]
            beside = field[plane + 1] + field[plane - 1]
            beside = beside + jnp.where(row == Y - 1, high_row, pltpu.roll(n, Y - 1, 0))
            beside = beside + jnp.where(row == 0, low_row, pltpu.roll(n, 1, 0))
            beside = beside + pltpu.roll(n, W - 1, 1) + pltpu.roll(n, 1, 1)
            return 2.0 * n - old + coef * (beside - 6.0 * n)

        def side_row(ref, index, x):
            return whole([ref[(*index, tile, pl.ds(x, 1), slice(None))] for tile in range(T)])

        def first(x, carry):
            B[x + 2] = update(
                A,
                x + 2,
                side_row(m.yrecv, (par, 0, 0), x),
                side_row(m.yrecv, (par, 1, 0), x),
                B[x + 2],
                C[x + 1],
            )
            return carry

        lax.fori_loop(0, X, first, 0)
        for plane, lines in ((1, (0, 1)), (X + 2, (2, 3))):
            B[plane] = update(
                A,
                plane,
                m.crecv[par, lines[0]],
                m.crecv[par, lines[1]],
                B[plane],
                C[plane - 1],
            )
        across = lax.broadcasted_iota(jnp.int32, (X, W), 0)
        for side in range(2):

            def plane_of(ref, *index):
                return whole([ref[(*index, tile)] for tile in range(T)])

            n = plane_of(m.yrecv, par, side, 0)
            outer = plane_of(m.yrecv, par, side, 1)
            inner = plane_of(m.ysend, side, 0)
            plus, minus = (inner, outer) if side == 0 else (outer, inner)
            beside = jnp.where(
                across == X - 1, m.crecv[par, 2 + side], pltpu.roll(n, X - 1, 0)
            )
            beside = beside + jnp.where(
                across == 0, m.crecv[par, side], pltpu.roll(n, 1, 0)
            )
            beside = beside + plus + minus
            beside = beside + pltpu.roll(n, W - 1, 1) + pltpu.roll(n, 1, 1)
            value = (
                2.0 * n
                - plane_of(m.yold, side)
                + plane_of(m.ycoef, side) * (beside - 6.0 * n)
            )
            for tile in range(T):
                m.yold[side, tile] = value[:, tile * LANES : (tile + 1) * LANES]
        if r == 0:
            sent(range(4), 0, 1)
            sent(range(4), 0, 2)
        else:
            sent(range(4), par, 0)
        sent(range(4, 8), par, 0)
        final_round = r == STEPS // 2 - 1

        def second(x, carry):
            after = update(
                B,
                x + 2,
                side_row(m.yold, (0,), x),
                side_row(m.yold, (1,), x),
                A[x + 2],
                C[x + 1],
            )
            if final_round:
                out_ref[x] = after[:, 0:Z]
            else:
                A[x + 2] = after
                put_rows(0, x, after, range(T), True)
            return carry

        lax.fori_loop(0, X, second, 0)
        if not final_round:
            put_lines()
            start(range(4, 8), 1 - par, 0)
            start(range(4), 1 - par, 0)
        if r == 0:
            load_in.wait()
            load_out.wait()
            forward(0)
            m.nsend[1] = count_finish(0)
            count_start(1)
        if r == 1:
            swap(m.inputs, 0).wait()
            forward(1)
            m.nsend[2] = count_finish(1)
            count_start(2)
        if r == 2:
            m.total[...] = count_finish(2)

    turn(out_ref)
    lax.fori_loop(0, slots, pick_targets, 0, unroll=8)
    m.targets[0:slots] = in_order(picked_values(), m.order[...], 2)
    swap(m.targets, 1).start()
    backward(0, m.nrecv[0, gx][0:1, 0:1])
    swap(m.targets, 1).wait()
    backward(1, m.nrecv[0, high * 2 + 1 - core][0:1, 0:1])
    grad_in = matmul(m.normed[...], m.dpre[...], ((0,), (0,)))
    dout = m.dout[...]
    for h in range(4):
        block = pl.multiple_of((h * 2 + core) * LANES, LANES)
        grad_out = matmul(m.act[:, pl.ds(block, LANES)], dout, ((0,), (0,)))
        m.sums[h, 0:64] = grad_in[h * 64 : (h + 1) * 64]
        m.sums[h, 64:128, 0:512] = grad_out[0:64]
        m.sums[h, 64:128, 512:1024] = grad_out[64:128]

    half = 512
    places = ((gz, lambda v: device(x=v)), (y, lambda v: device(y=v)))

    def ring(stage, colour, source, rows, relay, fin, send, sems):
        along = colour if stage == 0 else 1 - colour
        me, to = places[along]
        plus, minus, opposed = [lax.rem(me + d, 4) for d in (1, 3, 2)]

        def chunk(owner):
            return pl.ds(pl.multiple_of(owner * rows, 8), rows)

        begin, end = pl.ds(0, 2), pl.ds(2, 2)

        def piece(part, owner):
            return source(part, chunk(owner))

        def copy(src, dst, number, peer):
            return remote(
                src,
                dst,
                sems.at[colour, 0, number],
                sems.at[colour, 1, number],
                to(peer),
            )

        copies = [
            copy(piece(begin, opposed), relay.at[colour, 0], 0, plus),
            copy(piece(end, opposed), relay.at[colour, 1], 1, minus),
            copy(piece(end, plus), fin.at[colour, 0, end], 2, plus),
            copy(piece(begin, minus), fin.at[colour, 1, begin], 3, minus),
            copy(send.at[colour, 0], fin.at[colour, 0, begin], 4, plus),
            copy(send.at[colour, 1], fin.at[colour, 1, end], 5, minus),
        ]

        def open_ring():
            for one in copies[:4]:
                one.start()

        def pass_on():
            copies[0].wait_recv()
            send[colour, 0] = relay[colour, 0] + piece(begin, plus)[...]
            copies[4].start()
            copies[1].wait_recv()
            send[colour, 1] = relay[colour, 1] + piece(end, minus)[...]
            copies[5].start()

        def close_ring():
            for one in copies[2:]:
                one.wait_recv()
            own = piece(pl.ds(0, 4), me)[...]
            total = own + fin[colour, 0] + fin[colour, 1]
            for one in copies:
                one.wait_send()
            return total

        return open_ring, pass_on, close_ring

    def source1(colour):
        return lambda part, rows: m.sums.at[part, rows, pl.ds(colour * half, half)]

    def source2(colour):
        return lambda part, rows: m.held1.at[colour, part, rows, :]

    stage1 = [
        ring(0, colour, source1(colour), 32, m.relay1, m.fin1, m.send1, m.sems1)
        for colour in range(2)
    ]
    stage2 = [
        ring(1, colour, source2(colour), 8, m.relay2, m.fin2, m.send2, m.sems2)
        for colour in range(2)
    ]
    for rings, held in ((stage1, m.held1), (stage2, m.held2)):
        for one in rings:
            one[0]()
        for one in rings:
            one[1]()
        for colour, one in enumerate(rings):
            held[colour] = one[2]()

    z_me = high * 2 + low
    quarter = half // 2

    def z_piece(h, l):
        return m.held2.at[:, h, :, pl.ds(pl.multiple_of(l * quarter, quarter), quarter)]

    z_copies = []
    for number, (h, l) in enumerate(z_steps):
        ph, pw = lax.rem(high + h, 4), lax.rem(low + l, 2)
        peer = device(high=ph, low=pw)
        one = remote(
            z_piece(ph, pw),
            m.zgot.at[z_me],
            m.zp_send.at[number],
            m.zp_recv.at[z_me],
            peer,
        )
        one.start()
        z_copies.append((one, ph * 2 + pw, peer))
    m.zgot[z_me] = z_piece(high, low)[...]
    for one, slot, peer in z_copies:
        remote(
            z_piece(high, low),
            m.zgot.at[slot],
            m.zp_send.at[0],
            m.zp_recv.at[slot],
            peer,
        ).wait_recv()
    total = m.zgot[0]
    for slot in range(1, 8):
        total = total + m.zgot[slot]
    g_me = (gz * 4 + y) * 2 + low
    m.gathered[g_me] = total
    g_copies = []
    for number, (i, j, l) in enumerate(g_steps):
        px, py, pw = lax.rem(gz + i, 4), lax.rem(y + j, 4), lax.rem(low + l, 2)
        peer = device(x=px, y=py, low=pw)
        one = remote(
            m.gathered.at[g_me],
            m.gathered.at[g_me],
            m.g_send.at[number],
            m.g_recv.at[g_me],
            peer,
        )
        one.start()
        g_copies.append((one, (px * 4 + py) * 2 + pw, peer))
    for one, slot, peer in z_copies:
        one.wait_send()
    for one, slot, peer in g_copies:
        remote(
            m.gathered.at[slot],
            m.gathered.at[slot],
            m.g_send.at[0],
            m.g_recv.at[slot],
            peer,
        ).wait_recv()
    sum_ref[...] = m.gathered[...]
    for one, slot, peer in g_copies:
        one.wait_send()


def step(prev, now, material, table, used, anchors, w_in, w_out, sizes):
    X, Y, Z = now.shape
    W = Z + LANES
    T = W // LANES
    slots = anchors.shape[0]
    wide, hidden = w_in.shape
    vmem = pl.BlockSpec(memory_space=pltpu.VMEM)
    smem = pl.BlockSpec(memory_space=pltpu.SMEM)
    anywhere = pl.BlockSpec(memory_space=pl.ANY)
    dma = pltpu.SemaphoreType.DMA
    most = max(sizes)

    def f32(*shape):
        return pltpu.VMEM(shape, F32)

    def b16(*shape):
        return pltpu.VMEM(shape, BF16)

    scratch = dict(
        A=f32(X + 4, Y, W),
        B=f32(X + 4, Y, W),
        C=f32(X + 2, Y, W),
        xsend=f32(2, 4, Y, W),
        xrecv=f32(2, 2, 4, Y, W),
        ysend=f32(2, 4, T, X, LANES),
        yrecv=f32(2, 2, 4, T, X, LANES),
        yold=f32(2, T, X, LANES),
        ycoef=f32(2, T, X, LANES),
        csend=f32(4, 1, W),
        crecv=f32(2, 4, 1, W),
        zsend=f32(2, 3, Y, LANES),
        zrecv=f32(2, 3, Y, LANES),
        nsend=f32(3, 8, LANES),
        nrecv=f32(3, most, 8, LANES),
        total=f32(8, LANES),
        rows=f32(Z // LANES, X * Y, LANES),
        turned=f32(X * Y // LANES + 1, Z, LANES),
        picked=f32(8 * slots, LANES),
        where=pltpu.SMEM((3, slots), jnp.int32),
        order=b16(8 * LANES, wide),
        w_in=b16(wide, hidden),
        w_out=b16(hidden, wide),
        inputs=f32(2 * slots, wide),
        targets=f32(2 * slots, wide),
        base=f32(2 * slots, wide),
        normed=b16(2 * slots, wide // 2),
        act=b16(2 * slots, hidden),
        slope=f32(2 * slots, hidden),
        dout=b16(2 * slots, wide),
        dpre=b16(2 * slots, hidden),
        sums=f32(4, 128, 1024),
        relay1=f32(2, 2, 2, 32, 512),
        fin1=f32(2, 2, 4, 32, 512),
        send1=f32(2, 2, 2, 32, 512),
        held1=f32(2, 4, 32, 512),
        relay2=f32(2, 2, 2, 8, 512),
        fin2=f32(2, 2, 4, 8, 512),
        send2=f32(2, 2, 2, 8, 512),
        held2=f32(2, 4, 8, 512),
        zgot=f32(8, 2, 8, 256),
        gathered=f32(32, 2, 8, 256),
        load=dma((2,)),
        z_sem=dma((2, 2)),
        f_send=dma((12,)),
        f_recv=dma((2, 12)),
        n_send=dma((3, most)),
        n_recv=dma((3, most)),
        p_send=dma((2,)),
        p_recv=dma((2,)),
        sems1=dma((2, 2, 6)),
        sems2=dma((2, 2, 6)),
        zp_send=dma((7,)),
        zp_recv=dma((8,)),
        g_send=dma((31,)),
        g_recv=dma((32,)),
    )
    return pl.pallas_call(
        functools.partial(step_kernel, tuple(scratch), sizes),
        name="step",
        out_shape=(
            jax.ShapeDtypeStruct((X, Y, Z), F32),
            jax.ShapeDtypeStruct((32, 2, 8, 256), F32),
        ),
        in_specs=[vmem, vmem, vmem, smem, smem, smem, anywhere, anywhere],
        out_specs=(vmem, vmem),
        scratch_shapes=list(scratch.values()),
        compiler_params=pltpu.CompilerParams(
            collective_id=0,
            has_side_effects=True,
            vmem_limit_bytes=48 * 1024 * 1024,
        ),
    )(prev, now, material, table, used, anchors, w_in, w_out)


def place_kernel(final_ref, sum_ref, final_out, in_ref, out_ref):
    final_out[...] = final_ref[...]
    for slot in range(32):
        ix, iy, il = slot // 8, slot // 2 % 4, slot % 2
        for colour in range(2):
            row = ix * 32 + iy * 8 if colour == 0 else iy * 32 + ix * 8
            at = colour * 512 + il * 256
            value = sum_ref[slot, colour]
            if row < 64:
                in_ref[row : row + 8, at : at + 256] = value
            else:
                top = row - 64 + (64 if at >= 512 else 0)
                left = at % 512
                out_ref[top : top + 8, left : left + 256] = value


def place(final, sums):
    vmem = pl.BlockSpec(memory_space=pltpu.VMEM)
    return pl.pallas_call(
        place_kernel,
        name="place",
        out_shape=(
            jax.ShapeDtypeStruct(final.shape, F32),
            jax.ShapeDtypeStruct((64, 1024), F32),
            jax.ShapeDtypeStruct((128, 512), F32),
        ),
        in_specs=[vmem, vmem],
        out_specs=(vmem, vmem, vmem),
    )(final, sums)


def body(pressure_prev, pressure_now, material, speed_table, anchors, counts, w_in, w_out):
    sizes = tuple(lax.axis_size(axis) for axis in AXES)
    final, sums = step(
        pressure_prev,
        pressure_now,
        material,
        speed_table,
        counts.reshape(-1),
        anchors.reshape(-1),
        w_in,
        w_out,
        sizes,
    )
    return place(final, sums)


def solution(mesh):
    return jax.shard_map(
        body,
        mesh=mesh,
        in_specs=(
            P("gx", "gy", "gz"),
            P("gx", "gy", "gz"),
            P("gx", "gy", "gz"),
            P(),
            P("gx", "gy", "gz"),
            P("gx", "gy", "gz"),
            P(),
            P(),
        ),
        out_specs=(P("gx", "gy", "gz"), P("gx", None), P("gx", None)),
        check_vma=False,
    )
```

```python
import functools
import types

import jax
import jax.numpy as jnp
from jax import lax
from jax.experimental import pallas as pl
from jax.experimental.pallas import tpu as pltpu
from jax.sharding import PartitionSpec as P

STEPS = 8
PATCH = 8
LANES = 128
AXES = ("gx", "gy", "gz")
F32 = jnp.float32
BF16 = jnp.bfloat16


def remote(src, dst, send_sem, recv_sem, device):
    return pltpu.make_async_remote_copy(
        src_ref=src,
        dst_ref=dst,
        send_sem=send_sem,
        recv_sem=recv_sem,
        device_id=device,
        device_id_type=pl.DeviceIdType.MESH,
    )


def signal(sem, device):
    pl.semaphore_signal(
        sem, inc=1, device_id=device, device_id_type=pl.DeviceIdType.MESH
    )


def matmul(a, b, dims):
    return lax.dot_general(a, b, (dims, ((), ())), preferred_element_type=F32)


def in_order(values, order, parts):
    total = None
    rest = values
    for part in range(parts):
        piece = rest.astype(BF16)
        if part < parts - 1:
            rest = rest - piece.astype(F32)
        term = matmul(piece, order, ((1,), (0,)))
        total = term if total is None else total + term
    return total


def step_kernel(
    names,
    sizes,
    prev_hbm,
    now_hbm,
    mat_hbm,
    tab_ref,
    cnt_ref,
    anchor_ref,
    win_hbm,
    wout_hbm,
    out_ref,
    sum_ref,
    *scratch,
):
    m = types.SimpleNamespace(**dict(zip(names, scratch)))
    nx, ny, nz = sizes
    gx, gy, gz = [lax.axis_index(axis) for axis in AXES]
    here = (gx, gy, gz)
    core, high = lax.rem(gx, 2), gx // 2
    low, y = lax.rem(gy, 2), gy // 2
    X, Y, Z = now_hbm.shape
    W = Z + LANES
    T = W // LANES
    slots = anchor_ref.shape[0]
    wide, hidden = win_hbm.shape
    A, B, C = m.A, m.B, m.C

    def device(core=core, high=high, low=low, y=y, x=gz):
        return (high * 2 + core, y * 2 + low, x)

    def line_peer(axis, step):
        place = list(here)
        place[axis] = lax.rem(here[axis] + step, sizes[axis])
        return tuple(place)

    partner = device(core=1 - core)

    barrier = pltpu.get_barrier_semaphore()
    z_steps = [(h, l) for h in range(4) for l in range(2) if h or l]
    g_steps = [
        (i, j, l) for i in range(4) for j in range(4) for l in range(2) if i or j or l
    ]
    reached = []
    for axis in range(3):
        for step in range(1, sizes[axis]):
            reached.append(line_peer(axis, step))
    for dx in (nx - 1, 1):
        for dy in (ny - 1, 1):
            reached.append((lax.rem(gx + dx, nx), lax.rem(gy + dy, ny), gz))
    for h, l in z_steps:
        if h and l:
            reached.append(
                device(high=lax.rem(high + h, 4), low=lax.rem(low + l, 2))
            )
    for i, j, l in g_steps:
        if i and (j or l):
            reached.append(
                device(
                    x=lax.rem(gz + i, 4), y=lax.rem(y + j, 4), low=lax.rem(low + l, 2)
                )
            )

    bricks = (slice(2, X + 2), slice(None), slice(0, Z))
    loads = [
        pltpu.make_async_copy(mat_hbm, m.mat, m.load.at[2]),
        pltpu.make_async_copy(now_hbm, A.at[bricks], m.load.at[3]),
        pltpu.make_async_copy(prev_hbm, B.at[bricks], m.load.at[4]),
    ]
    for one in loads:
        one.start()
    load_in = pltpu.make_async_copy(win_hbm, m.w_in, m.load.at[0])
    load_out = pltpu.make_async_copy(wout_hbm, m.w_out, m.load.at[1])
    load_in.start()
    load_out.start()

    m.xrecv[...] = jnp.zeros(m.xrecv.shape, F32)
    m.yrecv[...] = jnp.zeros(m.yrecv.shape, F32)
    m.zrecv[...] = jnp.zeros(m.zrecv.shape, F32)
    m.crecv[...] = jnp.zeros(m.crecv.shape, F32)
    for place in reached:
        signal(barrier, place)

    lane = lax.broadcasted_iota(jnp.int32, (Y, LANES), 1)
    row = lax.broadcasted_iota(jnp.int32, (Y, W), 0)

    def put_rows(entry, x, value, tiles, first):
        for side, at in ((0, 0), (1, Y - 1)):
            for k, tile in enumerate(tiles):
                m.ysend[side, entry, tile, pl.ds(x, 1), :] = value[
                    at : at + 1, k * LANES : (k + 1) * LANES
                ]
                if first:
                    at2 = at + 1 - 2 * side
                    m.ysend[side, 1, tile, pl.ds(x, 1), :] = value[
                        at2 : at2 + 1, k * LANES : (k + 1) * LANES
                    ]

    inner_tiles = range(Z // LANES)
    last_tile = range(Z // LANES, T)

    for one in loads:
        one.wait()

    def pack(x, carry):
        material = m.mat[x]
        c = jnp.zeros((Y, Z), F32)
        for number in range(tab_ref.shape[0]):
            c = jnp.where(material == number, tab_ref[number], c)
        n, p = A[x + 2, :, 0:Z], B[x + 2, :, 0:Z]
        C[x + 1, :, 0:Z] = c
        put_rows(0, x, n, inner_tiles, True)
        put_rows(2, x, p, inner_tiles, False)
        put_rows(3, x, c, inner_tiles, False)
        mine = lax.shift_right_logical(lane, 3) == x
        up, down = [], []
        for field, held_up, held_down in zip((n, p, c), carry[0], carry[1]):
            last = pltpu.roll(field[:, Z - LANES :], lax.rem(x * 8 + 8, LANES), 1)
            first = pltpu.roll(field[:, :LANES], x * 8, 1)
            up.append(jnp.where(mine, last, held_up))
            down.append(jnp.where(mine, first, held_down))
        return tuple(up), tuple(down)

    empty = tuple(jnp.zeros((Y, LANES), F32) for _ in range(3))
    ups, downs = lax.fori_loop(0, X, pack, (empty, empty))
    for i in range(3):
        m.zsend[0, i] = ups[i]
        m.zsend[1, i] = downs[i]

    def stage_planes(lanes):
        sources = (
            ((A, 2), (A, 3), (B, 2), (C, 1)),
            ((A, X), (A, X + 1), (B, X + 1), (C, X)),
        )
        for side in range(2):
            for entry, (field, plane) in enumerate(sources[side]):
                m.xsend[side, entry, :, lanes] = field[plane, :, lanes]

    main, edge = slice(0, Z), slice(Z, W)
    stage_planes(main)
    m.nsend[0] = jnp.full((8, LANES), cnt_ref[0].astype(F32))

    pl.semaphore_wait(barrier, len(reached))

    def z_copy(side):
        step = 1 if side == 0 else nz - 1
        return remote(
            m.zsend.at[side],
            m.zrecv.at[side],
            m.z_sem.at[0, side],
            m.z_sem.at[1, side],
            (gx, gy, lax.rem(gz + step, nz)),
        )

    @pl.when(gz < nz - 1)
    def _():
        z_copy(0).start()

    @pl.when(gz > 0)
    def _():
        z_copy(1).start()

    left, right = lax.rem(gx + nx - 1, nx), lax.rem(gx + 1, nx)
    below, above = lax.rem(gy + ny - 1, ny), lax.rem(gy + 1, ny)
    targets_of = (
        (left, gy, gz),
        (right, gy, gz),
        (gx, below, gz),
        (gx, above, gz),
        (left, below, gz),
        (left, above, gz),
        (right, below, gz),
        (right, above, gz),
    )
    sides = (gx > 0, gx < nx - 1, gy > 0, gy < ny - 1)
    has = sides + tuple(
        jnp.logical_and(sides[i], sides[j]) for i in (0, 1) for j in (2, 3)
    )
    opposite = (1, 0, 3, 2, 7, 6, 5, 4)

    def face(d, par, form):
        if d < 2:
            if form == 0:
                src = A.at[2:4] if d == 0 else A.at[X : X + 2]
                dst = m.xrecv.at[par, 1 - d, 0:2]
            else:
                lanes = pl.ds(0, Z) if form == 1 else pl.ds(Z, LANES)
                src = m.xsend.at[d, :, :, lanes]
                dst = m.xrecv.at[par, 1 - d, :, :, lanes]
        elif d < 4:
            side = d - 2
            if form == 0:
                src = m.ysend.at[side, 0:2]
                dst = m.yrecv.at[par, 1 - side, 0:2]
            else:
                tiles = pl.ds(0, T - 1) if form == 1 else pl.ds(T - 1, 1)
                src = m.ysend.at[side, :, tiles]
                dst = m.yrecv.at[par, 1 - side, :, tiles]
        else:
            src = m.csend.at[d - 4]
            dst = m.crecv.at[par, 7 - d]
        number = d + 8 if form == 2 else d
        arrives = opposite[d] + 8 if form == 2 else opposite[d]
        return remote(
            src, dst, m.f_send.at[number], m.f_recv.at[par, arrives], targets_of[d]
        )

    def each(ds, action):
        for d in ds:

            @pl.when(has[d])
            def _():
                action(d)

    def start(ds, par, form):
        each(ds, lambda d: face(d, par, form).start())

    def sent(ds, par, form):
        each(ds, lambda d: face(d, par, form).wait_send())

    def came(ds, par, form):
        each(ds, lambda d: face(opposite[d], par, form).wait_recv())

    start(range(4), 0, 1)

    def count_copy(axis, step):
        return remote(
            m.nsend.at[axis],
            m.nrecv.at[axis, here[axis]],
            m.n_send.at[axis, step],
            m.n_recv.at[axis, here[axis]],
            line_peer(axis, step),
        )

    def count_start(axis):
        for step in range(1, sizes[axis]):
            count_copy(axis, step).start()
        m.nrecv[axis, here[axis]] = m.nsend[axis]

    def count_finish(axis):
        size = sizes[axis]
        for step in range(1, size):
            count_copy(axis, step).wait_send()
            source = lax.rem(here[axis] + step, size)
            remote(
                m.nsend.at[axis],
                m.nrecv.at[axis, source],
                m.n_send.at[axis, step],
                m.n_recv.at[axis, source],
                line_peer(axis, step),
            ).wait_recv()
        total = m.nrecv[axis, 0]
        for i in range(1, size):
            total = total + m.nrecv[axis, i]
        return total

    count_start(0)

    tiles = X * Y // LANES
    narrow = lax.broadcasted_iota(jnp.int32, (8, LANES), 1)

    def turn(field, first):
        for x in range(X):
            for half in range(Z // LANES):
                m.rows[half, pl.ds(x, Y, stride=X), :] = field[
                    x + first, :, half * LANES : (half + 1) * LANES
                ]
        for half in range(Z // LANES):
            for tile in range(tiles):
                m.turned[tile, half * LANES : (half + 1) * LANES, :] = m.rows[
                    half, tile * LANES : (tile + 1) * LANES, :
                ].T

    def pick_one(s, tile, k, by):
        first = m.turned[tile, pl.ds(k, 8), :]
        second = m.turned[tile + 1, pl.ds(k, 8), :]
        back = lax.rem(LANES - by, LANES)
        m.picked[pl.ds(pl.multiple_of(s * 8, 8), 8), :] = jnp.where(
            narrow < LANES - by,
            pltpu.roll(first, back, 1),
            pltpu.roll(second, back, 1),
        )

    def pick_inputs(s, carry):
        anchor = anchor_ref[s]
        i = anchor // (Y * Z)
        j = lax.rem(anchor // Z, Y)
        k = lax.rem(anchor, Z)
        shift = j * X + i
        tile, by = shift // LANES, lax.rem(shift, LANES)
        m.where[0, s] = tile
        m.where[1, s] = k
        m.where[2, s] = by
        pick_one(s, tile, k, by)
        return carry

    def pick_targets(s, carry):
        pick_one(s, m.where[0, s], m.where[1, s], m.where[2, s])
        return carry

    def picked_values():
        return jnp.concatenate(
            [m.picked[pl.ds(c, slots, stride=8), :] for c in range(8)], axis=1
        )

    def swap(ref, number):
        return remote(
            ref.at[0:slots],
            ref.at[slots : 2 * slots],
            m.p_send.at[number],
            m.p_recv.at[number],
            partner,
        )

    m.turned[tiles] = jnp.zeros((Z, LANES), F32)
    turn(A, 2)

    @pl.when(gz < nz - 1)
    def _():
        z_copy(0).wait_send()
        z_copy(1).wait_recv()

    @pl.when(gz > 0)
    def _():
        z_copy(1).wait_send()
        z_copy(0).wait_recv()

    def unpack(x, carry):
        for i, (field, at) in enumerate(((A, 2), (B, 2), (C, 1))):
            before = pltpu.roll(m.zrecv[0, i], lax.rem(120 + LANES - x * 8, LANES), 1)
            after = pltpu.roll(m.zrecv[1, i], lax.rem(LANES - x * 8, LANES), 1)
            value = jnp.where(lane < 8, after, jnp.where(lane >= 120, before, 0.0))
            field[x + at, :, Z:W] = value
            put_rows((0, 2, 3)[i], x, value, last_tile, i == 0)
        return carry

    lax.fori_loop(0, X, unpack, 0)

    def put_lines():
        for i in range(4):
            plane = 2 if i < 2 else X + 1
            at = 0 if i % 2 == 0 else Y - 1
            m.csend[i] = A[plane, at : at + 1, :]

    stage_planes(edge)
    put_lines()
    start(range(4, 8), 0, 0)
    start(range(4), 0, 2)

    lax.fori_loop(0, slots, pick_inputs, 0, unroll=8)
    at = lax.broadcasted_iota(jnp.int32, (8 * LANES, wide), 0)
    feature = lax.broadcasted_iota(jnp.int32, (8 * LANES, wide), 1)
    pa = jnp.bitwise_and(at, X - 1)
    pb = jnp.bitwise_and(lax.shift_right_logical(at, 4), 7)
    pc = lax.shift_right_logical(at, 7)
    m.order[...] = jnp.where(
        (pa < PATCH) & (feature == pa * 64 + pb * 8 + pc), 1.0, 0.0
    ).astype(BF16)
    m.inputs[0:slots] = in_order(picked_values(), m.order[...], 3)
    swap(m.inputs, 0).start()

    root = 0.7978845608028654

    def forward(part):
        rows = slice(part * slots, (part + 1) * slots)
        inputs = m.inputs[rows]
        mean = jnp.mean(inputs * inputs, axis=1, keepdims=True)
        normed = (inputs * lax.rsqrt(mean + 1e-06)).astype(BF16)
        pre = matmul(normed, m.w_in[...], ((1,), (0,)))
        tanh = jnp.tanh(root * (pre + 0.044715 * (pre * pre * pre)))
        cdf = 0.5 * (1.0 + tanh)
        act = (pre * cdf).astype(BF16)
        m.act[rows] = act
        m.slope[rows] = cdf + 0.5 * pre * (1.0 - tanh * tanh) * (
            root * (1.0 + (3.0 * 0.044715) * (pre * pre))
        )
        m.base[rows] = inputs + matmul(act, m.w_out[...], ((1,), (0,)))
        source = lax.broadcasted_iota(jnp.int32, (wide, wide // 2), 0)
        column = lax.broadcasted_iota(jnp.int32, (wide, wide // 2), 1)
        block = lax.shift_right_logical(column, 6) * 2 + core
        chosen = jnp.where(
            source == block * 64 + jnp.bitwise_and(column, 63), 1.0, 0.0
        ).astype(BF16)
        m.normed[rows] = matmul(normed, chosen, ((1,), (0,))).astype(BF16)

    def backward(part, count):
        rows = slice(part * slots, (part + 1) * slots)
        err = m.base[rows] - m.targets[rows]
        slot = lax.broadcasted_iota(jnp.int32, (slots, 1), 0).astype(F32)
        valid = (slot < count).astype(F32)
        dout = (2.0 * err * valid / m.total[0:1, 0:1]).astype(BF16)
        m.dout[rows] = dout
        dact = matmul(dout, m.w_out[...], ((1,), (1,)))
        m.dpre[rows] = (dact * m.slope[rows]).astype(BF16)

    for r in range(STEPS // 2):
        par = r % 2
        if r == 0:
            came(range(4), 0, 1)
            came(range(4), 0, 2)
        else:
            came(range(4), par, 0)
        came(range(4, 8), par, 0)
        A[0:2] = m.xrecv[par, 0, 0:2]
        A[X + 2 : X + 4] = m.xrecv[par, 1, 0:2]
        if r == 0:
            B[1] = m.xrecv[0, 0, 2]
            B[X + 2] = m.xrecv[0, 1, 2]
            C[0] = m.xrecv[0, 0, 3]
            C[X + 1] = m.xrecv[0, 1, 3]
            m.yold[...] = m.yrecv[0, :, 2]
            m.ycoef[...] = m.yrecv[0, :, 3]

        def whole(parts):
            return jnp.concatenate(parts, axis=1)

        def update(field, plane, low_row, high_row, old, coef):
            n = field[plane]
            beside = field[plane + 1] + field[plane - 1]
            beside = beside + jnp.where(row == Y - 1, high_row, pltpu.roll(n, Y - 1, 0))
            beside = beside + jnp.where(row == 0, low_row, pltpu.roll(n, 1, 0))
            beside = beside + pltpu.roll(n, W - 1, 1) + pltpu.roll(n, 1, 1)
            return 2.0 * n - old + coef * (beside - 6.0 * n)

        def side_row(ref, index, x):
            return whole([ref[(*index, tile, pl.ds(x, 1), slice(None))] for tile in range(T)])

        def first(x, carry):
            B[x + 2] = update(
                A,
                x + 2,
                side_row(m.yrecv, (par, 0, 0), x),
                side_row(m.yrecv, (par, 1, 0), x),
                B[x + 2],
                C[x + 1],
            )
            return carry

        lax.fori_loop(0, X, first, 0)
        for plane, lines in ((1, (0, 1)), (X + 2, (2, 3))):
            B[plane] = update(
                A,
                plane,
                m.crecv[par, lines[0]],
                m.crecv[par, lines[1]],
                B[plane],
                C[plane - 1],
            )
        across = lax.broadcasted_iota(jnp.int32, (X, W), 0)
        for side in range(2):

            def plane_of(ref, *index):
                return whole([ref[(*index, tile)] for tile in range(T)])

            n = plane_of(m.yrecv, par, side, 0)
            outer = plane_of(m.yrecv, par, side, 1)
            inner = plane_of(m.ysend, side, 0)
            plus, minus = (inner, outer) if side == 0 else (outer, inner)
            beside = jnp.where(
                across == X - 1, m.crecv[par, 2 + side], pltpu.roll(n, X - 1, 0)
            )
            beside = beside + jnp.where(
                across == 0, m.crecv[par, side], pltpu.roll(n, 1, 0)
            )
            beside = beside + plus + minus
            beside = beside + pltpu.roll(n, W - 1, 1) + pltpu.roll(n, 1, 1)
            value = (
                2.0 * n
                - plane_of(m.yold, side)
                + plane_of(m.ycoef, side) * (beside - 6.0 * n)
            )
            for tile in range(T):
                m.yold[side, tile] = value[:, tile * LANES : (tile + 1) * LANES]
        if r == 0:
            sent(range(4), 0, 1)
            sent(range(4), 0, 2)
        else:
            sent(range(4), par, 0)
        sent(range(4, 8), par, 0)
        final_round = r == STEPS // 2 - 1

        def second(x, carry):
            after = update(
                B,
                x + 2,
                side_row(m.yold, (0,), x),
                side_row(m.yold, (1,), x),
                A[x + 2],
                C[x + 1],
            )
            if final_round:
                out_ref[x] = after[:, 0:Z]
            else:
                A[x + 2] = after
                put_rows(0, x, after, range(T), True)
            return carry

        lax.fori_loop(0, X, second, 0)
        if not final_round:
            put_lines()
            start(range(4, 8), 1 - par, 0)
            start(range(4), 1 - par, 0)
        if r == 0:
            load_in.wait()
            load_out.wait()
            forward(0)
            m.nsend[1] = count_finish(0)
            count_start(1)
        if r == 1:
            swap(m.inputs, 0).wait()
            forward(1)
            m.nsend[2] = count_finish(1)
            count_start(2)
        if r == 2:
            m.total[...] = count_finish(2)

    turn(out_ref, 0)
    lax.fori_loop(0, slots, pick_targets, 0, unroll=8)
    m.targets[0:slots] = in_order(picked_values(), m.order[...], 2)
    swap(m.targets, 1).start()
    backward(0, m.nrecv[0, gx][0:1, 0:1])
    swap(m.targets, 1).wait()
    backward(1, m.nrecv[0, high * 2 + 1 - core][0:1, 0:1])
    grad_in = matmul(m.normed[...], m.dpre[...], ((0,), (0,)))
    dout = m.dout[...]
    for h in range(4):
        block = pl.multiple_of((h * 2 + core) * LANES, LANES)
        grad_out = matmul(m.act[:, pl.ds(block, LANES)], dout, ((0,), (0,)))
        m.sums[h, 0:64] = grad_in[h * 64 : (h + 1) * 64]
        m.sums[h, 64:128, 0:512] = grad_out[0:64]
        m.sums[h, 64:128, 512:1024] = grad_out[64:128]

    half = 512
    places = ((gz, lambda v: device(x=v)), (y, lambda v: device(y=v)))

    def ring(stage, colour, source, rows, relay, fin, send, sems):
        along = colour if stage == 0 else 1 - colour
        me, to = places[along]
        plus, minus, opposed = [lax.rem(me + d, 4) for d in (1, 3, 2)]

        def chunk(owner):
            return pl.ds(pl.multiple_of(owner * rows, 8), rows)

        begin, end = pl.ds(0, 2), pl.ds(2, 2)

        def piece(part, owner):
            return source(part, chunk(owner))

        def copy(src, dst, number, peer):
            return remote(
                src,
                dst,
                sems.at[colour, 0, number],
                sems.at[colour, 1, number],
                to(peer),
            )

        copies = [
            copy(piece(begin, opposed), relay.at[colour, 0], 0, plus),
            copy(piece(end, opposed), relay.at[colour, 1], 1, minus),
            copy(piece(end, plus), fin.at[colour, 0, end], 2, plus),
            copy(piece(begin, minus), fin.at[colour, 1, begin], 3, minus),
            copy(send.at[colour, 0], fin.at[colour, 0, begin], 4, plus),
            copy(send.at[colour, 1], fin.at[colour, 1, end], 5, minus),
        ]

        def open_ring():
            for one in copies[:4]:
                one.start()

        def pass_on():
            copies[0].wait_recv()
            send[colour, 0] = relay[colour, 0] + piece(begin, plus)[...]
            copies[4].start()
            copies[1].wait_recv()
            send[colour, 1] = relay[colour, 1] + piece(end, minus)[...]
            copies[5].start()

        def close_ring():
            for one in copies[2:]:
                one.wait_recv()
            own = piece(pl.ds(0, 4), me)[...]
            total = own + fin[colour, 0] + fin[colour, 1]
            for one in copies:
                one.wait_send()
            return total

        return open_ring, pass_on, close_ring

    def source1(colour):
        return lambda part, rows: m.sums.at[part, rows, pl.ds(colour * half, half)]

    def source2(colour):
        return lambda part, rows: m.held1.at[colour, part, rows, :]

    stage1 = [
        ring(0, colour, source1(colour), 32, m.relay1, m.fin1, m.send1, m.sems1)
        for colour in range(2)
    ]
    stage2 = [
        ring(1, colour, source2(colour), 8, m.relay2, m.fin2, m.send2, m.sems2)
        for colour in range(2)
    ]
    for rings, held in ((stage1, m.held1), (stage2, m.held2)):
        for one in rings:
            one[0]()
        for one in rings:
            one[1]()
        for colour, one in enumerate(rings):
            held[colour] = one[2]()

    z_me = high * 2 + low
    quarter = half // 2

    def z_piece(h, l):
        return m.held2.at[:, h, :, pl.ds(pl.multiple_of(l * quarter, quarter), quarter)]

    z_copies = []
    for number, (h, l) in enumerate(z_steps):
        ph, pw = lax.rem(high + h, 4), lax.rem(low + l, 2)
        peer = device(high=ph, low=pw)
        one = remote(
            z_piece(ph, pw),
            m.zgot.at[z_me],
            m.zp_send.at[number],
            m.zp_recv.at[z_me],
            peer,
        )
        one.start()
        z_copies.append((one, ph * 2 + pw, peer))
    m.zgot[z_me] = z_piece(high, low)[...]
    for one, slot, peer in z_copies:
        remote(
            z_piece(high, low),
            m.zgot.at[slot],
            m.zp_send.at[0],
            m.zp_recv.at[slot],
            peer,
        ).wait_recv()
    total = m.zgot[0]
    for slot in range(1, 8):
        total = total + m.zgot[slot]
    g_me = (gz * 4 + y) * 2 + low
    m.gathered[g_me] = total
    g_copies = []
    for number, (i, j, l) in enumerate(g_steps):
        px, py, pw = lax.rem(gz + i, 4), lax.rem(y + j, 4), lax.rem(low + l, 2)
        peer = device(x=px, y=py, low=pw)
        one = remote(
            m.gathered.at[g_me],
            m.gathered.at[g_me],
            m.g_send.at[number],
            m.g_recv.at[g_me],
            peer,
        )
        one.start()
        g_copies.append((one, (px * 4 + py) * 2 + pw, peer))
    for one, slot, peer in z_copies:
        one.wait_send()
    for one, slot, peer in g_copies:
        remote(
            m.gathered.at[slot],
            m.gathered.at[slot],
            m.g_send.at[0],
            m.g_recv.at[slot],
            peer,
        ).wait_recv()
    sum_ref[...] = m.gathered[...]
    for one, slot, peer in g_copies:
        one.wait_send()


def step(prev, now, material, table, used, anchors, w_in, w_out, sizes):
    X, Y, Z = now.shape
    W = Z + LANES
    T = W // LANES
    slots = anchors.shape[0]
    wide, hidden = w_in.shape
    vmem = pl.BlockSpec(memory_space=pltpu.VMEM)
    smem = pl.BlockSpec(memory_space=pltpu.SMEM)
    hbm = pl.BlockSpec(memory_space=pltpu.HBM)
    dma = pltpu.SemaphoreType.DMA
    most = max(sizes)

    def f32(*shape):
        return pltpu.VMEM(shape, F32)

    def b16(*shape):
        return pltpu.VMEM(shape, BF16)

    scratch = dict(
        A=f32(X + 4, Y, W),
        B=f32(X + 4, Y, W),
        C=f32(X + 2, Y, W),
        xsend=f32(2, 4, Y, W),
        xrecv=f32(2, 2, 4, Y, W),
        ysend=f32(2, 4, T, X, LANES),
        yrecv=f32(2, 2, 4, T, X, LANES),
        yold=f32(2, T, X, LANES),
        ycoef=f32(2, T, X, LANES),
        csend=f32(4, 1, W),
        crecv=f32(2, 4, 1, W),
        zsend=f32(2, 3, Y, LANES),
        zrecv=f32(2, 3, Y, LANES),
        nsend=f32(3, 8, LANES),
        nrecv=f32(3, most, 8, LANES),
        total=f32(8, LANES),
        rows=f32(Z // LANES, X * Y, LANES),
        turned=f32(X * Y // LANES + 1, Z, LANES),
        picked=f32(8 * slots, LANES),
        mat=pltpu.VMEM((X, Y, Z), jnp.int32),
        where=pltpu.SMEM((3, slots), jnp.int32),
        order=b16(8 * LANES, wide),
        w_in=b16(wide, hidden),
        w_out=b16(hidden, wide),
        inputs=f32(2 * slots, wide),
        targets=f32(2 * slots, wide),
        base=f32(2 * slots, wide),
        normed=b16(2 * slots, wide // 2),
        act=b16(2 * slots, hidden),
        slope=f32(2 * slots, hidden),
        dout=b16(2 * slots, wide),
        dpre=b16(2 * slots, hidden),
        sums=f32(4, 128, 1024),
        relay1=f32(2, 2, 2, 32, 512),
        fin1=f32(2, 2, 4, 32, 512),
        send1=f32(2, 2, 2, 32, 512),
        held1=f32(2, 4, 32, 512),
        relay2=f32(2, 2, 2, 8, 512),
        fin2=f32(2, 2, 4, 8, 512),
        send2=f32(2, 2, 2, 8, 512),
        held2=f32(2, 4, 8, 512),
        zgot=f32(8, 2, 8, 256),
        gathered=f32(32, 2, 8, 256),
        load=dma((5,)),
        z_sem=dma((2, 2)),
        f_send=dma((12,)),
        f_recv=dma((2, 12)),
        n_send=dma((3, most)),
        n_recv=dma((3, most)),
        p_send=dma((2,)),
        p_recv=dma((2,)),
        sems1=dma((2, 2, 6)),
        sems2=dma((2, 2, 6)),
        zp_send=dma((7,)),
        zp_recv=dma((8,)),
        g_send=dma((31,)),
        g_recv=dma((32,)),
    )
    return pl.pallas_call(
        functools.partial(step_kernel, tuple(scratch), sizes),
        name="step",
        out_shape=(
            jax.ShapeDtypeStruct((X, Y, Z), F32),
            jax.ShapeDtypeStruct((32, 2, 8, 256), F32),
        ),
        in_specs=[hbm, hbm, hbm, smem, smem, smem, hbm, hbm],
        out_specs=(vmem, vmem),
        scratch_shapes=list(scratch.values()),
        compiler_params=pltpu.CompilerParams(
            collective_id=0,
            has_side_effects=True,
            vmem_limit_bytes=40 * 1024 * 1024,
        ),
    )(prev, now, material, table, used, anchors, w_in, w_out)


def place_kernel(final_ref, sum_ref, final_out, in_ref, out_ref):
    final_out[...] = final_ref[...]
    for slot in range(32):
        ix, iy, il = slot // 8, slot // 2 % 4, slot % 2
        for colour in range(2):
            row = ix * 32 + iy * 8 if colour == 0 else iy * 32 + ix * 8
            at = colour * 512 + il * 256
            value = sum_ref[slot, colour]
            if row < 64:
                in_ref[row : row + 8, at : at + 256] = value
            else:
                top = row - 64 + (64 if at >= 512 else 0)
                left = at % 512
                out_ref[top : top + 8, left : left + 256] = value


def place(final, sums):
    vmem = pl.BlockSpec(memory_space=pltpu.VMEM)
    return pl.pallas_call(
        place_kernel,
        name="place",
        out_shape=(
            jax.ShapeDtypeStruct(final.shape, F32),
            jax.ShapeDtypeStruct((64, 1024), F32),
            jax.ShapeDtypeStruct((128, 512), F32),
        ),
        in_specs=[vmem, vmem],
        out_specs=(vmem, vmem, vmem),
        compiler_params=pltpu.CompilerParams(vmem_limit_bytes=8 * 1024 * 1024),
    )(final, sums)


def body(pressure_prev, pressure_now, material, speed_table, anchors, counts, w_in, w_out):
    sizes = tuple(lax.axis_size(axis) for axis in AXES)
    pressure_prev, pressure_now, material, speed_table, anchors, w_in, w_out = [
        pltpu.with_memory_space_constraint(v, pltpu.HBM)
        for v in (
            pressure_prev,
            pressure_now,
            material,
            speed_table,
            anchors.reshape(-1),
            w_in,
            w_out,
        )
    ]
    final, sums = step(
        pressure_prev,
        pressure_now,
        material,
        speed_table,
        counts.reshape(-1),
        anchors,
        w_in,
        w_out,
        sizes,
    )
    return place(final, sums)


def solution(mesh):
    return jax.shard_map(
        body,
        mesh=mesh,
        in_specs=(
            P("gx", "gy", "gz"),
            P("gx", "gy", "gz"),
            P("gx", "gy", "gz"),
            P(),
            P("gx", "gy", "gz"),
            P("gx", "gy", "gz"),
            P(),
            P(),
        ),
        out_specs=(P("gx", "gy", "gz"), P("gx", None), P("gx", None)),
        check_vma=False,
    )
```

```python
import functools
import types

import jax
import jax.numpy as jnp
from jax import lax
from jax.experimental import pallas as pl
from jax.experimental.pallas import tpu as pltpu
from jax.sharding import PartitionSpec as P

STEPS = 8
PATCH = 8
LANES = 128
R = 32
PAD = 8
AXES = ("gx", "gy", "gz")
F32 = jnp.float32
BF16 = jnp.bfloat16


def remote(src, dst, send_sem, recv_sem, device):
    return pltpu.make_async_remote_copy(
        src_ref=src,
        dst_ref=dst,
        send_sem=send_sem,
        recv_sem=recv_sem,
        device_id=device,
        device_id_type=pl.DeviceIdType.MESH,
    )


def signal(sem, device):
    pl.semaphore_signal(
        sem, inc=1, device_id=device, device_id_type=pl.DeviceIdType.MESH
    )


def matmul(a, b, dims):
    return lax.dot_general(a, b, (dims, ((), ())), preferred_element_type=F32)


def in_order(values, order, parts):
    total = None
    rest = values
    for part in range(parts):
        piece = rest.astype(BF16)
        if part < parts - 1:
            rest = rest - piece.astype(F32)
        term = matmul(piece, order, ((1,), (0,)))
        total = term if total is None else total + term
    return total


def step_kernel(
    names,
    sizes,
    prev_hbm,
    now_hbm,
    mat_hbm,
    tab_ref,
    cnt_ref,
    anchor_ref,
    win_hbm,
    wout_hbm,
    out_ref,
    sum_ref,
    *scratch,
):
    m = types.SimpleNamespace(**dict(zip(names, scratch)))
    nx, ny, nz = sizes
    gx, gy, gz = [lax.axis_index(axis) for axis in AXES]
    here = (gx, gy, gz)
    core, high = lax.rem(gx, 2), gx // 2
    low, y = lax.rem(gy, 2), gy // 2
    X, Y, Z = now_hbm.shape
    W = Z + LANES
    T = W // LANES
    slots = anchor_ref.shape[0]
    wide, hidden = win_hbm.shape
    A, B, C, D = m.A, m.B, m.C, m.D

    def rows_of(p, t, shift=0, count=Y):
        start = p * (T * R) + (PAD + t * R)
        if not isinstance(p, int):
            start = pl.multiple_of(start, 8)
        return pl.ds(start + shift, count)

    def rows_over(t, shift):
        return pl.ds(2 * T * R + PAD + t * R + shift, X, stride=T * R)

    def coef_of(p, t):
        start = p * (T * Y) + t * Y
        if not isinstance(p, int):
            start = pl.multiple_of(start, 8)
        return pl.ds(start, Y)

    def coef_over(t, shift):
        return pl.ds(T * Y + t * Y + shift, X, stride=T * Y)

    def tile_of(t):
        return slice(t * LANES, (t + 1) * LANES)


    def device(core=core, high=high, low=low, y=y, x=gz):
        return (high * 2 + core, y * 2 + low, x)

    def line_peer(axis, step):
        place = list(here)
        place[axis] = lax.rem(here[axis] + step, sizes[axis])
        return tuple(place)

    partner = device(core=1 - core)

    barrier = pltpu.get_barrier_semaphore()
    z_steps = [(h, l) for h in range(4) for l in range(2) if h or l]
    g_steps = [
        (i, j, l) for i in range(4) for j in range(4) for l in range(2) if i or j or l
    ]
    reached = []
    for axis in range(3):
        for step in range(1, sizes[axis]):
            reached.append(line_peer(axis, step))
    for dx in (nx - 1, 1):
        for dy in (ny - 1, 1):
            reached.append((lax.rem(gx + dx, nx), lax.rem(gy + dy, ny), gz))
    for h, l in z_steps:
        if h and l:
            reached.append(
                device(high=lax.rem(high + h, 4), low=lax.rem(low + l, 2))
            )
    for i, j, l in g_steps:
        if i and (j or l):
            reached.append(
                device(
                    x=lax.rem(gz + i, 4), y=lax.rem(y + j, 4), low=lax.rem(low + l, 2)
                )
            )

    loads = [
        pltpu.make_async_copy(mat_hbm, m.mat, m.load.at[2]),
        pltpu.make_async_copy(now_hbm, m.now, m.load.at[3]),
        pltpu.make_async_copy(prev_hbm, m.prev, m.load.at[4]),
    ]
    for one in loads:
        one.start()
    load_in = pltpu.make_async_copy(win_hbm, m.w_in, m.load.at[0])
    load_out = pltpu.make_async_copy(wout_hbm, m.w_out, m.load.at[1])
    load_in.start()
    load_out.start()

    m.xrecv[...] = jnp.zeros(m.xrecv.shape, F32)
    m.yrecv[...] = jnp.zeros(m.yrecv.shape, F32)
    m.zrecv[...] = jnp.zeros(m.zrecv.shape, F32)
    m.crecv[...] = jnp.zeros(m.crecv.shape, F32)
    for place in reached:
        signal(barrier, place)

    lane = lax.broadcasted_iota(jnp.int32, (Y, LANES), 1)
    def put_rows(entries, tiles):
        for side, at, second in ((0, 0, 1), (1, Y - 1, Y - 2)):
            for t in tiles:
                m.ysend[side, 0, t] = A[rows_over(t, at), :]
                m.ysend[side, 1, t] = A[rows_over(t, second), :]
                if entries > 2:
                    m.ysend[side, 2, t] = B[rows_over(t, at), :]
                    m.ysend[side, 3, t] = C[coef_over(t, at), :]

    def put_planes(entries, tiles):
        for side, planes in enumerate(((2, 3, 2, 1), (X, X + 1, X + 1, X))):
            for t in tiles:
                m.xsend[side, 0, t] = A[rows_of(planes[0], t), :]
                m.xsend[side, 1, t] = A[rows_of(planes[1], t), :]
                if entries > 2:
                    m.xsend[side, 2, t] = B[rows_of(planes[2], t), :]
                    m.xsend[side, 3, t] = C[coef_of(planes[3], t), :]

    inner_tiles = range(Z // LANES)
    last_tile = range(Z // LANES, T)

    for one in loads:
        one.wait()

    def pack(x, carry):
        material = m.mat[x]
        c = jnp.zeros((Y, Z), F32)
        for number in range(tab_ref.shape[0]):
            c = jnp.where(material == number, tab_ref[number], c)
        n, p = m.now[x], m.prev[x]
        for t in inner_tiles:
            A[rows_of(x + 2, t), :] = n[:, tile_of(t)]
            B[rows_of(x + 2, t), :] = p[:, tile_of(t)]
            C[coef_of(x + 1, t), :] = c[:, tile_of(t)]
            D[coef_of(x + 1, t), :] = 2.0 - 6.0 * c[:, tile_of(t)]
        mine = lax.shift_right_logical(lane, 3) == x
        up, down = [], []
        for field, held_up, held_down in zip((n, p, c), carry[0], carry[1]):
            last = pltpu.roll(field[:, Z - LANES :], lax.rem(x * 8 + 8, LANES), 1)
            first = pltpu.roll(field[:, :LANES], x * 8, 1)
            up.append(jnp.where(mine, last, held_up))
            down.append(jnp.where(mine, first, held_down))
        return tuple(up), tuple(down)

    empty = tuple(jnp.zeros((Y, LANES), F32) for _ in range(3))
    ups, downs = lax.fori_loop(0, X, pack, (empty, empty))
    for i in range(3):
        m.zsend[0, i] = ups[i]
        m.zsend[1, i] = downs[i]

    put_planes(4, inner_tiles)
    put_rows(4, inner_tiles)
    m.nsend[0] = jnp.full((8, LANES), cnt_ref[0].astype(F32))

    pl.semaphore_wait(barrier, len(reached))

    def z_copy(side):
        step = 1 if side == 0 else nz - 1
        return remote(
            m.zsend.at[side],
            m.zrecv.at[side],
            m.z_sem.at[0, side],
            m.z_sem.at[1, side],
            (gx, gy, lax.rem(gz + step, nz)),
        )

    @pl.when(gz < nz - 1)
    def _():
        z_copy(0).start()

    @pl.when(gz > 0)
    def _():
        z_copy(1).start()

    left, right = lax.rem(gx + nx - 1, nx), lax.rem(gx + 1, nx)
    below, above = lax.rem(gy + ny - 1, ny), lax.rem(gy + 1, ny)
    targets_of = (
        (left, gy, gz),
        (right, gy, gz),
        (gx, below, gz),
        (gx, above, gz),
        (left, below, gz),
        (left, above, gz),
        (right, below, gz),
        (right, above, gz),
    )
    sides = (gx > 0, gx < nx - 1, gy > 0, gy < ny - 1)
    has = sides + tuple(
        jnp.logical_and(sides[i], sides[j]) for i in (0, 1) for j in (2, 3)
    )
    opposite = (1, 0, 3, 2, 7, 6, 5, 4)

    def face(d, par, form):
        if d < 2:
            if form == 0:
                src = m.xsend.at[d, 0:2]
                dst = m.xrecv.at[par, 1 - d, 0:2]
            else:
                tiles = pl.ds(0, T - 1) if form == 1 else pl.ds(T - 1, 1)
                src = m.xsend.at[d, :, tiles]
                dst = m.xrecv.at[par, 1 - d, :, tiles]
        elif d < 4:
            side = d - 2
            if form == 0:
                src = m.ysend.at[side, 0:2]
                dst = m.yrecv.at[par, 1 - side, 0:2]
            else:
                tiles = pl.ds(0, T - 1) if form == 1 else pl.ds(T - 1, 1)
                src = m.ysend.at[side, :, tiles]
                dst = m.yrecv.at[par, 1 - side, :, tiles]
        else:
            src = m.csend.at[d - 4]
            dst = m.crecv.at[par, 7 - d]
        number = d + 8 if form == 2 else d
        arrives = opposite[d] + 8 if form == 2 else opposite[d]
        return remote(
            src, dst, m.f_send.at[number], m.f_recv.at[par, arrives], targets_of[d]
        )

    def each(ds, action):
        for d in ds:

            @pl.when(has[d])
            def _():
                action(d)

    def start(ds, par, form):
        each(ds, lambda d: face(d, par, form).start())

    def sent(ds, par, form):
        each(ds, lambda d: face(d, par, form).wait_send())

    def came(ds, par, form):
        each(ds, lambda d: face(opposite[d], par, form).wait_recv())

    start(range(4), 0, 1)

    def count_copy(axis, step):
        return remote(
            m.nsend.at[axis],
            m.nrecv.at[axis, here[axis]],
            m.n_send.at[axis, step],
            m.n_recv.at[axis, here[axis]],
            line_peer(axis, step),
        )

    def count_start(axis):
        for step in range(1, sizes[axis]):
            count_copy(axis, step).start()
        m.nrecv[axis, here[axis]] = m.nsend[axis]

    def count_finish(axis):
        size = sizes[axis]
        for step in range(1, size):
            count_copy(axis, step).wait_send()
            source = lax.rem(here[axis] + step, size)
            remote(
                m.nsend.at[axis],
                m.nrecv.at[axis, source],
                m.n_send.at[axis, step],
                m.n_recv.at[axis, source],
                line_peer(axis, step),
            ).wait_recv()
        total = m.nrecv[axis, 0]
        for i in range(1, size):
            total = total + m.nrecv[axis, i]
        return total

    count_start(0)

    tiles = X * Y // LANES
    narrow = lax.broadcasted_iota(jnp.int32, (8, LANES), 1)

    def turn(field):
        for x in range(X):
            for half in range(Z // LANES):
                m.rows[half, pl.ds(x, Y, stride=X), :] = field[
                    x, :, half * LANES : (half + 1) * LANES
                ]
        for half in range(Z // LANES):
            for tile in range(tiles):
                m.turned[tile, half * LANES : (half + 1) * LANES, :] = m.rows[
                    half, tile * LANES : (tile + 1) * LANES, :
                ].T

    def pick_one(s, tile, k, by):
        first = m.turned[tile, pl.ds(k, 8), :]
        second = m.turned[tile + 1, pl.ds(k, 8), :]
        back = lax.rem(LANES - by, LANES)
        m.picked[pl.ds(pl.multiple_of(s * 8, 8), 8), :] = jnp.where(
            narrow < LANES - by,
            pltpu.roll(first, back, 1),
            pltpu.roll(second, back, 1),
        )

    def pick_inputs(s, carry):
        anchor = anchor_ref[s]
        i = anchor // (Y * Z)
        j = lax.rem(anchor // Z, Y)
        k = lax.rem(anchor, Z)
        shift = j * X + i
        tile, by = shift // LANES, lax.rem(shift, LANES)
        m.where[0, s] = tile
        m.where[1, s] = k
        m.where[2, s] = by
        pick_one(s, tile, k, by)
        return carry

    def pick_targets(s, carry):
        pick_one(s, m.where[0, s], m.where[1, s], m.where[2, s])
        return carry

    def picked_values():
        return jnp.concatenate(
            [m.picked[pl.ds(c, slots, stride=8), :] for c in range(8)], axis=1
        )

    def swap(ref, number):
        return remote(
            ref.at[0:slots],
            ref.at[slots : 2 * slots],
            m.p_send.at[number],
            m.p_recv.at[number],
            partner,
        )

    m.turned[tiles] = jnp.zeros((Z, LANES), F32)
    turn(m.now)

    @pl.when(gz < nz - 1)
    def _():
        z_copy(0).wait_send()
        z_copy(1).wait_recv()

    @pl.when(gz > 0)
    def _():
        z_copy(1).wait_send()
        z_copy(0).wait_recv()

    def unpack(x, carry):
        values = []
        for i in range(3):
            before = pltpu.roll(m.zrecv[0, i], lax.rem(120 + LANES - x * 8, LANES), 1)
            after = pltpu.roll(m.zrecv[1, i], lax.rem(LANES - x * 8, LANES), 1)
            values.append(
                jnp.where(lane < 8, after, jnp.where(lane >= 120, before, 0.0))
            )
        A[rows_of(x + 2, T - 1), :] = values[0]
        B[rows_of(x + 2, T - 1), :] = values[1]
        C[coef_of(x + 1, T - 1), :] = values[2]
        D[coef_of(x + 1, T - 1), :] = 2.0 - 6.0 * values[2]
        return carry

    lax.fori_loop(0, X, unpack, 0, unroll=2)

    def put_lines():
        for i in range(4):
            plane = 2 if i < 2 else X + 1
            at = 0 if i % 2 == 0 else Y - 1
            for t in range(T):
                m.csend[i, :, tile_of(t)] = A[rows_of(plane, t, at, 1), :]

    put_planes(4, last_tile)
    put_rows(4, last_tile)
    put_lines()
    start(range(4, 8), 0, 0)
    start(range(4), 0, 2)

    lax.fori_loop(0, slots, pick_inputs, 0, unroll=8)
    at = lax.broadcasted_iota(jnp.int32, (8 * LANES, wide), 0)
    feature = lax.broadcasted_iota(jnp.int32, (8 * LANES, wide), 1)
    pa = jnp.bitwise_and(at, X - 1)
    pb = jnp.bitwise_and(lax.shift_right_logical(at, 4), 7)
    pc = lax.shift_right_logical(at, 7)
    m.order[...] = jnp.where(
        (pa < PATCH) & (feature == pa * 64 + pb * 8 + pc), 1.0, 0.0
    ).astype(BF16)
    m.inputs[0:slots] = in_order(picked_values(), m.order[...], 3)
    swap(m.inputs, 0).start()

    root = 0.7978845608028654

    def forward(part):
        rows = slice(part * slots, (part + 1) * slots)
        inputs = m.inputs[rows]
        mean = jnp.mean(inputs * inputs, axis=1, keepdims=True)
        normed = (inputs * lax.rsqrt(mean + 1e-06)).astype(BF16)
        pre = matmul(normed, m.w_in[...], ((1,), (0,)))
        tanh = jnp.tanh(root * (pre + 0.044715 * (pre * pre * pre)))
        cdf = 0.5 * (1.0 + tanh)
        act = (pre * cdf).astype(BF16)
        m.act[rows] = act
        m.slope[rows] = cdf + 0.5 * pre * (1.0 - tanh * tanh) * (
            root * (1.0 + (3.0 * 0.044715) * (pre * pre))
        )
        m.base[rows] = inputs + matmul(act, m.w_out[...], ((1,), (0,)))
        source = lax.broadcasted_iota(jnp.int32, (wide, wide // 2), 0)
        column = lax.broadcasted_iota(jnp.int32, (wide, wide // 2), 1)
        block = lax.shift_right_logical(column, 6) * 2 + core
        chosen = jnp.where(
            source == block * 64 + jnp.bitwise_and(column, 63), 1.0, 0.0
        ).astype(BF16)
        m.normed[rows] = matmul(normed, chosen, ((1,), (0,))).astype(BF16)

    def backward(part, count):
        rows = slice(part * slots, (part + 1) * slots)
        err = m.base[rows] - m.targets[rows]
        slot = lax.broadcasted_iota(jnp.int32, (slots, 1), 0).astype(F32)
        valid = (slot < count).astype(F32)
        dout = (2.0 * err * valid / m.total[0:1, 0:1]).astype(BF16)
        m.dout[rows] = dout
        dact = matmul(dout, m.w_out[...], ((1,), (1,)))
        m.dpre[rows] = (dact * m.slope[rows]).astype(BF16)

    for r in range(STEPS // 2):
        par = r % 2
        if r == 0:
            came(range(4), 0, 1)
            came(range(4), 0, 2)
        else:
            came(range(4), par, 0)
        came(range(4, 8), par, 0)
        for t in range(T):
            for e in range(2):
                A[rows_of(e, t), :] = m.xrecv[par, 0, e, t]
                A[rows_of(X + 2 + e, t), :] = m.xrecv[par, 1, e, t]
            A[rows_over(t, -1), :] = m.yrecv[par, 0, 0, t]
            A[rows_over(t, Y), :] = m.yrecv[par, 1, 0, t]
            for i in range(4):
                plane = 1 if i < 2 else X + 2
                at = -1 if i % 2 == 0 else Y
                A[rows_of(plane, t, at, 1), :] = m.crecv[par, i, :, tile_of(t)]
            if r == 0:
                for side, plane, ring_coef in ((0, 1, 0), (1, X + 2, X + 1)):
                    B[rows_of(plane, t), :] = m.xrecv[0, side, 2, t]
                    c = m.xrecv[0, side, 3, t]
                    C[coef_of(ring_coef, t), :] = c
                    D[coef_of(ring_coef, t), :] = 2.0 - 6.0 * c
        if r == 0:
            m.yold[...] = m.yrecv[0, :, 2]
            m.ycoef[...] = m.yrecv[0, :, 3]

        def whole(parts):
            return jnp.concatenate(parts, axis=1)

        def beside_of(field, p):
            def at(plane, shift):
                return whole([field[rows_of(plane, t, shift), :] for t in range(T)])

            n = at(p, 0)
            beside = at(p + 1, 0) + at(p - 1, 0)
            beside = beside + at(p, 1) + at(p, -1)
            return n, beside + pltpu.roll(n, W - 1, 1) + pltpu.roll(n, 1, 1)

        def update(field, other, p):
            n, beside = beside_of(field, p)
            old = whole([other[rows_of(p, t), :] for t in range(T)])
            c = whole([C[coef_of(p - 1, t), :] for t in range(T)])
            d = whole([D[coef_of(p - 1, t), :] for t in range(T)])
            return d * n - old + c * beside

        def first(p, carry):
            after = update(A, B, p)
            for t in range(T):
                B[rows_of(p, t), :] = after[:, tile_of(t)]
            return carry

        lax.fori_loop(1, X + 3, first, 0, unroll=2)
        across = lax.broadcasted_iota(jnp.int32, (X, W), 0)
        for side in range(2):

            def plane_of(ref, *index):
                return whole([ref[(*index, tile)] for tile in range(T)])

            n = plane_of(m.yrecv, par, side, 0)
            outer = plane_of(m.yrecv, par, side, 1)
            inner = plane_of(m.ysend, side, 0)
            plus, minus = (inner, outer) if side == 0 else (outer, inner)
            beside = jnp.where(
                across == X - 1, m.crecv[par, 2 + side], pltpu.roll(n, X - 1, 0)
            )
            beside = beside + jnp.where(
                across == 0, m.crecv[par, side], pltpu.roll(n, 1, 0)
            )
            beside = beside + plus + minus
            beside = beside + pltpu.roll(n, W - 1, 1) + pltpu.roll(n, 1, 1)
            value = (
                2.0 * n
                - plane_of(m.yold, side)
                + plane_of(m.ycoef, side) * (beside - 6.0 * n)
            )
            for t in range(T):
                m.yold[side, t] = value[:, tile_of(t)]
                B[rows_over(t, -1 if side == 0 else Y), :] = value[:, tile_of(t)]
        if r == 0:
            sent(range(4), 0, 1)
            sent(range(4), 0, 2)
        else:
            sent(range(4), par, 0)
        sent(range(4, 8), par, 0)
        final_round = r == STEPS // 2 - 1

        def second(p, carry):
            after = update(B, A, p)
            if final_round:
                out_ref[p - 2] = after[:, 0:Z]
            else:
                for t in range(T):
                    A[rows_of(p, t), :] = after[:, tile_of(t)]
            return carry

        lax.fori_loop(2, X + 2, second, 0, unroll=2)
        if not final_round:
            put_lines()
            start(range(4, 8), 1 - par, 0)
            put_planes(2, range(T))
            start(range(2), 1 - par, 0)
            put_rows(2, range(T))
            start(range(2, 4), 1 - par, 0)
        if r == 0:
            load_in.wait()
            load_out.wait()
            forward(0)
            m.nsend[1] = count_finish(0)
            count_start(1)
        if r == 1:
            swap(m.inputs, 0).wait()
            forward(1)
            m.nsend[2] = count_finish(1)
            count_start(2)
        if r == 2:
            m.total[...] = count_finish(2)

    turn(out_ref)
    lax.fori_loop(0, slots, pick_targets, 0, unroll=8)
    m.targets[0:slots] = in_order(picked_values(), m.order[...], 2)
    swap(m.targets, 1).start()
    backward(0, m.nrecv[0, gx][0:1, 0:1])
    swap(m.targets, 1).wait()
    backward(1, m.nrecv[0, high * 2 + 1 - core][0:1, 0:1])
    half = 512
    places = ((gz, lambda v: device(x=v)), (y, lambda v: device(y=v)))

    def ring(along, piece, relay, fin, send, sems):
        me, to = places[along]
        plus, minus, opposed = [lax.rem(me + d, 4) for d in (1, 3, 2)]
        begin, end = pl.ds(0, 2), pl.ds(2, 2)

        def copy(src, dst, number, peer):
            return remote(src, dst, sems.at[0, number], sems.at[1, number], to(peer))

        copies = [
            copy(piece(begin, opposed), relay.at[0], 0, plus),
            copy(piece(end, opposed), relay.at[1], 1, minus),
            copy(piece(end, plus), fin.at[0, end], 2, plus),
            copy(piece(begin, minus), fin.at[1, begin], 3, minus),
            copy(send.at[0], fin.at[0, begin], 4, plus),
            copy(send.at[1], fin.at[1, end], 5, minus),
        ]

        def open_ring():
            for one in copies[:4]:
                one.start()

        def pass_on():
            copies[0].wait_recv()
            send[0] = relay[0] + piece(begin, plus)[...]
            copies[4].start()
            copies[1].wait_recv()
            send[1] = relay[1] + piece(end, minus)[...]
            copies[5].start()

        def close_ring():
            for one in copies[2:]:
                one.wait_recv()
            total = piece(pl.ds(0, 4), me)[...] + fin[0] + fin[1]
            for one in copies:
                one.wait_send()
            return total

        return open_ring, pass_on, close_ring

    def piece1(batch, colour):
        def piece(part, owner):
            rows = pl.ds(pl.multiple_of(batch * 64 + owner * 16, 8), 16)
            return m.sums.at[part, rows, pl.ds(colour * half, half)]

        return piece

    def piece2(number):
        def piece(part, owner):
            lanes = pl.ds(pl.multiple_of(owner * LANES, LANES), LANES)
            return m.held1.at[number, part, :, lanes]

        return piece

    def rings_of(batch):
        one, two = [], []
        for colour in range(2):
            q = batch * 2 + colour
            one.append(
                ring(
                    colour,
                    piece1(batch, colour),
                    m.relay1.at[q],
                    m.fin1.at[q],
                    m.send1.at[q],
                    m.sems1.at[q],
                )
            )
            two.append(
                ring(
                    1 - colour,
                    piece2(q),
                    m.relay2.at[q],
                    m.fin2.at[q],
                    m.send2.at[q],
                    m.sems2.at[q],
                )
            )
        return one, two

    batches = [rings_of(batch) for batch in range(2)]

    def run(batch, stage, what, held=None):
        for colour, one in enumerate(batches[batch][stage]):
            value = one[what]()
            if held is not None:
                held[batch * 2 + colour] = value

    z_me = high * 2 + low

    def z_piece(batch, h, l):
        rows = pl.ds(pl.multiple_of(l * 8, 8), 8)
        return m.held2.at[pl.ds(batch * 2, 2), h, rows, :]

    z_peers = []
    for h, l in z_steps:
        ph, pw = lax.rem(high + h, 4), lax.rem(low + l, 2)
        z_peers.append((ph, pw, ph * 2 + pw, device(high=ph, low=pw)))

    def z_copy_out(batch, number):
        ph, pw, slot, peer = z_peers[number]
        return remote(
            z_piece(batch, ph, pw),
            m.zgot.at[z_me, batch],
            m.zp_send.at[batch, number],
            m.zp_recv.at[batch, z_me],
            peer,
        )

    def z_start(batch):
        for number in range(7):
            z_copy_out(batch, number).start()
        m.zgot[z_me, batch] = z_piece(batch, high, low)[...]

    def z_finish(batch):
        for number in range(7):
            ph, pw, slot, peer = z_peers[number]
            remote(
                z_piece(batch, high, low),
                m.zgot.at[slot, batch],
                m.zp_send.at[batch, number],
                m.zp_recv.at[batch, slot],
                peer,
            ).wait_recv()

    grad_in = matmul(m.normed[...], m.dpre[...], ((0,), (0,)))
    for h in range(4):
        m.sums[h, 0:64] = grad_in[h * 64 : (h + 1) * 64]
    run(0, 0, 0)
    dout = m.dout[...]
    for h in range(4):
        block = pl.multiple_of((h * 2 + core) * LANES, LANES)
        grad_out = matmul(m.act[:, pl.ds(block, LANES)], dout, ((0,), (0,)))
        m.sums[h, 64:128, 0:512] = grad_out[0:64]
        m.sums[h, 64:128, 512:1024] = grad_out[64:128]
    run(1, 0, 0)
    run(0, 0, 1)
    run(1, 0, 1)
    run(0, 0, 2, m.held1)
    run(0, 1, 0)
    run(1, 0, 2, m.held1)
    run(1, 1, 0)
    run(0, 1, 1)
    run(1, 1, 1)
    run(0, 1, 2, m.held2)
    z_start(0)
    run(1, 1, 2, m.held2)
    z_start(1)
    z_finish(0)
    z_finish(1)
    total = m.zgot[0]
    for slot in range(1, 8):
        total = total + m.zgot[slot]
    g_me = (gz * 4 + y) * 2 + low
    m.gathered[g_me] = total
    g_copies = []
    for number, (i, j, l) in enumerate(g_steps):
        px, py, pw = lax.rem(gz + i, 4), lax.rem(y + j, 4), lax.rem(low + l, 2)
        peer = device(x=px, y=py, low=pw)
        one = remote(
            m.gathered.at[g_me],
            m.gathered.at[g_me],
            m.g_send.at[number],
            m.g_recv.at[g_me],
            peer,
        )
        one.start()
        g_copies.append((one, (px * 4 + py) * 2 + pw, peer))
    for batch in range(2):
        for number in range(7):
            z_copy_out(batch, number).wait_send()
    for one, slot, peer in g_copies:
        remote(
            m.gathered.at[slot],
            m.gathered.at[slot],
            m.g_send.at[0],
            m.g_recv.at[slot],
            peer,
        ).wait_recv()
    sum_ref[...] = m.gathered[...]
    for one, slot, peer in g_copies:
        one.wait_send()


def step(prev, now, material, table, used, anchors, w_in, w_out, sizes):
    X, Y, Z = now.shape
    W = Z + LANES
    T = W // LANES
    slots = anchors.shape[0]
    wide, hidden = w_in.shape
    vmem = pl.BlockSpec(memory_space=pltpu.VMEM)
    smem = pl.BlockSpec(memory_space=pltpu.SMEM)
    hbm = pl.BlockSpec(memory_space=pltpu.HBM)
    dma = pltpu.SemaphoreType.DMA
    most = max(sizes)

    def f32(*shape):
        return pltpu.VMEM(shape, F32)

    def b16(*shape):
        return pltpu.VMEM(shape, BF16)

    scratch = dict(
        A=f32(2 * PAD + (X + 4) * T * R, LANES),
        B=f32(2 * PAD + (X + 4) * T * R, LANES),
        C=f32((X + 2) * T * Y, LANES),
        D=f32((X + 2) * T * Y, LANES),
        now=f32(X, Y, Z),
        prev=f32(X, Y, Z),
        xsend=f32(2, 4, T, Y, LANES),
        xrecv=f32(2, 2, 4, T, Y, LANES),
        ysend=f32(2, 4, T, X, LANES),
        yrecv=f32(2, 2, 4, T, X, LANES),
        yold=f32(2, T, X, LANES),
        ycoef=f32(2, T, X, LANES),
        csend=f32(4, 1, W),
        crecv=f32(2, 4, 1, W),
        zsend=f32(2, 3, Y, LANES),
        zrecv=f32(2, 3, Y, LANES),
        nsend=f32(3, 8, LANES),
        nrecv=f32(3, most, 8, LANES),
        total=f32(8, LANES),
        rows=f32(Z // LANES, X * Y, LANES),
        turned=f32(X * Y // LANES + 1, Z, LANES),
        picked=f32(8 * slots, LANES),
        mat=pltpu.VMEM((X, Y, Z), jnp.int32),
        where=pltpu.SMEM((3, slots), jnp.int32),
        order=b16(8 * LANES, wide),
        w_in=b16(wide, hidden),
        w_out=b16(hidden, wide),
        inputs=f32(2 * slots, wide),
        targets=f32(2 * slots, wide),
        base=f32(2 * slots, wide),
        normed=b16(2 * slots, wide // 2),
        act=b16(2 * slots, hidden),
        slope=f32(2 * slots, hidden),
        dout=b16(2 * slots, wide),
        dpre=b16(2 * slots, hidden),
        sums=f32(4, 128, 1024),
        relay1=f32(4, 2, 2, 16, 512),
        fin1=f32(4, 2, 4, 16, 512),
        send1=f32(4, 2, 2, 16, 512),
        held1=f32(4, 4, 16, 512),
        relay2=f32(4, 2, 2, 16, LANES),
        fin2=f32(4, 2, 4, 16, LANES),
        send2=f32(4, 2, 2, 16, LANES),
        held2=f32(4, 4, 16, LANES),
        zgot=f32(8, 2, 2, 8, LANES),
        gathered=f32(32, 2, 2, 8, LANES),
        load=dma((5,)),
        z_sem=dma((2, 2)),
        f_send=dma((12,)),
        f_recv=dma((2, 12)),
        n_send=dma((3, most)),
        n_recv=dma((3, most)),
        p_send=dma((2,)),
        p_recv=dma((2,)),
        sems1=dma((4, 2, 6)),
        sems2=dma((4, 2, 6)),
        zp_send=dma((2, 7)),
        zp_recv=dma((2, 8)),
        g_send=dma((31,)),
        g_recv=dma((32,)),
    )
    return pl.pallas_call(
        functools.partial(step_kernel, tuple(scratch), sizes),
        name="step",
        out_shape=(
            jax.ShapeDtypeStruct((X, Y, Z), F32),
            jax.ShapeDtypeStruct((32, 2, 2, 8, LANES), F32),
        ),
        in_specs=[hbm, hbm, hbm, smem, smem, smem, hbm, hbm],
        out_specs=(vmem, vmem),
        scratch_shapes=list(scratch.values()),
        compiler_params=pltpu.CompilerParams(
            collective_id=0,
            has_side_effects=True,
            vmem_limit_bytes=40 * 1024 * 1024,
        ),
    )(prev, now, material, table, used, anchors, w_in, w_out)


def place_kernel(final_ref, sum_ref, final_out, in_ref, out_ref):
    final_out[...] = final_ref[...]
    for slot in range(32):
        ix, iy, il = slot // 8, slot // 2 % 4, slot % 2
        for colour in range(2):
            one, two = (ix, iy) if colour == 0 else (iy, ix)
            top = one * 16 + il * 8
            at = two * LANES
            left = colour * 512 + at
            low = colour * 64 + top
            in_ref[top : top + 8, left : left + LANES] = sum_ref[slot, 0, colour]
            out_ref[low : low + 8, at : at + LANES] = sum_ref[slot, 1, colour]


def place(final, sums):
    vmem = pl.BlockSpec(memory_space=pltpu.VMEM)
    return pl.pallas_call(
        place_kernel,
        name="place",
        out_shape=(
            jax.ShapeDtypeStruct(final.shape, F32),
            jax.ShapeDtypeStruct((64, 1024), F32),
            jax.ShapeDtypeStruct((128, 512), F32),
        ),
        in_specs=[vmem, vmem],
        out_specs=(vmem, vmem, vmem),
        compiler_params=pltpu.CompilerParams(vmem_limit_bytes=8 * 1024 * 1024),
    )(final, sums)


def body(pressure_prev, pressure_now, material, speed_table, anchors, counts, w_in, w_out):
    sizes = tuple(lax.axis_size(axis) for axis in AXES)
    pressure_prev, pressure_now, material, speed_table, anchors, w_in, w_out = [
        pltpu.with_memory_space_constraint(v, pltpu.HBM)
        for v in (
            pressure_prev,
            pressure_now,
            material,
            speed_table,
            anchors.reshape(-1),
            w_in,
            w_out,
        )
    ]
    final, sums = step(
        pressure_prev,
        pressure_now,
        material,
        speed_table,
        counts.reshape(-1),
        anchors,
        w_in,
        w_out,
        sizes,
    )
    return place(final, sums)


def solution(mesh):
    return jax.shard_map(
        body,
        mesh=mesh,
        in_specs=(
            P("gx", "gy", "gz"),
            P("gx", "gy", "gz"),
            P("gx", "gy", "gz"),
            P(),
            P("gx", "gy", "gz"),
            P("gx", "gy", "gz"),
            P(),
            P(),
        ),
        out_specs=(P("gx", "gy", "gz"), P("gx", None), P("gx", None)),
        check_vma=False,
    )
```

```python
import functools
import types

import jax
import jax.numpy as jnp
from jax import lax
from jax.experimental import pallas as pl
from jax.experimental.pallas import tpu as pltpu
from jax.sharding import PartitionSpec as P

STEPS = 8
PATCH = 8
LANES = 128
R = 32
PAD = 8
AXES = ("gx", "gy", "gz")
F32 = jnp.float32
BF16 = jnp.bfloat16


def remote(src, dst, send_sem, recv_sem, device):
    return pltpu.make_async_remote_copy(
        src_ref=src,
        dst_ref=dst,
        send_sem=send_sem,
        recv_sem=recv_sem,
        device_id=device,
        device_id_type=pl.DeviceIdType.MESH,
    )


def signal(sem, device):
    pl.semaphore_signal(
        sem, inc=1, device_id=device, device_id_type=pl.DeviceIdType.MESH
    )


def matmul(a, b, dims):
    return lax.dot_general(a, b, (dims, ((), ())), preferred_element_type=F32)


def in_order(values, order, parts):
    total = None
    rest = values
    for part in range(parts):
        piece = rest.astype(BF16)
        if part < parts - 1:
            rest = rest - piece.astype(F32)
        term = matmul(piece, order, ((1,), (0,)))
        total = term if total is None else total + term
    return total


def step_kernel(
    names,
    sizes,
    prev_hbm,
    now_hbm,
    mat_hbm,
    tab_ref,
    cnt_ref,
    anchor_ref,
    win_hbm,
    wout_hbm,
    out_ref,
    sum_ref,
    *scratch,
):
    m = types.SimpleNamespace(**dict(zip(names, scratch)))
    nx, ny, nz = sizes
    gx, gy, gz = [lax.axis_index(axis) for axis in AXES]
    here = (gx, gy, gz)
    core, high = lax.rem(gx, 2), gx // 2
    low, y = lax.rem(gy, 2), gy // 2
    X, Y, Z = now_hbm.shape
    W = Z + LANES
    T = W // LANES
    slots = anchor_ref.shape[0]
    wide, hidden = win_hbm.shape
    A, B, C, D = m.A, m.B, m.C, m.D

    def rows_of(p, t, shift=0, count=Y):
        start = p * (T * R) + (PAD + t * R)
        if not isinstance(p, int):
            start = pl.multiple_of(start, 8)
        return pl.ds(start + shift, count)

    def rows_over(t, shift):
        return pl.ds(2 * T * R + PAD + t * R + shift, X, stride=T * R)

    def coef_of(p, t):
        start = p * (T * Y) + t * Y
        if not isinstance(p, int):
            start = pl.multiple_of(start, 8)
        return pl.ds(start, Y)

    def coef_over(t, shift):
        return pl.ds(T * Y + t * Y + shift, X, stride=T * Y)

    def tile_of(t):
        return slice(t * LANES, (t + 1) * LANES)


    def device(core=core, high=high, low=low, y=y, x=gz):
        return (high * 2 + core, y * 2 + low, x)

    def line_peer(axis, step):
        place = list(here)
        place[axis] = lax.rem(here[axis] + step, sizes[axis])
        return tuple(place)

    partner = device(core=1 - core)

    barrier = pltpu.get_barrier_semaphore()
    z_steps = [(h, l) for h in range(4) for l in range(2) if h or l]
    g_steps = [
        (i, j, l) for i in range(4) for j in range(4) for l in range(2) if i or j or l
    ]
    reached = []
    for axis in range(3):
        for step in range(1, sizes[axis]):
            reached.append(line_peer(axis, step))
    for dx in (nx - 1, 1):
        for dy in (ny - 1, 1):
            reached.append((lax.rem(gx + dx, nx), lax.rem(gy + dy, ny), gz))
    for h, l in z_steps:
        if h and l:
            reached.append(
                device(high=lax.rem(high + h, 4), low=lax.rem(low + l, 2))
            )
    for i, j, l in g_steps:
        if i and (j or l):
            reached.append(
                device(
                    x=lax.rem(gz + i, 4), y=lax.rem(y + j, 4), low=lax.rem(low + l, 2)
                )
            )

    loads = [
        pltpu.make_async_copy(mat_hbm, m.mat, m.load.at[2]),
        pltpu.make_async_copy(now_hbm, m.now, m.load.at[3]),
        pltpu.make_async_copy(prev_hbm, m.prev, m.load.at[4]),
    ]
    for one in loads:
        one.start()
    load_in = pltpu.make_async_copy(win_hbm, m.w_in, m.load.at[0])
    load_out = pltpu.make_async_copy(wout_hbm, m.w_out, m.load.at[1])
    load_in.start()
    load_out.start()

    def clear(missing, ref, *index):
        @pl.when(missing)
        def _():
            for par in range(2):
                ref[(par, *index)] = jnp.zeros(ref.shape[1 + len(index) :], F32)

    ends = ((gx == 0, gx == nx - 1), (gy == 0, gy == ny - 1))
    for side in range(2):
        clear(ends[0][side], m.xrecv, side)
        clear(ends[1][side], m.yrecv, side)
        for other in range(2):
            clear(
                jnp.logical_or(ends[0][side], ends[1][other]),
                m.crecv,
                side * 2 + other,
            )

    @pl.when(gz == 0)
    def _():
        m.zrecv[0] = jnp.zeros(m.zrecv.shape[1:], F32)

    @pl.when(gz == nz - 1)
    def _():
        m.zrecv[1] = jnp.zeros(m.zrecv.shape[1:], F32)

    for place in reached:
        signal(barrier, place)

    lane = lax.broadcasted_iota(jnp.int32, (Y, LANES), 1)
    def pack_edge(values):
        at = lax.broadcasted_iota(jnp.int32, values[0].shape, 1)
        group = lax.shift_right_logical(jnp.bitwise_and(at + 8, LANES - 1), 4)
        packed = values[0]
        for e, value in enumerate(values[1:], 1):
            packed = jnp.where(group == e, pltpu.roll(value, 16 * e, 1), packed)
        return packed

    def open_edge(packed, e, masked=False):
        value = pltpu.roll(packed, LANES - 16 * e, 1) if e else packed
        if masked:
            at = lax.broadcasted_iota(jnp.int32, value.shape, 1)
            value = jnp.where((at < 8) | (at >= LANES - 8), value, 0.0)
        return value

    def face_tiles(ref, index, e, masked=False):
        tiles = [ref[(*index, 1 + 2 * e + t)] for t in range(2)]
        return tiles + [open_edge(ref[(*index, 0)], e, masked)]

    def put_face(ref, side, sources, main, edge):
        if main:
            for e, source in enumerate(sources):
                for t in range(2):
                    ref[side, 1 + 2 * e + t] = source(t)
        if edge:
            ref[side, 0] = pack_edge([source(2) for source in sources])

    def put_rows(entries, main, edge):
        for side, at, second in ((0, 0, 1), (1, Y - 1, Y - 2)):
            sources = [
                lambda t, at=at: A[rows_over(t, at), :],
                lambda t, second=second: A[rows_over(t, second), :],
                lambda t, at=at: B[rows_over(t, at), :],
                lambda t, at=at: C[coef_over(t, at), :],
            ][:entries]
            put_face(m.ysend, side, sources, main, edge)

    def put_planes(entries, main, edge):
        for side, planes in enumerate(((2, 3, 2, 1), (X, X + 1, X + 1, X))):
            sources = [
                lambda t, p=planes[0]: A[rows_of(p, t), :],
                lambda t, p=planes[1]: A[rows_of(p, t), :],
                lambda t, p=planes[2]: B[rows_of(p, t), :],
                lambda t, p=planes[3]: C[coef_of(p, t), :],
            ][:entries]
            put_face(m.xsend, side, sources, main, edge)

    inner_tiles = range(Z // LANES)

    for one in loads:
        one.wait()

    def pack(x, carry):
        material = m.mat[x]
        c = jnp.zeros((Y, Z), F32)
        for number in range(tab_ref.shape[0]):
            c = jnp.where(material == number, tab_ref[number], c)
        n, p = m.now[x], m.prev[x]
        for t in inner_tiles:
            A[rows_of(x + 2, t), :] = n[:, tile_of(t)]
            B[rows_of(x + 2, t), :] = p[:, tile_of(t)]
            C[coef_of(x + 1, t), :] = c[:, tile_of(t)]
            D[coef_of(x + 1, t), :] = 2.0 - 6.0 * c[:, tile_of(t)]
        mine = lax.shift_right_logical(lane, 3) == x
        up, down = [], []
        for field, held_up, held_down in zip((n, p, c), carry[0], carry[1]):
            last = pltpu.roll(field[:, Z - LANES :], lax.rem(x * 8 + 8, LANES), 1)
            first = pltpu.roll(field[:, :LANES], x * 8, 1)
            up.append(jnp.where(mine, last, held_up))
            down.append(jnp.where(mine, first, held_down))
        return tuple(up), tuple(down)

    empty = tuple(jnp.zeros((Y, LANES), F32) for _ in range(3))
    ups, downs = lax.fori_loop(0, X, pack, (empty, empty))
    for i in range(3):
        m.zsend[0, i] = ups[i]
        m.zsend[1, i] = downs[i]

    put_planes(4, True, False)
    put_rows(4, True, False)
    m.nsend[0] = jnp.full((8, LANES), cnt_ref[0].astype(F32))

    pl.semaphore_wait(barrier, len(reached))

    def z_copy(side):
        step = 1 if side == 0 else nz - 1
        return remote(
            m.zsend.at[side],
            m.zrecv.at[side],
            m.z_sem.at[0, side],
            m.z_sem.at[1, side],
            (gx, gy, lax.rem(gz + step, nz)),
        )

    @pl.when(gz < nz - 1)
    def _():
        z_copy(0).start()

    @pl.when(gz > 0)
    def _():
        z_copy(1).start()

    left, right = lax.rem(gx + nx - 1, nx), lax.rem(gx + 1, nx)
    below, above = lax.rem(gy + ny - 1, ny), lax.rem(gy + 1, ny)
    targets_of = (
        (left, gy, gz),
        (right, gy, gz),
        (gx, below, gz),
        (gx, above, gz),
        (left, below, gz),
        (left, above, gz),
        (right, below, gz),
        (right, above, gz),
    )
    sides = (gx > 0, gx < nx - 1, gy > 0, gy < ny - 1)
    has = sides + tuple(
        jnp.logical_and(sides[i], sides[j]) for i in (0, 1) for j in (2, 3)
    )
    opposite = (1, 0, 3, 2, 7, 6, 5, 4)

    def face(d, par, form):
        if d < 4:
            side = d % 2
            send, got = (m.xsend, m.xrecv) if d < 2 else (m.ysend, m.yrecv)
            tiles = (pl.ds(0, 5), pl.ds(1, 8), pl.ds(0, 1))[form]
            src = send.at[side, tiles]
            dst = got.at[par, 1 - side, tiles]
        else:
            src = m.csend.at[d - 4]
            dst = m.crecv.at[par, 7 - d]
        number = d + 8 if form == 2 else d
        arrives = opposite[d] + 8 if form == 2 else opposite[d]
        return remote(
            src, dst, m.f_send.at[number], m.f_recv.at[par, arrives], targets_of[d]
        )

    def each(ds, action):
        for d in ds:

            @pl.when(has[d])
            def _():
                action(d)

    def start(ds, par, form):
        each(ds, lambda d: face(d, par, form).start())

    def sent(ds, par, form):
        each(ds, lambda d: face(d, par, form).wait_send())

    def came(ds, par, form):
        each(ds, lambda d: face(opposite[d], par, form).wait_recv())

    start(range(4), 0, 1)

    def count_copy(axis, step):
        return remote(
            m.nsend.at[axis],
            m.nrecv.at[axis, here[axis]],
            m.n_send.at[axis, step],
            m.n_recv.at[axis, here[axis]],
            line_peer(axis, step),
        )

    def count_start(axis):
        for step in range(1, sizes[axis]):
            count_copy(axis, step).start()
        m.nrecv[axis, here[axis]] = m.nsend[axis]

    def count_finish(axis):
        size = sizes[axis]
        for step in range(1, size):
            count_copy(axis, step).wait_send()
            source = lax.rem(here[axis] + step, size)
            remote(
                m.nsend.at[axis],
                m.nrecv.at[axis, source],
                m.n_send.at[axis, step],
                m.n_recv.at[axis, source],
                line_peer(axis, step),
            ).wait_recv()
        total = m.nrecv[axis, 0]
        for i in range(1, size):
            total = total + m.nrecv[axis, i]
        return total

    count_start(0)

    tiles = X * Y // LANES
    narrow = lax.broadcasted_iota(jnp.int32, (8, LANES), 1)

    def turn(field):
        for x in range(X):
            for half in range(Z // LANES):
                m.rows[half, pl.ds(x, Y, stride=X), :] = field[
                    x, :, half * LANES : (half + 1) * LANES
                ]
        for half in range(Z // LANES):
            for tile in range(tiles):
                at = tile * Z + half * LANES
                m.turned[at : at + LANES, :] = m.rows[
                    half, tile * LANES : (tile + 1) * LANES, :
                ].T

    def pick_one(s, first_row, keep):
        first = m.turned[pl.ds(first_row, 8), :]
        second = m.turned[pl.ds(first_row + Z, 8), :]
        back = jnp.bitwise_and(keep, LANES - 1)
        m.picked[pl.ds(pl.multiple_of(s * 8, 8), 8), :] = jnp.where(
            narrow < keep, pltpu.roll(first, back, 1), pltpu.roll(second, back, 1)
        )

    def pick_inputs(s, carry):
        anchor = anchor_ref[s]
        i = anchor // (Y * Z)
        rest = anchor - i * (Y * Z)
        j = rest // Z
        shift = j * X + i
        first_row = (shift // LANES) * Z + (rest - j * Z)
        keep = LANES - jnp.bitwise_and(shift, LANES - 1)
        m.where[0, s] = first_row
        m.where[1, s] = keep
        pick_one(s, first_row, keep)
        return carry

    def pick_targets(s, carry):
        pick_one(s, m.where[0, s], m.where[1, s])
        return carry

    def picked_values():
        return jnp.concatenate(
            [m.picked[pl.ds(c, slots, stride=8), :] for c in range(8)], axis=1
        )

    def swap(ref, number):
        return remote(
            ref.at[0:slots],
            ref.at[slots : 2 * slots],
            m.p_send.at[number],
            m.p_recv.at[number],
            partner,
        )

    m.turned[tiles * Z : (tiles + 1) * Z, :] = jnp.zeros((Z, LANES), F32)
    turn(m.now)

    @pl.when(gz < nz - 1)
    def _():
        z_copy(0).wait_send()
        z_copy(1).wait_recv()

    @pl.when(gz > 0)
    def _():
        z_copy(1).wait_send()
        z_copy(0).wait_recv()

    def unpack(x, carry):
        values = []
        for i in range(3):
            before = pltpu.roll(m.zrecv[0, i], lax.rem(120 + LANES - x * 8, LANES), 1)
            after = pltpu.roll(m.zrecv[1, i], lax.rem(LANES - x * 8, LANES), 1)
            values.append(
                jnp.where(lane < 8, after, jnp.where(lane >= 120, before, 0.0))
            )
        A[rows_of(x + 2, T - 1), :] = values[0]
        B[rows_of(x + 2, T - 1), :] = values[1]
        C[coef_of(x + 1, T - 1), :] = values[2]
        D[coef_of(x + 1, T - 1), :] = 2.0 - 6.0 * values[2]
        return carry

    lax.fori_loop(0, X, unpack, 0, unroll=2)

    def put_lines():
        for i in range(4):
            plane = 2 if i < 2 else X + 1
            at = 0 if i % 2 == 0 else Y - 1
            for t in range(T):
                m.csend[i, :, tile_of(t)] = A[rows_of(plane, t, at, 1), :]

    put_planes(4, False, True)
    put_rows(4, False, True)
    put_lines()
    start(range(4, 8), 0, 0)
    start(range(4), 0, 2)

    lax.fori_loop(0, slots, pick_inputs, 0, unroll=8)
    at = lax.broadcasted_iota(jnp.int32, (8 * LANES, wide), 0)
    feature = lax.broadcasted_iota(jnp.int32, (8 * LANES, wide), 1)
    pa = jnp.bitwise_and(at, X - 1)
    pb = jnp.bitwise_and(lax.shift_right_logical(at, 4), 7)
    pc = lax.shift_right_logical(at, 7)
    m.order[...] = jnp.where(
        (pa < PATCH) & (feature == pa * 64 + pb * 8 + pc), 1.0, 0.0
    ).astype(BF16)
    m.inputs[0:slots] = in_order(picked_values(), m.order[...], 3)
    swap(m.inputs, 0).start()

    root = 0.7978845608028654

    def forward(part):
        rows = slice(part * slots, (part + 1) * slots)
        inputs = m.inputs[rows]
        mean = jnp.mean(inputs * inputs, axis=1, keepdims=True)
        normed = (inputs * lax.rsqrt(mean + 1e-06)).astype(BF16)
        pre = matmul(normed, m.w_in[...], ((1,), (0,)))
        tanh = jnp.tanh(root * (pre + 0.044715 * (pre * pre * pre)))
        cdf = 0.5 * (1.0 + tanh)
        act = (pre * cdf).astype(BF16)
        m.act[rows] = act
        m.slope[rows] = cdf + 0.5 * pre * (1.0 - tanh * tanh) * (
            root * (1.0 + (3.0 * 0.044715) * (pre * pre))
        )
        m.base[rows] = inputs + matmul(act, m.w_out[...], ((1,), (0,)))
        source = lax.broadcasted_iota(jnp.int32, (wide, wide // 2), 0)
        column = lax.broadcasted_iota(jnp.int32, (wide, wide // 2), 1)
        block = lax.shift_right_logical(column, 6) * 2 + core
        chosen = jnp.where(
            source == block * 64 + jnp.bitwise_and(column, 63), 1.0, 0.0
        ).astype(BF16)
        m.normed[rows] = matmul(normed, chosen, ((1,), (0,))).astype(BF16)

    def backward(part, count):
        rows = slice(part * slots, (part + 1) * slots)
        err = m.base[rows] - m.targets[rows]
        slot = lax.broadcasted_iota(jnp.int32, (slots, 1), 0).astype(F32)
        valid = (slot < count).astype(F32)
        dout = (2.0 * err * valid / m.total[0:1, 0:1]).astype(BF16)
        m.dout[rows] = dout
        dact = matmul(dout, m.w_out[...], ((1,), (1,)))
        m.dpre[rows] = (dact * m.slope[rows]).astype(BF16)

    for r in range(STEPS // 2):
        par = r % 2
        if r == 0:
            came(range(4), 0, 1)
            came(range(4), 0, 2)
        else:
            came(range(4), par, 0)
        came(range(4, 8), par, 0)
        for side in range(2):
            for e in range(2):
                plane = e + side * (X + 2)
                for t, value in enumerate(face_tiles(m.xrecv, (par, side), e)):
                    A[rows_of(plane, t), :] = value
            for t, value in enumerate(face_tiles(m.yrecv, (par, side), 0)):
                A[rows_over(t, -1 if side == 0 else Y), :] = value
        for t in range(T):
            for i in range(4):
                plane = 1 if i < 2 else X + 2
                at = -1 if i % 2 == 0 else Y
                A[rows_of(plane, t, at, 1), :] = m.crecv[par, i, :, tile_of(t)]
        if r == 0:
            for side, plane, ring_coef in ((0, 1, 0), (1, X + 2, X + 1)):
                olds = face_tiles(m.xrecv, (0, side), 2)
                coefs = face_tiles(m.xrecv, (0, side), 3, True)
                side_olds = face_tiles(m.yrecv, (0, side), 2)
                side_coefs = face_tiles(m.yrecv, (0, side), 3, True)
                for t in range(T):
                    B[rows_of(plane, t), :] = olds[t]
                    C[coef_of(ring_coef, t), :] = coefs[t]
                    D[coef_of(ring_coef, t), :] = 2.0 - 6.0 * coefs[t]
                    m.yold[side, t] = side_olds[t]
                    m.ycoef[side, t] = side_coefs[t]

        def whole(parts):
            return jnp.concatenate(parts, axis=1)

        def beside_of(field, p):
            def at(plane, shift):
                return whole([field[rows_of(plane, t, shift), :] for t in range(T)])

            n = at(p, 0)
            beside = at(p + 1, 0) + at(p - 1, 0)
            beside = beside + at(p, 1) + at(p, -1)
            return n, beside + pltpu.roll(n, W - 1, 1) + pltpu.roll(n, 1, 1)

        def update(field, other, p):
            n, beside = beside_of(field, p)
            old = whole([other[rows_of(p, t), :] for t in range(T)])
            c = whole([C[coef_of(p - 1, t), :] for t in range(T)])
            d = whole([D[coef_of(p - 1, t), :] for t in range(T)])
            return d * n - old + c * beside

        def first(p, carry):
            after = update(A, B, p)
            for t in range(T):
                B[rows_of(p, t), :] = after[:, tile_of(t)]
            return carry

        lax.fori_loop(1, X + 3, first, 0, unroll=2)
        across = lax.broadcasted_iota(jnp.int32, (X, W), 0)
        for side in range(2):

            def plane_of(ref, *index):
                return whole([ref[(*index, tile)] for tile in range(T)])

            n = whole(face_tiles(m.yrecv, (par, side), 0))
            outer = whole(face_tiles(m.yrecv, (par, side), 1))
            inner = whole([A[rows_over(t, side * (Y - 1)), :] for t in range(T)])
            plus, minus = (inner, outer) if side == 0 else (outer, inner)
            beside = jnp.where(
                across == X - 1, m.crecv[par, 2 + side], pltpu.roll(n, X - 1, 0)
            )
            beside = beside + jnp.where(
                across == 0, m.crecv[par, side], pltpu.roll(n, 1, 0)
            )
            beside = beside + plus + minus
            beside = beside + pltpu.roll(n, W - 1, 1) + pltpu.roll(n, 1, 1)
            value = (
                2.0 * n
                - plane_of(m.yold, side)
                + plane_of(m.ycoef, side) * (beside - 6.0 * n)
            )
            for t in range(T):
                m.yold[side, t] = value[:, tile_of(t)]
                B[rows_over(t, -1 if side == 0 else Y), :] = value[:, tile_of(t)]
        if r == 0:
            sent(range(4), 0, 1)
            sent(range(4), 0, 2)
        else:
            sent(range(4), par, 0)
        sent(range(4, 8), par, 0)
        final_round = r == STEPS // 2 - 1

        def second(p, carry):
            after = update(B, A, p)
            if final_round:
                out_ref[p - 2] = after[:, 0:Z]
            else:
                for t in range(T):
                    A[rows_of(p, t), :] = after[:, tile_of(t)]
            return carry

        lax.fori_loop(2, X + 2, second, 0, unroll=2)
        if not final_round:
            put_lines()
            start(range(4, 8), 1 - par, 0)
            put_planes(2, True, True)
            start(range(2), 1 - par, 0)
            put_rows(2, True, True)
            start(range(2, 4), 1 - par, 0)
        if r == 0:
            load_in.wait()
            load_out.wait()
            forward(0)
            m.nsend[1] = count_finish(0)
            count_start(1)
        if r == 1:
            swap(m.inputs, 0).wait()
            forward(1)
            m.nsend[2] = count_finish(1)
            count_start(2)
        if r == 2:
            m.total[...] = count_finish(2)

    turn(out_ref)
    lax.fori_loop(0, slots, pick_targets, 0, unroll=16)
    m.targets[0:slots] = in_order(picked_values(), m.order[...], 2)
    swap(m.targets, 1).start()
    backward(0, m.nrecv[0, gx][0:1, 0:1])
    swap(m.targets, 1).wait()
    backward(1, m.nrecv[0, high * 2 + 1 - core][0:1, 0:1])
    half = 512
    places = ((gz, lambda v: device(x=v)), (y, lambda v: device(y=v)))

    def ring(along, piece, relay, fin, send, sems):
        me, to = places[along]
        plus, minus, opposed = [lax.rem(me + d, 4) for d in (1, 3, 2)]
        begin, end = pl.ds(0, 2), pl.ds(2, 2)

        def copy(src, dst, number, peer):
            return remote(src, dst, sems.at[0, number], sems.at[1, number], to(peer))

        copies = [
            copy(piece(begin, opposed), relay.at[0], 0, plus),
            copy(piece(end, opposed), relay.at[1], 1, minus),
            copy(piece(end, plus), fin.at[0, end], 2, plus),
            copy(piece(begin, minus), fin.at[1, begin], 3, minus),
            copy(send.at[0], fin.at[0, begin], 4, plus),
            copy(send.at[1], fin.at[1, end], 5, minus),
        ]

        def open_ring():
            for one in copies[:4]:
                one.start()

        def pass_on():
            copies[0].wait_recv()
            send[0] = relay[0] + piece(begin, plus)[...]
            copies[4].start()
            copies[1].wait_recv()
            send[1] = relay[1] + piece(end, minus)[...]
            copies[5].start()

        def close_ring():
            for one in copies[2:]:
                one.wait_recv()
            total = piece(pl.ds(0, 4), me)[...] + fin[0] + fin[1]
            for one in copies:
                one.wait_send()
            return total

        return open_ring, pass_on, close_ring

    def piece1(batch, colour):
        def piece(part, owner):
            rows = pl.ds(pl.multiple_of(batch * 64 + owner * 16, 8), 16)
            return m.sums.at[part, rows, pl.ds(colour * half, half)]

        return piece

    def piece2(number):
        def piece(part, owner):
            lanes = pl.ds(pl.multiple_of(owner * LANES, LANES), LANES)
            return m.held1.at[number, part, :, lanes]

        return piece

    def rings_of(batch):
        one, two = [], []
        for colour in range(2):
            q = batch * 2 + colour
            one.append(
                ring(
                    colour,
                    piece1(batch, colour),
                    m.relay1.at[q],
                    m.fin1.at[q],
                    m.send1.at[q],
                    m.sems1.at[q],
                )
            )
            two.append(
                ring(
                    1 - colour,
                    piece2(q),
                    m.relay2.at[q],
                    m.fin2.at[q],
                    m.send2.at[q],
                    m.sems2.at[q],
                )
            )
        return one, two

    batches = [rings_of(batch) for batch in range(2)]

    def run(batch, stage, what, held=None):
        for colour, one in enumerate(batches[batch][stage]):
            value = one[what]()
            if held is not None:
                held[batch * 2 + colour] = value

    z_me = high * 2 + low

    def z_piece(batch, h, l):
        rows = pl.ds(pl.multiple_of(l * 8, 8), 8)
        return m.held2.at[pl.ds(batch * 2, 2), h, rows, :]

    z_peers = []
    for h, l in z_steps:
        ph, pw = lax.rem(high + h, 4), lax.rem(low + l, 2)
        z_peers.append((ph, pw, ph * 2 + pw, device(high=ph, low=pw)))

    def z_copy_out(batch, number):
        ph, pw, slot, peer = z_peers[number]
        return remote(
            z_piece(batch, ph, pw),
            m.zgot.at[z_me, batch],
            m.zp_send.at[batch, number],
            m.zp_recv.at[batch, z_me],
            peer,
        )

    def z_start(batch):
        for number in range(7):
            z_copy_out(batch, number).start()
        m.zgot[z_me, batch] = z_piece(batch, high, low)[...]

    def z_finish(batch):
        for number in range(7):
            ph, pw, slot, peer = z_peers[number]
            remote(
                z_piece(batch, high, low),
                m.zgot.at[slot, batch],
                m.zp_send.at[batch, number],
                m.zp_recv.at[batch, slot],
                peer,
            ).wait_recv()

    grad_in = matmul(m.normed[...], m.dpre[...], ((0,), (0,)))
    for h in range(4):
        m.sums[h, 0:64] = grad_in[h * 64 : (h + 1) * 64]
    run(0, 0, 0)
    dout = m.dout[...]
    for h in range(4):
        block = pl.multiple_of((h * 2 + core) * LANES, LANES)
        grad_out = matmul(m.act[:, pl.ds(block, LANES)], dout, ((0,), (0,)))
        m.sums[h, 64:128, 0:512] = grad_out[0:64]
        m.sums[h, 64:128, 512:1024] = grad_out[64:128]
    run(1, 0, 0)
    run(0, 0, 1)
    run(1, 0, 1)
    run(0, 0, 2, m.held1)
    run(0, 1, 0)
    run(1, 0, 2, m.held1)
    run(1, 1, 0)
    run(0, 1, 1)
    run(1, 1, 1)
    run(0, 1, 2, m.held2)
    z_start(0)
    run(1, 1, 2, m.held2)
    z_start(1)
    g_me = (gz * 4 + y) * 2 + low
    g_peers = []
    for i, j, l in g_steps:
        px, py, pw = lax.rem(gz + i, 4), lax.rem(y + j, 4), lax.rem(low + l, 2)
        g_peers.append(((px * 4 + py) * 2 + pw, device(x=px, y=py, low=pw)))

    def g_copy(batch, number, slot):
        return remote(
            m.gathered.at[slot, batch],
            m.gathered.at[slot, batch],
            m.g_send.at[batch, number],
            m.g_recv.at[batch, slot],
            g_peers[number][1],
        )

    for batch in range(2):
        z_finish(batch)
        total = m.zgot[0, batch]
        for slot in range(1, 8):
            total = total + m.zgot[slot, batch]
        m.gathered[g_me, batch] = total
        for number in range(31):
            g_copy(batch, number, g_me).start()
    for batch in range(2):
        for number in range(7):
            z_copy_out(batch, number).wait_send()
    for batch in range(2):
        for number in range(31):
            g_copy(batch, number, g_peers[number][0]).wait_recv()
    sum_ref[...] = m.gathered[...]
    for batch in range(2):
        for number in range(31):
            g_copy(batch, number, g_me).wait_send()


def step(prev, now, material, table, used, anchors, w_in, w_out, sizes):
    X, Y, Z = now.shape
    W = Z + LANES
    T = W // LANES
    slots = anchors.shape[0]
    wide, hidden = w_in.shape
    vmem = pl.BlockSpec(memory_space=pltpu.VMEM)
    smem = pl.BlockSpec(memory_space=pltpu.SMEM)
    hbm = pl.BlockSpec(memory_space=pltpu.HBM)
    dma = pltpu.SemaphoreType.DMA
    most = max(sizes)

    def f32(*shape):
        return pltpu.VMEM(shape, F32)

    def b16(*shape):
        return pltpu.VMEM(shape, BF16)

    scratch = dict(
        A=f32(2 * PAD + (X + 4) * T * R, LANES),
        B=f32(2 * PAD + (X + 4) * T * R, LANES),
        C=f32((X + 2) * T * Y, LANES),
        D=f32((X + 2) * T * Y, LANES),
        now=f32(X, Y, Z),
        prev=f32(X, Y, Z),
        xsend=f32(2, 9, Y, LANES),
        xrecv=f32(2, 2, 9, Y, LANES),
        ysend=f32(2, 9, X, LANES),
        yrecv=f32(2, 2, 9, X, LANES),
        yold=f32(2, T, X, LANES),
        ycoef=f32(2, T, X, LANES),
        csend=f32(4, 1, W),
        crecv=f32(2, 4, 1, W),
        zsend=f32(2, 3, Y, LANES),
        zrecv=f32(2, 3, Y, LANES),
        nsend=f32(3, 8, LANES),
        nrecv=f32(3, most, 8, LANES),
        total=f32(8, LANES),
        rows=f32(Z // LANES, X * Y, LANES),
        turned=f32((X * Y // LANES + 1) * Z, LANES),
        picked=f32(8 * slots, LANES),
        mat=pltpu.VMEM((X, Y, Z), jnp.int32),
        where=pltpu.SMEM((2, slots), jnp.int32),
        order=b16(8 * LANES, wide),
        w_in=b16(wide, hidden),
        w_out=b16(hidden, wide),
        inputs=f32(2 * slots, wide),
        targets=f32(2 * slots, wide),
        base=f32(2 * slots, wide),
        normed=b16(2 * slots, wide // 2),
        act=b16(2 * slots, hidden),
        slope=f32(2 * slots, hidden),
        dout=b16(2 * slots, wide),
        dpre=b16(2 * slots, hidden),
        sums=f32(4, 128, 1024),
        relay1=f32(4, 2, 2, 16, 512),
        fin1=f32(4, 2, 4, 16, 512),
        send1=f32(4, 2, 2, 16, 512),
        held1=f32(4, 4, 16, 512),
        relay2=f32(4, 2, 2, 16, LANES),
        fin2=f32(4, 2, 4, 16, LANES),
        send2=f32(4, 2, 2, 16, LANES),
        held2=f32(4, 4, 16, LANES),
        zgot=f32(8, 2, 2, 8, LANES),
        gathered=f32(32, 2, 2, 8, LANES),
        load=dma((5,)),
        z_sem=dma((2, 2)),
        f_send=dma((12,)),
        f_recv=dma((2, 12)),
        n_send=dma((3, most)),
        n_recv=dma((3, most)),
        p_send=dma((2,)),
        p_recv=dma((2,)),
        sems1=dma((4, 2, 6)),
        sems2=dma((4, 2, 6)),
        zp_send=dma((2, 7)),
        zp_recv=dma((2, 8)),
        g_send=dma((2, 31)),
        g_recv=dma((2, 32)),
    )
    return pl.pallas_call(
        functools.partial(step_kernel, tuple(scratch), sizes),
        name="step",
        out_shape=(
            jax.ShapeDtypeStruct((X, Y, Z), F32),
            jax.ShapeDtypeStruct((32, 2, 2, 8, LANES), F32),
        ),
        in_specs=[hbm, hbm, hbm, smem, smem, smem, hbm, hbm],
        out_specs=(vmem, vmem),
        scratch_shapes=list(scratch.values()),
        compiler_params=pltpu.CompilerParams(
            collective_id=0,
            has_side_effects=True,
            vmem_limit_bytes=40 * 1024 * 1024,
        ),
    )(prev, now, material, table, used, anchors, w_in, w_out)


def place_kernel(final_ref, sum_ref, final_out, in_ref, out_ref):
    final_out[...] = final_ref[...]
    for slot in range(32):
        ix, iy, il = slot // 8, slot // 2 % 4, slot % 2
        for colour in range(2):
            one, two = (ix, iy) if colour == 0 else (iy, ix)
            top = one * 16 + il * 8
            at = two * LANES
            left = colour * 512 + at
            low = colour * 64 + top
            in_ref[top : top + 8, left : left + LANES] = sum_ref[slot, 0, colour]
            out_ref[low : low + 8, at : at + LANES] = sum_ref[slot, 1, colour]


def place(final, sums):
    vmem = pl.BlockSpec(memory_space=pltpu.VMEM)
    return pl.pallas_call(
        place_kernel,
        name="place",
        out_shape=(
            jax.ShapeDtypeStruct(final.shape, F32),
            jax.ShapeDtypeStruct((64, 1024), F32),
            jax.ShapeDtypeStruct((128, 512), F32),
        ),
        in_specs=[vmem, vmem],
        out_specs=(vmem, vmem, vmem),
        compiler_params=pltpu.CompilerParams(vmem_limit_bytes=8 * 1024 * 1024),
    )(final, sums)


def body(pressure_prev, pressure_now, material, speed_table, anchors, counts, w_in, w_out):
    sizes = tuple(lax.axis_size(axis) for axis in AXES)
    pressure_prev, pressure_now, material, speed_table, anchors, w_in, w_out = [
        pltpu.with_memory_space_constraint(v, pltpu.HBM)
        for v in (
            pressure_prev,
            pressure_now,
            material,
            speed_table,
            anchors.reshape(-1),
            w_in,
            w_out,
        )
    ]
    final, sums = step(
        pressure_prev,
        pressure_now,
        material,
        speed_table,
        counts.reshape(-1),
        anchors,
        w_in,
        w_out,
        sizes,
    )
    return place(final, sums)


def solution(mesh):
    return jax.shard_map(
        body,
        mesh=mesh,
        in_specs=(
            P("gx", "gy", "gz"),
            P("gx", "gy", "gz"),
            P("gx", "gy", "gz"),
            P(),
            P("gx", "gy", "gz"),
            P("gx", "gy", "gz"),
            P(),
            P(),
        ),
        out_specs=(P("gx", "gy", "gz"), P("gx", None), P("gx", None)),
        check_vma=False,
    )
```

```python
import functools
import types

import jax
import jax.numpy as jnp
from jax import lax
from jax.experimental import pallas as pl
from jax.experimental.pallas import tpu as pltpu
from jax.sharding import PartitionSpec as P

STEPS = 8
PATCH = 8
LANES = 128
R = 32
PAD = 8
AXES = ("gx", "gy", "gz")
F32 = jnp.float32
BF16 = jnp.bfloat16


def remote(src, dst, send_sem, recv_sem, device):
    return pltpu.make_async_remote_copy(
        src_ref=src,
        dst_ref=dst,
        send_sem=send_sem,
        recv_sem=recv_sem,
        device_id=device,
        device_id_type=pl.DeviceIdType.MESH,
    )


def signal(sem, device):
    pl.semaphore_signal(
        sem, inc=1, device_id=device, device_id_type=pl.DeviceIdType.MESH
    )


def matmul(a, b, dims):
    return lax.dot_general(a, b, (dims, ((), ())), preferred_element_type=F32)


def in_order(values, order, parts):
    total = None
    rest = values
    for part in range(parts):
        piece = rest.astype(BF16)
        if part < parts - 1:
            rest = rest - piece.astype(F32)
        term = matmul(piece, order, ((1,), (0,)))
        total = term if total is None else total + term
    return total


def step_kernel(
    names,
    sizes,
    prev_hbm,
    now_hbm,
    mat_hbm,
    tab_ref,
    cnt_ref,
    anchor_ref,
    win_hbm,
    wout_hbm,
    out_ref,
    sum_ref,
    *scratch,
):
    m = types.SimpleNamespace(**dict(zip(names, scratch)))
    nx, ny, nz = sizes
    gx, gy, gz = [lax.axis_index(axis) for axis in AXES]
    here = (gx, gy, gz)
    core, high = lax.rem(gx, 2), gx // 2
    low, y = lax.rem(gy, 2), gy // 2
    X, Y, Z = now_hbm.shape
    W = Z + LANES
    T = W // LANES
    slots = anchor_ref.shape[0]
    wide, hidden = win_hbm.shape
    A, B, C, D = m.A, m.B, m.C, m.D

    def rows_of(p, t, shift=0, count=Y):
        start = p * (T * R) + (PAD + t * R)
        if not isinstance(p, int):
            start = pl.multiple_of(start, 8)
        return pl.ds(start + shift, count)

    def rows_over(t, shift):
        return pl.ds(2 * T * R + PAD + t * R + shift, X, stride=T * R)

    def coef_of(p, t):
        start = p * (T * Y) + t * Y
        if not isinstance(p, int):
            start = pl.multiple_of(start, 8)
        return pl.ds(start, Y)

    def coef_over(t, shift):
        return pl.ds(T * Y + t * Y + shift, X, stride=T * Y)

    def tile_of(t):
        return slice(t * LANES, (t + 1) * LANES)


    def device(core=core, high=high, low=low, y=y, x=gz):
        return (high * 2 + core, y * 2 + low, x)

    def line_peer(axis, step):
        place = list(here)
        place[axis] = lax.rem(here[axis] + step, sizes[axis])
        return tuple(place)

    partner = device(core=1 - core)

    barrier = pltpu.get_barrier_semaphore()
    z_steps = [(h, l) for h in range(4) for l in range(2) if h or l]
    g_steps = [
        (i, j, l) for i in range(4) for j in range(4) for l in range(2) if i or j or l
    ]
    reached = []
    for axis in range(3):
        for step in range(1, sizes[axis]):
            reached.append(line_peer(axis, step))
    for dx in (nx - 1, 1):
        for dy in (ny - 1, 1):
            reached.append((lax.rem(gx + dx, nx), lax.rem(gy + dy, ny), gz))
    for h, l in z_steps:
        if h and l:
            reached.append(
                device(high=lax.rem(high + h, 4), low=lax.rem(low + l, 2))
            )
    for i, j, l in g_steps:
        if i and (j or l):
            reached.append(
                device(
                    x=lax.rem(gz + i, 4), y=lax.rem(y + j, 4), low=lax.rem(low + l, 2)
                )
            )

    loads = [
        pltpu.make_async_copy(mat_hbm, m.mat, m.load.at[2]),
        pltpu.make_async_copy(now_hbm, m.now, m.load.at[3]),
        pltpu.make_async_copy(prev_hbm, m.prev, m.load.at[4]),
    ]
    for one in loads:
        one.start()
    load_in = pltpu.make_async_copy(win_hbm, m.w_in, m.load.at[0])
    load_out = pltpu.make_async_copy(wout_hbm, m.w_out, m.load.at[1])
    load_in.start()
    load_out.start()

    def clear(missing, ref, *index):
        @pl.when(missing)
        def _():
            for par in range(2):
                ref[(par, *index)] = jnp.zeros(ref.shape[1 + len(index) :], F32)

    ends = ((gx == 0, gx == nx - 1), (gy == 0, gy == ny - 1))
    for side in range(2):
        clear(ends[0][side], m.xrecv, side)
        clear(ends[1][side], m.yrecv, side)
        for other in range(2):
            clear(
                jnp.logical_or(ends[0][side], ends[1][other]),
                m.crecv,
                side * 2 + other,
            )

    @pl.when(gz == 0)
    def _():
        m.zrecv[0] = jnp.zeros(m.zrecv.shape[1:], F32)

    @pl.when(gz == nz - 1)
    def _():
        m.zrecv[1] = jnp.zeros(m.zrecv.shape[1:], F32)

    for place in reached:
        signal(barrier, place)

    lane = lax.broadcasted_iota(jnp.int32, (Y, LANES), 1)
    def pack_edge(values):
        at = lax.broadcasted_iota(jnp.int32, values[0].shape, 1)
        group = lax.shift_right_logical(jnp.bitwise_and(at + 8, LANES - 1), 4)
        packed = values[0]
        for e, value in enumerate(values[1:], 1):
            packed = jnp.where(group == e, pltpu.roll(value, 16 * e, 1), packed)
        return packed

    def open_edge(packed, e, masked=False):
        value = pltpu.roll(packed, LANES - 16 * e, 1) if e else packed
        if masked:
            at = lax.broadcasted_iota(jnp.int32, value.shape, 1)
            value = jnp.where((at < 8) | (at >= LANES - 8), value, 0.0)
        return value

    def face_tiles(ref, index, e, masked=False):
        tiles = [ref[(*index, 1 + 2 * e + t)] for t in range(2)]
        return tiles + [open_edge(ref[(*index, 0)], e, masked)]

    def put_face(ref, side, sources, main, edge):
        if main:
            for e, source in enumerate(sources):
                for t in range(2):
                    ref[side, 1 + 2 * e + t] = source(t)
        if edge:
            ref[side, 0] = pack_edge([source(2) for source in sources])

    def put_rows(entries, main, edge):
        for side, at, second in ((0, 0, 1), (1, Y - 1, Y - 2)):
            sources = [
                lambda t, at=at: A[rows_over(t, at), :],
                lambda t, second=second: A[rows_over(t, second), :],
                lambda t, at=at: B[rows_over(t, at), :],
                lambda t, at=at: C[coef_over(t, at), :],
            ][:entries]
            put_face(m.ysend, side, sources, main, edge)

    def put_planes(entries, main, edge):
        for side, planes in enumerate(((2, 3, 2, 1), (X, X + 1, X + 1, X))):
            sources = [
                lambda t, p=planes[0]: A[rows_of(p, t), :],
                lambda t, p=planes[1]: A[rows_of(p, t), :],
                lambda t, p=planes[2]: B[rows_of(p, t), :],
                lambda t, p=planes[3]: C[coef_of(p, t), :],
            ][:entries]
            put_face(m.xsend, side, sources, main, edge)

    inner_tiles = range(Z // LANES)

    for one in loads:
        one.wait()

    def pack(x, carry):
        material = m.mat[x]
        c = jnp.zeros((Y, Z), F32)
        for number in range(tab_ref.shape[0]):
            c = jnp.where(material == number, tab_ref[number], c)
        n, p = m.now[x], m.prev[x]
        for t in inner_tiles:
            A[rows_of(x + 2, t), :] = n[:, tile_of(t)]
            B[rows_of(x + 2, t), :] = p[:, tile_of(t)]
            C[coef_of(x + 1, t), :] = c[:, tile_of(t)]
            D[coef_of(x + 1, t), :] = 2.0 - 6.0 * c[:, tile_of(t)]
        mine = lax.shift_right_logical(lane, 3) == x
        up, down = [], []
        for field, held_up, held_down in zip((n, p, c), carry[0], carry[1]):
            last = pltpu.roll(field[:, Z - LANES :], lax.rem(x * 8 + 8, LANES), 1)
            first = pltpu.roll(field[:, :LANES], x * 8, 1)
            up.append(jnp.where(mine, last, held_up))
            down.append(jnp.where(mine, first, held_down))
        return tuple(up), tuple(down)

    empty = tuple(jnp.zeros((Y, LANES), F32) for _ in range(3))
    ups, downs = lax.fori_loop(0, X, pack, (empty, empty))
    for i in range(3):
        m.zsend[0, i] = ups[i]
        m.zsend[1, i] = downs[i]

    put_planes(4, True, False)
    put_rows(4, True, False)
    m.nsend[0] = jnp.full((8, LANES), cnt_ref[0].astype(F32))

    pl.semaphore_wait(barrier, len(reached))

    def z_copy(side):
        step = 1 if side == 0 else nz - 1
        return remote(
            m.zsend.at[side],
            m.zrecv.at[side],
            m.z_sem.at[0, side],
            m.z_sem.at[1, side],
            (gx, gy, lax.rem(gz + step, nz)),
        )

    @pl.when(gz < nz - 1)
    def _():
        z_copy(0).start()

    @pl.when(gz > 0)
    def _():
        z_copy(1).start()

    left, right = lax.rem(gx + nx - 1, nx), lax.rem(gx + 1, nx)
    below, above = lax.rem(gy + ny - 1, ny), lax.rem(gy + 1, ny)
    targets_of = (
        (left, gy, gz),
        (right, gy, gz),
        (gx, below, gz),
        (gx, above, gz),
        (left, below, gz),
        (left, above, gz),
        (right, below, gz),
        (right, above, gz),
    )
    sides = (gx > 0, gx < nx - 1, gy > 0, gy < ny - 1)
    has = sides + tuple(
        jnp.logical_and(sides[i], sides[j]) for i in (0, 1) for j in (2, 3)
    )
    opposite = (1, 0, 3, 2, 7, 6, 5, 4)

    def face(d, par, form):
        if d < 4:
            side = d % 2
            send, got = (m.xsend, m.xrecv) if d < 2 else (m.ysend, m.yrecv)
            tiles = (pl.ds(0, 5), pl.ds(1, 8), pl.ds(0, 1))[form]
            src = send.at[side, tiles]
            dst = got.at[par, 1 - side, tiles]
        else:
            src = m.csend.at[d - 4]
            dst = m.crecv.at[par, 7 - d]
        number = d + 8 if form == 2 else d
        arrives = opposite[d] + 8 if form == 2 else opposite[d]
        return remote(
            src, dst, m.f_send.at[number], m.f_recv.at[par, arrives], targets_of[d]
        )

    def each(ds, action):
        for d in ds:

            @pl.when(has[d])
            def _():
                action(d)

    def start(ds, par, form):
        each(ds, lambda d: face(d, par, form).start())

    def sent(ds, par, form):
        each(ds, lambda d: face(d, par, form).wait_send())

    def came(ds, par, form):
        each(ds, lambda d: face(opposite[d], par, form).wait_recv())

    start(range(4), 0, 1)

    def count_copy(axis, step):
        return remote(
            m.nsend.at[axis],
            m.nrecv.at[axis, here[axis]],
            m.n_send.at[axis, step],
            m.n_recv.at[axis, here[axis]],
            line_peer(axis, step),
        )

    def count_start(axis):
        for step in range(1, sizes[axis]):
            count_copy(axis, step).start()
        m.nrecv[axis, here[axis]] = m.nsend[axis]

    def count_finish(axis):
        size = sizes[axis]
        for step in range(1, size):
            count_copy(axis, step).wait_send()
            source = lax.rem(here[axis] + step, size)
            remote(
                m.nsend.at[axis],
                m.nrecv.at[axis, source],
                m.n_send.at[axis, step],
                m.n_recv.at[axis, source],
                line_peer(axis, step),
            ).wait_recv()
        total = m.nrecv[axis, 0]
        for i in range(1, size):
            total = total + m.nrecv[axis, i]
        return total

    count_start(0)

    def whole(parts):
        return jnp.concatenate(parts, axis=1)

    def beside_of(field, p):
        def at(plane, shift):
            return whole([field[rows_of(plane, t, shift), :] for t in range(T)])

        n = at(p, 0)
        beside = at(p + 1, 0) + at(p - 1, 0)
        beside = beside + at(p, 1) + at(p, -1)
        return n, beside + pltpu.roll(n, W - 1, 1) + pltpu.roll(n, 1, 1)

    def update(field, other, p):
        n, beside = beside_of(field, p)
        old = whole([other[rows_of(p, t), :] for t in range(T)])
        c = whole([C[coef_of(p - 1, t), :] for t in range(T)])
        d = whole([D[coef_of(p - 1, t), :] for t in range(T)])
        return d * n - old + c * beside

    across = lax.broadcasted_iota(jnp.int32, (X, W), 0)

    def side_update(n, plus, minus, ends, old, c, d):
        beside = jnp.where(across == X - 1, ends[1], pltpu.roll(n, X - 1, 0))
        beside = beside + jnp.where(across == 0, ends[0], pltpu.roll(n, 1, 0))
        beside = beside + plus + minus
        beside = beside + pltpu.roll(n, W - 1, 1) + pltpu.roll(n, 1, 1)
        return d * n - old + c * beside

    def row_update(field, old, at):
        def row(shift):
            return whole([field[rows_over(t, at + shift), :] for t in range(T)])

        ends = [
            whole([field[rows_of(p, t, at, 1), :] for t in range(T)])
            for p in (1, X + 2)
        ]
        c = whole([C[coef_over(t, at), :] for t in range(T)])
        d = whole([D[coef_over(t, at), :] for t in range(T)])
        return side_update(row(0), row(1), row(-1), ends, old, c, d)

    def first(p, carry=0):
        after = update(A, B, p)
        for t in range(T):
            B[rows_of(p, t), :] = after[:, tile_of(t)]
        return carry

    def second(p, carry=0):
        after = update(B, A, p)
        for t in range(T):
            A[rows_of(p, t), :] = after[:, tile_of(t)]
        return carry

    def last(p, carry):
        out_ref[p - 2] = update(B, A, p)[:, 0:Z]
        return carry

    def early():
        for side in range(2):
            for t in range(T):
                m.held_rows[side, t] = B[rows_over(t, side * (Y - 1)), :]
        lax.fori_loop(3, X + 1, first, 0, unroll=2)

    tiles = X * Y // LANES
    narrow = lax.broadcasted_iota(jnp.int32, (8, LANES), 1)

    def turn(field):
        for x in range(X):
            for half in range(Z // LANES):
                m.rows[half, pl.ds(x, Y, stride=X), :] = field[
                    x, :, half * LANES : (half + 1) * LANES
                ]
        for half in range(Z // LANES):
            for tile in range(tiles):
                at = tile * Z + half * LANES
                m.turned[at : at + LANES, :] = m.rows[
                    half, tile * LANES : (tile + 1) * LANES, :
                ].T

    def pick_one(s, first_row, keep):
        first = m.turned[pl.ds(first_row, 8), :]
        second = m.turned[pl.ds(first_row + Z, 8), :]
        back = jnp.bitwise_and(keep, LANES - 1)
        m.picked[pl.ds(pl.multiple_of(s * 8, 8), 8), :] = jnp.where(
            narrow < keep, pltpu.roll(first, back, 1), pltpu.roll(second, back, 1)
        )

    def pick_inputs(s, carry):
        anchor = anchor_ref[s]
        i = anchor // (Y * Z)
        rest = anchor - i * (Y * Z)
        j = rest // Z
        shift = j * X + i
        first_row = (shift // LANES) * Z + (rest - j * Z)
        keep = LANES - jnp.bitwise_and(shift, LANES - 1)
        m.where[0, s] = first_row
        m.where[1, s] = keep
        pick_one(s, first_row, keep)
        return carry

    def pick_targets(s, carry):
        pick_one(s, m.where[0, s], m.where[1, s])
        return carry

    def picked_values():
        return jnp.concatenate(
            [m.picked[pl.ds(c, slots, stride=8), :] for c in range(8)], axis=1
        )

    def swap(ref, number):
        return remote(
            ref.at[0:slots],
            ref.at[slots : 2 * slots],
            m.p_send.at[number],
            m.p_recv.at[number],
            partner,
        )

    m.turned[tiles * Z : (tiles + 1) * Z, :] = jnp.zeros((Z, LANES), F32)
    turn(m.now)

    @pl.when(gz < nz - 1)
    def _():
        z_copy(0).wait_send()
        z_copy(1).wait_recv()

    @pl.when(gz > 0)
    def _():
        z_copy(1).wait_send()
        z_copy(0).wait_recv()

    def unpack(x, carry):
        values = []
        for i in range(3):
            before = pltpu.roll(m.zrecv[0, i], lax.rem(120 + LANES - x * 8, LANES), 1)
            after = pltpu.roll(m.zrecv[1, i], lax.rem(LANES - x * 8, LANES), 1)
            values.append(
                jnp.where(lane < 8, after, jnp.where(lane >= 120, before, 0.0))
            )
        A[rows_of(x + 2, T - 1), :] = values[0]
        B[rows_of(x + 2, T - 1), :] = values[1]
        C[coef_of(x + 1, T - 1), :] = values[2]
        D[coef_of(x + 1, T - 1), :] = 2.0 - 6.0 * values[2]
        return carry

    lax.fori_loop(0, X, unpack, 0, unroll=2)

    def put_lines():
        for i in range(4):
            plane = 2 if i < 2 else X + 1
            at = 0 if i % 2 == 0 else Y - 1
            for t in range(T):
                m.csend[i, :, tile_of(t)] = A[rows_of(plane, t, at, 1), :]

    put_planes(4, False, True)
    put_rows(4, False, True)
    put_lines()
    start(range(4, 8), 0, 0)
    start(range(4), 0, 2)
    early()

    lax.fori_loop(0, slots, pick_inputs, 0, unroll=8)
    at = lax.broadcasted_iota(jnp.int32, (8 * LANES, wide), 0)
    feature = lax.broadcasted_iota(jnp.int32, (8 * LANES, wide), 1)
    pa = jnp.bitwise_and(at, X - 1)
    pb = jnp.bitwise_and(lax.shift_right_logical(at, 4), 7)
    pc = lax.shift_right_logical(at, 7)
    m.order[...] = jnp.where(
        (pa < PATCH) & (feature == pa * 64 + pb * 8 + pc), 1.0, 0.0
    ).astype(BF16)
    m.inputs[0:slots] = in_order(picked_values(), m.order[...], 3)
    swap(m.inputs, 0).start()

    root = 0.7978845608028654

    def forward(part):
        rows = slice(part * slots, (part + 1) * slots)
        inputs = m.inputs[rows]
        mean = jnp.mean(inputs * inputs, axis=1, keepdims=True)
        normed = (inputs * lax.rsqrt(mean + 1e-06)).astype(BF16)
        pre = matmul(normed, m.w_in[...], ((1,), (0,)))
        tanh = jnp.tanh(root * (pre + 0.044715 * (pre * pre * pre)))
        cdf = 0.5 * (1.0 + tanh)
        act = (pre * cdf).astype(BF16)
        m.act[rows] = act
        m.slope[rows] = cdf + 0.5 * pre * (1.0 - tanh * tanh) * (
            root * (1.0 + (3.0 * 0.044715) * (pre * pre))
        )
        m.base[rows] = inputs + matmul(act, m.w_out[...], ((1,), (0,)))
        source = lax.broadcasted_iota(jnp.int32, (wide, wide // 2), 0)
        column = lax.broadcasted_iota(jnp.int32, (wide, wide // 2), 1)
        block = lax.shift_right_logical(column, 6) * 2 + core
        chosen = jnp.where(
            source == block * 64 + jnp.bitwise_and(column, 63), 1.0, 0.0
        ).astype(BF16)
        m.normed[rows] = matmul(normed, chosen, ((1,), (0,))).astype(BF16)

    def backward(part, count):
        rows = slice(part * slots, (part + 1) * slots)
        err = m.base[rows] - m.targets[rows]
        slot = lax.broadcasted_iota(jnp.int32, (slots, 1), 0).astype(F32)
        valid = (slot < count).astype(F32)
        dout = (2.0 * err * valid / m.total[0:1, 0:1]).astype(BF16)
        m.dout[rows] = dout
        dact = matmul(dout, m.w_out[...], ((1,), (1,)))
        m.dpre[rows] = (dact * m.slope[rows]).astype(BF16)

    for r in range(STEPS // 2):
        par = r % 2
        if r == 0:
            came(range(4), 0, 1)
            came(range(4), 0, 2)
        else:
            came(range(4), par, 0)
        came(range(4, 8), par, 0)
        for side in range(2):
            for e in range(2):
                plane = e + side * (X + 2)
                for t, value in enumerate(face_tiles(m.xrecv, (par, side), e)):
                    A[rows_of(plane, t), :] = value
            for t, value in enumerate(face_tiles(m.yrecv, (par, side), 0)):
                A[rows_over(t, -1 if side == 0 else Y), :] = value
        for t in range(T):
            for i in range(4):
                plane = 1 if i < 2 else X + 2
                at = -1 if i % 2 == 0 else Y
                A[rows_of(plane, t, at, 1), :] = m.crecv[par, i, :, tile_of(t)]
        if r == 0:
            for side, plane, ring_coef in ((0, 1, 0), (1, X + 2, X + 1)):
                olds = face_tiles(m.xrecv, (0, side), 2)
                coefs = face_tiles(m.xrecv, (0, side), 3, True)
                side_olds = face_tiles(m.yrecv, (0, side), 2)
                side_coefs = face_tiles(m.yrecv, (0, side), 3, True)
                for t in range(T):
                    B[rows_of(plane, t), :] = olds[t]
                    C[coef_of(ring_coef, t), :] = coefs[t]
                    D[coef_of(ring_coef, t), :] = 2.0 - 6.0 * coefs[t]
                    m.yold[side, t] = side_olds[t]
                    m.ycoef[side, t] = side_coefs[t]

        for p in (1, 2, X + 1, X + 2):
            first(p)
        for side in range(2):
            at = side * (Y - 1)
            old = whole([m.held_rows[side, t] for t in range(T)])
            value = row_update(A, old, at)
            for t in range(T):
                B[rows_over(t, at), :] = value[:, tile_of(t)]
        for side in range(2):

            def plane_of(ref, *index):
                return whole([ref[(*index, tile)] for tile in range(T)])

            n = whole(face_tiles(m.yrecv, (par, side), 0))
            outer = whole(face_tiles(m.yrecv, (par, side), 1))
            inner = whole([A[rows_over(t, side * (Y - 1)), :] for t in range(T)])
            plus, minus = (inner, outer) if side == 0 else (outer, inner)
            c = plane_of(m.ycoef, side)
            value = side_update(
                n,
                plus,
                minus,
                (m.crecv[par, side], m.crecv[par, 2 + side]),
                plane_of(m.yold, side),
                c,
                2.0 - 6.0 * c,
            )
            for t in range(T):
                m.yold[side, t] = value[:, tile_of(t)]
                B[rows_over(t, -1 if side == 0 else Y), :] = value[:, tile_of(t)]
        if r == 0:
            sent(range(4), 0, 1)
            sent(range(4), 0, 2)
        else:
            sent(range(4), par, 0)
        sent(range(4, 8), par, 0)
        final_round = r == STEPS // 2 - 1

        if final_round:
            lax.fori_loop(2, X + 2, last, 0, unroll=2)
        else:
            for side, rows in ((0, (0, 1)), (1, (Y - 1, Y - 2))):
                values = []
                for at in rows:
                    old = whole([A[rows_over(t, at), :] for t in range(T)])
                    values.append(row_update(B, old, at))
                sources = [lambda t, v=v: v[:, tile_of(t)] for v in values]
                put_face(m.ysend, side, sources, True, True)
                start((2 + side,), 1 - par, 0)
            for p in (2, 3, X, X + 1):
                second(p)
            put_lines()
            start(range(4, 8), 1 - par, 0)
            put_planes(2, True, True)
            start(range(2), 1 - par, 0)
            lax.fori_loop(4, X, second, 0, unroll=2)
            early()
        if r == 0:
            load_in.wait()
            load_out.wait()
            forward(0)
            m.nsend[1] = count_finish(0)
            count_start(1)
        if r == 1:
            swap(m.inputs, 0).wait()
            forward(1)
            m.nsend[2] = count_finish(1)
            count_start(2)
        if r == 2:
            m.total[...] = count_finish(2)

    turn(out_ref)
    lax.fori_loop(0, slots, pick_targets, 0, unroll=16)
    m.targets[0:slots] = in_order(picked_values(), m.order[...], 2)
    swap(m.targets, 1).start()
    backward(0, m.nrecv[0, gx][0:1, 0:1])
    swap(m.targets, 1).wait()
    backward(1, m.nrecv[0, high * 2 + 1 - core][0:1, 0:1])
    half = 512
    places = ((gz, lambda v: device(x=v)), (y, lambda v: device(y=v)))

    def ring(along, piece, relay, fin, send, sems):
        me, to = places[along]
        plus, minus, opposed = [lax.rem(me + d, 4) for d in (1, 3, 2)]
        begin, end = pl.ds(0, 2), pl.ds(2, 2)

        def copy(src, dst, number, peer):
            return remote(src, dst, sems.at[0, number], sems.at[1, number], to(peer))

        copies = [
            copy(piece(begin, opposed), relay.at[0], 0, plus),
            copy(piece(end, opposed), relay.at[1], 1, minus),
            copy(piece(end, plus), fin.at[0, end], 2, plus),
            copy(piece(begin, minus), fin.at[1, begin], 3, minus),
            copy(send.at[0], fin.at[0, begin], 4, plus),
            copy(send.at[1], fin.at[1, end], 5, minus),
        ]

        def open_ring():
            for one in copies[:4]:
                one.start()

        def pass_on():
            copies[0].wait_recv()
            send[0] = relay[0] + piece(begin, plus)[...]
            copies[4].start()
            copies[1].wait_recv()
            send[1] = relay[1] + piece(end, minus)[...]
            copies[5].start()

        def close_ring():
            for one in copies[2:]:
                one.wait_recv()
            total = piece(pl.ds(0, 4), me)[...] + fin[0] + fin[1]
            for one in copies:
                one.wait_send()
            return total

        return open_ring, pass_on, close_ring

    def piece1(batch, colour):
        def piece(part, owner):
            rows = pl.ds(pl.multiple_of(batch * 64 + owner * 16, 8), 16)
            return m.sums.at[part, rows, pl.ds(colour * half, half)]

        return piece

    def piece2(number):
        def piece(part, owner):
            lanes = pl.ds(pl.multiple_of(owner * LANES, LANES), LANES)
            return m.held1.at[number, part, :, lanes]

        return piece

    def rings_of(batch):
        one, two = [], []
        for colour in range(2):
            q = batch * 2 + colour
            one.append(
                ring(
                    colour,
                    piece1(batch, colour),
                    m.relay1.at[q],
                    m.fin1.at[q],
                    m.send1.at[q],
                    m.sems1.at[q],
                )
            )
            two.append(
                ring(
                    1 - colour,
                    piece2(q),
                    m.relay2.at[q],
                    m.fin2.at[q],
                    m.send2.at[q],
                    m.sems2.at[q],
                )
            )
        return one, two

    batches = [rings_of(batch) for batch in range(2)]

    def run(batch, stage, what, held=None):
        for colour, one in enumerate(batches[batch][stage]):
            value = one[what]()
            if held is not None:
                held[batch * 2 + colour] = value

    z_me = high * 2 + low

    def z_piece(batch, h, l):
        rows = pl.ds(pl.multiple_of(l * 8, 8), 8)
        return m.held2.at[pl.ds(batch * 2, 2), h, rows, :]

    z_peers = []
    for h, l in z_steps:
        ph, pw = lax.rem(high + h, 4), lax.rem(low + l, 2)
        z_peers.append((ph, pw, ph * 2 + pw, device(high=ph, low=pw)))

    def z_copy_out(batch, number):
        ph, pw, slot, peer = z_peers[number]
        return remote(
            z_piece(batch, ph, pw),
            m.zgot.at[z_me, batch],
            m.zp_send.at[batch, number],
            m.zp_recv.at[batch, z_me],
            peer,
        )

    def z_start(batch):
        for number in range(7):
            z_copy_out(batch, number).start()
        m.zgot[z_me, batch] = z_piece(batch, high, low)[...]

    def z_finish(batch):
        for number in range(7):
            ph, pw, slot, peer = z_peers[number]
            remote(
                z_piece(batch, high, low),
                m.zgot.at[slot, batch],
                m.zp_send.at[batch, number],
                m.zp_recv.at[batch, slot],
                peer,
            ).wait_recv()

    grad_in = matmul(m.normed[...], m.dpre[...], ((0,), (0,)))
    for h in range(4):
        m.sums[h, 0:64] = grad_in[h * 64 : (h + 1) * 64]
    run(0, 0, 0)
    dout = m.dout[...]
    for h in range(4):
        block = pl.multiple_of((h * 2 + core) * LANES, LANES)
        grad_out = matmul(m.act[:, pl.ds(block, LANES)], dout, ((0,), (0,)))
        m.sums[h, 64:128, 0:512] = grad_out[0:64]
        m.sums[h, 64:128, 512:1024] = grad_out[64:128]
    run(1, 0, 0)
    run(0, 0, 1)
    run(1, 0, 1)
    run(0, 0, 2, m.held1)
    run(0, 1, 0)
    run(1, 0, 2, m.held1)
    run(1, 1, 0)
    run(0, 1, 1)
    run(1, 1, 1)
    run(0, 1, 2, m.held2)
    z_start(0)
    run(1, 1, 2, m.held2)
    z_start(1)
    g_me = (gz * 4 + y) * 2 + low
    g_peers = []
    for i, j, l in g_steps:
        px, py, pw = lax.rem(gz + i, 4), lax.rem(y + j, 4), lax.rem(low + l, 2)
        g_peers.append(((px * 4 + py) * 2 + pw, device(x=px, y=py, low=pw)))

    def g_copy(batch, number, slot):
        return remote(
            m.gathered.at[slot, batch],
            m.gathered.at[slot, batch],
            m.g_send.at[batch, number],
            m.g_recv.at[batch, slot],
            g_peers[number][1],
        )

    for batch in range(2):
        z_finish(batch)
        total = m.zgot[0, batch]
        for slot in range(1, 8):
            total = total + m.zgot[slot, batch]
        m.gathered[g_me, batch] = total
        for number in range(31):
            g_copy(batch, number, g_me).start()
    for batch in range(2):
        for number in range(7):
            z_copy_out(batch, number).wait_send()
    for batch in range(2):
        for number in range(31):
            g_copy(batch, number, g_peers[number][0]).wait_recv()
    sum_ref[...] = m.gathered[...]
    for batch in range(2):
        for number in range(31):
            g_copy(batch, number, g_me).wait_send()


def step(prev, now, material, table, used, anchors, w_in, w_out, sizes):
    X, Y, Z = now.shape
    W = Z + LANES
    T = W // LANES
    slots = anchors.shape[0]
    wide, hidden = w_in.shape
    vmem = pl.BlockSpec(memory_space=pltpu.VMEM)
    smem = pl.BlockSpec(memory_space=pltpu.SMEM)
    hbm = pl.BlockSpec(memory_space=pltpu.HBM)
    dma = pltpu.SemaphoreType.DMA
    most = max(sizes)

    def f32(*shape):
        return pltpu.VMEM(shape, F32)

    def b16(*shape):
        return pltpu.VMEM(shape, BF16)

    scratch = dict(
        A=f32(2 * PAD + (X + 4) * T * R, LANES),
        B=f32(2 * PAD + (X + 4) * T * R, LANES),
        C=f32((X + 2) * T * Y, LANES),
        D=f32((X + 2) * T * Y, LANES),
        now=f32(X, Y, Z),
        prev=f32(X, Y, Z),
        xsend=f32(2, 9, Y, LANES),
        xrecv=f32(2, 2, 9, Y, LANES),
        ysend=f32(2, 9, X, LANES),
        yrecv=f32(2, 2, 9, X, LANES),
        yold=f32(2, T, X, LANES),
        ycoef=f32(2, T, X, LANES),
        held_rows=f32(2, T, X, LANES),
        csend=f32(4, 1, W),
        crecv=f32(2, 4, 1, W),
        zsend=f32(2, 3, Y, LANES),
        zrecv=f32(2, 3, Y, LANES),
        nsend=f32(3, 8, LANES),
        nrecv=f32(3, most, 8, LANES),
        total=f32(8, LANES),
        rows=f32(Z // LANES, X * Y, LANES),
        turned=f32((X * Y // LANES + 1) * Z, LANES),
        picked=f32(8 * slots, LANES),
        mat=pltpu.VMEM((X, Y, Z), jnp.int32),
        where=pltpu.SMEM((2, slots), jnp.int32),
        order=b16(8 * LANES, wide),
        w_in=b16(wide, hidden),
        w_out=b16(hidden, wide),
        inputs=f32(2 * slots, wide),
        targets=f32(2 * slots, wide),
        base=f32(2 * slots, wide),
        normed=b16(2 * slots, wide // 2),
        act=b16(2 * slots, hidden),
        slope=f32(2 * slots, hidden),
        dout=b16(2 * slots, wide),
        dpre=b16(2 * slots, hidden),
        sums=f32(4, 128, 1024),
        relay1=f32(4, 2, 2, 16, 512),
        fin1=f32(4, 2, 4, 16, 512),
        send1=f32(4, 2, 2, 16, 512),
        held1=f32(4, 4, 16, 512),
        relay2=f32(4, 2, 2, 16, LANES),
        fin2=f32(4, 2, 4, 16, LANES),
        send2=f32(4, 2, 2, 16, LANES),
        held2=f32(4, 4, 16, LANES),
        zgot=f32(8, 2, 2, 8, LANES),
        gathered=f32(32, 2, 2, 8, LANES),
        load=dma((5,)),
        z_sem=dma((2, 2)),
        f_send=dma((12,)),
        f_recv=dma((2, 12)),
        n_send=dma((3, most)),
        n_recv=dma((3, most)),
        p_send=dma((2,)),
        p_recv=dma((2,)),
        sems1=dma((4, 2, 6)),
        sems2=dma((4, 2, 6)),
        zp_send=dma((2, 7)),
        zp_recv=dma((2, 8)),
        g_send=dma((2, 31)),
        g_recv=dma((2, 32)),
    )
    return pl.pallas_call(
        functools.partial(step_kernel, tuple(scratch), sizes),
        name="step",
        out_shape=(
            jax.ShapeDtypeStruct((X, Y, Z), F32),
            jax.ShapeDtypeStruct((32, 2, 2, 8, LANES), F32),
        ),
        in_specs=[hbm, hbm, hbm, smem, smem, smem, hbm, hbm],
        out_specs=(vmem, vmem),
        scratch_shapes=list(scratch.values()),
        compiler_params=pltpu.CompilerParams(
            collective_id=0,
            has_side_effects=True,
            vmem_limit_bytes=40 * 1024 * 1024,
        ),
    )(prev, now, material, table, used, anchors, w_in, w_out)


def place_kernel(final_ref, sum_ref, final_out, in_ref, out_ref):
    final_out[...] = final_ref[...]
    for slot in range(32):
        ix, iy, il = slot // 8, slot // 2 % 4, slot % 2
        for colour in range(2):
            one, two = (ix, iy) if colour == 0 else (iy, ix)
            top = one * 16 + il * 8
            at = two * LANES
            left = colour * 512 + at
            low = colour * 64 + top
            in_ref[top : top + 8, left : left + LANES] = sum_ref[slot, 0, colour]
            out_ref[low : low + 8, at : at + LANES] = sum_ref[slot, 1, colour]


def place(final, sums):
    vmem = pl.BlockSpec(memory_space=pltpu.VMEM)
    return pl.pallas_call(
        place_kernel,
        name="place",
        out_shape=(
            jax.ShapeDtypeStruct(final.shape, F32),
            jax.ShapeDtypeStruct((64, 1024), F32),
            jax.ShapeDtypeStruct((128, 512), F32),
        ),
        in_specs=[vmem, vmem],
        out_specs=(vmem, vmem, vmem),
        compiler_params=pltpu.CompilerParams(vmem_limit_bytes=8 * 1024 * 1024),
    )(final, sums)


def body(pressure_prev, pressure_now, material, speed_table, anchors, counts, w_in, w_out):
    sizes = tuple(lax.axis_size(axis) for axis in AXES)
    pressure_prev, pressure_now, material, speed_table, anchors, w_in, w_out = [
        pltpu.with_memory_space_constraint(v, pltpu.HBM)
        for v in (
            pressure_prev,
            pressure_now,
            material,
            speed_table,
            anchors.reshape(-1),
            w_in,
            w_out,
        )
    ]
    final, sums = step(
        pressure_prev,
        pressure_now,
        material,
        speed_table,
        counts.reshape(-1),
        anchors,
        w_in,
        w_out,
        sizes,
    )
    return place(final, sums)


def solution(mesh):
    return jax.shard_map(
        body,
        mesh=mesh,
        in_specs=(
            P("gx", "gy", "gz"),
            P("gx", "gy", "gz"),
            P("gx", "gy", "gz"),
            P(),
            P("gx", "gy", "gz"),
            P("gx", "gy", "gz"),
            P(),
            P(),
        ),
        out_specs=(P("gx", "gy", "gz"), P("gx", None), P("gx", None)),
        check_vma=False,
    )
```

```python
import functools
import types

import jax
import jax.numpy as jnp
from jax import lax
from jax.experimental import pallas as pl
from jax.experimental.pallas import tpu as pltpu
from jax.sharding import PartitionSpec as P

STEPS = 8
PATCH = 8
LANES = 128
R = 32
PAD = 8
AXES = ("gx", "gy", "gz")
F32 = jnp.float32
BF16 = jnp.bfloat16


def remote(src, dst, send_sem, recv_sem, device):
    return pltpu.make_async_remote_copy(
        src_ref=src,
        dst_ref=dst,
        send_sem=send_sem,
        recv_sem=recv_sem,
        device_id=device,
        device_id_type=pl.DeviceIdType.MESH,
    )


def signal(sem, device):
    pl.semaphore_signal(
        sem, inc=1, device_id=device, device_id_type=pl.DeviceIdType.MESH
    )


def matmul(a, b, dims):
    return lax.dot_general(a, b, (dims, ((), ())), preferred_element_type=F32)


def in_order(values, order, parts):
    pieces, rest = [], values
    for part in range(parts):
        pieces.append(rest.astype(BF16))
        rest = rest - pieces[-1].astype(F32)
    terms = matmul(jnp.concatenate(pieces, axis=0), order, ((1,), (0,)))
    rows = values.shape[0]
    total = terms[0:rows]
    for part in range(1, parts):
        total = total + terms[part * rows : (part + 1) * rows]
    return total


def step_kernel(
    names,
    sizes,
    prev_hbm,
    now_hbm,
    mat_hbm,
    tab_ref,
    cnt_ref,
    anchor_ref,
    win_hbm,
    wout_hbm,
    out_ref,
    sum_ref,
    *scratch,
):
    m = types.SimpleNamespace(**dict(zip(names, scratch)))
    nx, ny, nz = sizes
    gx, gy, gz = [lax.axis_index(axis) for axis in AXES]
    here = (gx, gy, gz)
    core, high = lax.rem(gx, 2), gx // 2
    low, y = lax.rem(gy, 2), gy // 2
    X, Y, Z = now_hbm.shape
    W = Z + LANES
    T = W // LANES
    slots = anchor_ref.shape[0]
    wide, hidden = win_hbm.shape
    A, B, C, D = m.A, m.B, m.C, m.D

    def rows_of(p, t, shift=0, count=Y):
        start = p * (T * R) + (PAD + t * R)
        if not isinstance(p, int):
            start = pl.multiple_of(start, 8)
        return pl.ds(start + shift, count)

    def rows_over(t, shift):
        return pl.ds(2 * T * R + PAD + t * R + shift, X, stride=T * R)

    def coef_of(p, t):
        start = p * (T * Y) + t * Y
        if not isinstance(p, int):
            start = pl.multiple_of(start, 8)
        return pl.ds(start, Y)

    def coef_over(t, shift):
        return pl.ds(T * Y + t * Y + shift, X, stride=T * Y)

    def tile_of(t):
        return slice(t * LANES, (t + 1) * LANES)


    def device(core=core, high=high, low=low, y=y, x=gz):
        return (high * 2 + core, y * 2 + low, x)

    def line_peer(axis, step):
        place = list(here)
        place[axis] = lax.rem(here[axis] + step, sizes[axis])
        return tuple(place)

    partner = device(core=1 - core)

    barrier = pltpu.get_barrier_semaphore()
    z_steps = [(h, l) for h in range(4) for l in range(2) if h or l]
    g_steps = [
        (i, j, l) for i in range(4) for j in range(4) for l in range(2) if i or j or l
    ]
    reached = []
    for axis in range(3):
        for step in range(1, sizes[axis]):
            reached.append(line_peer(axis, step))
    for dx in (nx - 1, 1):
        for dy in (ny - 1, 1):
            reached.append((lax.rem(gx + dx, nx), lax.rem(gy + dy, ny), gz))
    for h, l in z_steps:
        if h and l:
            reached.append(
                device(high=lax.rem(high + h, 4), low=lax.rem(low + l, 2))
            )
    for i, j, l in g_steps:
        if i and (j or l):
            reached.append(
                device(
                    x=lax.rem(gz + i, 4), y=lax.rem(y + j, 4), low=lax.rem(low + l, 2)
                )
            )

    loads = [
        pltpu.make_async_copy(mat_hbm, m.mat, m.load.at[2]),
        pltpu.make_async_copy(now_hbm, m.now, m.load.at[3]),
        pltpu.make_async_copy(prev_hbm, m.prev, m.load.at[4]),
    ]
    for one in loads:
        one.start()
    load_in = pltpu.make_async_copy(win_hbm, m.w_in, m.load.at[0])
    load_out = pltpu.make_async_copy(wout_hbm, m.w_out, m.load.at[1])
    load_in.start()
    load_out.start()

    def clear(missing, ref, *index):
        @pl.when(missing)
        def _():
            for par in range(2):
                ref[(par, *index)] = jnp.zeros(ref.shape[1 + len(index) :], F32)

    ends = ((gx == 0, gx == nx - 1), (gy == 0, gy == ny - 1))
    for side in range(2):
        clear(ends[0][side], m.xrecv, side)
        clear(ends[1][side], m.yrecv, side)
        for other in range(2):
            clear(
                jnp.logical_or(ends[0][side], ends[1][other]),
                m.crecv,
                side * 2 + other,
            )

    @pl.when(gz == 0)
    def _():
        m.zrecv[0] = jnp.zeros(m.zrecv.shape[1:], F32)

    @pl.when(gz == nz - 1)
    def _():
        m.zrecv[1] = jnp.zeros(m.zrecv.shape[1:], F32)

    for place in reached:
        signal(barrier, place)

    lane = lax.broadcasted_iota(jnp.int32, (Y, LANES), 1)
    def pack_edge(values):
        at = lax.broadcasted_iota(jnp.int32, values[0].shape, 1)
        group = lax.shift_right_logical(jnp.bitwise_and(at + 8, LANES - 1), 4)
        packed = values[0]
        for e, value in enumerate(values[1:], 1):
            packed = jnp.where(group == e, pltpu.roll(value, 16 * e, 1), packed)
        return packed

    def open_edge(packed, e, masked=False):
        value = pltpu.roll(packed, LANES - 16 * e, 1) if e else packed
        if masked:
            at = lax.broadcasted_iota(jnp.int32, value.shape, 1)
            value = jnp.where((at < 8) | (at >= LANES - 8), value, 0.0)
        return value

    def face_tiles(ref, index, e, masked=False):
        tiles = [ref[(*index, 1 + 2 * e + t)] for t in range(2)]
        return tiles + [open_edge(ref[(*index, 0)], e, masked)]

    def put_face(ref, side, sources, main, edge):
        if main:
            for e, source in enumerate(sources):
                for t in range(2):
                    ref[side, 1 + 2 * e + t] = source(t)
        if edge:
            ref[side, 0] = pack_edge([source(2) for source in sources])

    def put_rows(entries, main, edge):
        for side, at, second in ((0, 0, 1), (1, Y - 1, Y - 2)):
            sources = [
                lambda t, at=at: A[rows_over(t, at), :],
                lambda t, second=second: A[rows_over(t, second), :],
                lambda t, at=at: B[rows_over(t, at), :],
                lambda t, at=at: C[coef_over(t, at), :],
            ][:entries]
            put_face(m.ysend, side, sources, main, edge)

    def put_planes(entries, main, edge):
        for side, planes in enumerate(((2, 3, 2, 1), (X, X + 1, X + 1, X))):
            sources = [
                lambda t, p=planes[0]: A[rows_of(p, t), :],
                lambda t, p=planes[1]: A[rows_of(p, t), :],
                lambda t, p=planes[2]: B[rows_of(p, t), :],
                lambda t, p=planes[3]: C[coef_of(p, t), :],
            ][:entries]
            put_face(m.xsend, side, sources, main, edge)

    inner_tiles = range(Z // LANES)

    for one in loads:
        one.wait()

    def pack(x, carry):
        material = m.mat[x]
        c = jnp.zeros((Y, Z), F32)
        for number in range(tab_ref.shape[0]):
            c = jnp.where(material == number, tab_ref[number], c)
        n, p = m.now[x], m.prev[x]
        for t in inner_tiles:
            A[rows_of(x + 2, t), :] = n[:, tile_of(t)]
            B[rows_of(x + 2, t), :] = p[:, tile_of(t)]
            C[coef_of(x + 1, t), :] = c[:, tile_of(t)]
            D[coef_of(x + 1, t), :] = 2.0 - 6.0 * c[:, tile_of(t)]
        mine = lax.shift_right_logical(lane, 3) == x
        up, down = [], []
        for field, held_up, held_down in zip((n, p, c), carry[0], carry[1]):
            last = pltpu.roll(field[:, Z - LANES :], lax.rem(x * 8 + 8, LANES), 1)
            first = pltpu.roll(field[:, :LANES], x * 8, 1)
            up.append(jnp.where(mine, last, held_up))
            down.append(jnp.where(mine, first, held_down))
        return tuple(up), tuple(down)

    empty = tuple(jnp.zeros((Y, LANES), F32) for _ in range(3))
    ups, downs = lax.fori_loop(0, X, pack, (empty, empty), unroll=2)
    for i in range(3):
        m.zsend[0, i] = ups[i]
        m.zsend[1, i] = downs[i]

    put_planes(4, True, False)
    put_rows(4, True, False)
    m.nsend[0] = jnp.full((8, LANES), cnt_ref[0].astype(F32))

    pl.semaphore_wait(barrier, len(reached))

    def z_copy(side):
        step = 1 if side == 0 else nz - 1
        return remote(
            m.zsend.at[side],
            m.zrecv.at[side],
            m.z_sem.at[0, side],
            m.z_sem.at[1, side],
            (gx, gy, lax.rem(gz + step, nz)),
        )

    @pl.when(gz < nz - 1)
    def _():
        z_copy(0).start()

    @pl.when(gz > 0)
    def _():
        z_copy(1).start()

    left, right = lax.rem(gx + nx - 1, nx), lax.rem(gx + 1, nx)
    below, above = lax.rem(gy + ny - 1, ny), lax.rem(gy + 1, ny)
    targets_of = (
        (left, gy, gz),
        (right, gy, gz),
        (gx, below, gz),
        (gx, above, gz),
        (left, below, gz),
        (left, above, gz),
        (right, below, gz),
        (right, above, gz),
    )
    sides = (gx > 0, gx < nx - 1, gy > 0, gy < ny - 1)
    has = sides + tuple(
        jnp.logical_and(sides[i], sides[j]) for i in (0, 1) for j in (2, 3)
    )
    opposite = (1, 0, 3, 2, 7, 6, 5, 4)

    def face(d, par, form):
        if d < 4:
            side = d % 2
            send, got = (m.xsend, m.xrecv) if d < 2 else (m.ysend, m.yrecv)
            tiles = (pl.ds(0, 5), pl.ds(1, 8), pl.ds(0, 1))[form]
            src = send.at[side, tiles]
            dst = got.at[par, 1 - side, tiles]
        else:
            src = m.csend.at[d - 4]
            dst = m.crecv.at[par, 7 - d]
        number = d + 8 if form == 2 else d
        arrives = opposite[d] + 8 if form == 2 else opposite[d]
        return remote(
            src, dst, m.f_send.at[number], m.f_recv.at[par, arrives], targets_of[d]
        )

    def each(ds, action):
        for d in ds:

            @pl.when(has[d])
            def _():
                action(d)

    def start(ds, par, form):
        each(ds, lambda d: face(d, par, form).start())

    def sent(ds, par, form):
        each(ds, lambda d: face(d, par, form).wait_send())

    def came(ds, par, form):
        each(ds, lambda d: face(opposite[d], par, form).wait_recv())

    start(range(4), 0, 1)

    def count_copy(axis, step):
        return remote(
            m.nsend.at[axis],
            m.nrecv.at[axis, here[axis]],
            m.n_send.at[axis],
            m.n_recv.at[axis],
            line_peer(axis, step),
        )

    def count_start(axis):
        for step in range(1, sizes[axis]):
            count_copy(axis, step).start()
        m.nrecv[axis, here[axis]] = m.nsend[axis]

    def count_finish(axis):
        size = sizes[axis]
        others = m.nrecv.at[axis, 0 : size - 1]
        all_of_them = remote(
            others, others, m.n_send.at[axis], m.n_recv.at[axis], line_peer(axis, 1)
        )
        all_of_them.wait_send()
        all_of_them.wait_recv()
        total = m.nrecv[axis, 0]
        for i in range(1, size):
            total = total + m.nrecv[axis, i]
        return total

    count_start(0)

    def whole(parts):
        return jnp.concatenate(parts, axis=1)

    def beside_of(field, p):
        def at(plane, shift):
            return whole([field[rows_of(plane, t, shift), :] for t in range(T)])

        n = at(p, 0)
        beside = at(p + 1, 0) + at(p - 1, 0)
        beside = beside + at(p, 1) + at(p, -1)
        return n, beside + pltpu.roll(n, W - 1, 1) + pltpu.roll(n, 1, 1)

    def update(field, other, p):
        n, beside = beside_of(field, p)
        old = whole([other[rows_of(p, t), :] for t in range(T)])
        c = whole([C[coef_of(p - 1, t), :] for t in range(T)])
        d = whole([D[coef_of(p - 1, t), :] for t in range(T)])
        return d * n - old + c * beside

    across = lax.broadcasted_iota(jnp.int32, (X, W), 0)

    def side_update(n, plus, minus, ends, old, c, d):
        beside = jnp.where(across == X - 1, ends[1], pltpu.roll(n, X - 1, 0))
        beside = beside + jnp.where(across == 0, ends[0], pltpu.roll(n, 1, 0))
        beside = beside + plus + minus
        beside = beside + pltpu.roll(n, W - 1, 1) + pltpu.roll(n, 1, 1)
        return d * n - old + c * beside

    def row_update(field, old, at):
        def row(shift):
            return whole([field[rows_over(t, at + shift), :] for t in range(T)])

        ends = [
            whole([field[rows_of(p, t, at, 1), :] for t in range(T)])
            for p in (1, X + 2)
        ]
        c = whole([C[coef_over(t, at), :] for t in range(T)])
        d = whole([D[coef_over(t, at), :] for t in range(T)])
        return side_update(row(0), row(1), row(-1), ends, old, c, d)

    def first(p, carry=0):
        after = update(A, B, p)
        for t in range(T):
            B[rows_of(p, t), :] = after[:, tile_of(t)]
        return carry

    def second(p, carry=0):
        after = update(B, A, p)
        for t in range(T):
            A[rows_of(p, t), :] = after[:, tile_of(t)]
        return carry

    def last(p, carry):
        out_ref[p - 2] = update(B, A, p)[:, 0:Z]
        return carry

    def early():
        for side in range(2):
            for t in range(T):
                m.held_rows[side, t] = B[rows_over(t, side * (Y - 1)), :]
        lax.fori_loop(3, X + 1, first, 0, unroll=2)

    tiles = X * Y // LANES
    narrow = lax.broadcasted_iota(jnp.int32, (8, LANES), 1)

    def turn(field):
        for x in range(X):
            for half in range(Z // LANES):
                m.rows[half, pl.ds(x, Y, stride=X), :] = field[
                    x, :, half * LANES : (half + 1) * LANES
                ]
        for half in range(Z // LANES):
            for tile in range(tiles):
                at = tile * Z + half * LANES
                m.turned[at : at + LANES, :] = m.rows[
                    half, tile * LANES : (tile + 1) * LANES, :
                ].T

    def pick_one(s, first_row, keep):
        first = m.turned[pl.ds(first_row, 8), :]
        second = m.turned[pl.ds(first_row + Z, 8), :]
        back = jnp.bitwise_and(keep, LANES - 1)
        m.picked[pl.ds(pl.multiple_of(s * 8, 8), 8), :] = jnp.where(
            narrow < keep, pltpu.roll(first, back, 1), pltpu.roll(second, back, 1)
        )

    def pick_inputs(s, carry):
        anchor = anchor_ref[s]
        i = anchor // (Y * Z)
        rest = anchor - i * (Y * Z)
        j = rest // Z
        shift = j * X + i
        first_row = (shift // LANES) * Z + (rest - j * Z)
        keep = LANES - jnp.bitwise_and(shift, LANES - 1)
        m.where[0, s] = first_row
        m.where[1, s] = keep
        pick_one(s, first_row, keep)
        return carry

    def pick_targets(s, carry):
        pick_one(s, m.where[0, s], m.where[1, s])
        return carry

    def picked_values():
        return jnp.concatenate(
            [m.picked[pl.ds(c, slots, stride=8), :] for c in range(8)], axis=1
        )

    def swap(ref, number):
        return remote(
            ref.at[0:slots],
            ref.at[slots : 2 * slots],
            m.p_send.at[number],
            m.p_recv.at[number],
            partner,
        )

    m.turned[tiles * Z : (tiles + 1) * Z, :] = jnp.zeros((Z, LANES), F32)
    turn(m.now)

    @pl.when(gz < nz - 1)
    def _():
        z_copy(0).wait_send()
        z_copy(1).wait_recv()

    @pl.when(gz > 0)
    def _():
        z_copy(1).wait_send()
        z_copy(0).wait_recv()

    def unpack(x, carry):
        values = []
        for i in range(3):
            before = pltpu.roll(m.zrecv[0, i], lax.rem(120 + LANES - x * 8, LANES), 1)
            after = pltpu.roll(m.zrecv[1, i], lax.rem(LANES - x * 8, LANES), 1)
            values.append(
                jnp.where(lane < 8, after, jnp.where(lane >= 120, before, 0.0))
            )
        A[rows_of(x + 2, T - 1), :] = values[0]
        B[rows_of(x + 2, T - 1), :] = values[1]
        C[coef_of(x + 1, T - 1), :] = values[2]
        D[coef_of(x + 1, T - 1), :] = 2.0 - 6.0 * values[2]
        return carry

    lax.fori_loop(0, X, unpack, 0, unroll=2)

    def put_lines():
        for i in range(4):
            plane = 2 if i < 2 else X + 1
            at = 0 if i % 2 == 0 else Y - 1
            for t in range(T):
                m.csend[i, :, tile_of(t)] = A[rows_of(plane, t, at, 1), :]

    put_planes(4, False, True)
    put_rows(4, False, True)
    put_lines()
    start(range(4, 8), 0, 0)
    start(range(4), 0, 2)
    early()

    lax.fori_loop(0, slots, pick_inputs, 0, unroll=8)
    at = lax.broadcasted_iota(jnp.int32, (8 * LANES, wide), 0)
    feature = lax.broadcasted_iota(jnp.int32, (8 * LANES, wide), 1)
    pa = jnp.bitwise_and(at, X - 1)
    pb = jnp.bitwise_and(lax.shift_right_logical(at, 4), 7)
    pc = lax.shift_right_logical(at, 7)
    m.order[...] = jnp.where(
        (pa < PATCH) & (feature == pa * 64 + pb * 8 + pc), 1.0, 0.0
    ).astype(BF16)
    m.inputs[0:slots] = in_order(picked_values(), m.order[...], 3)
    swap(m.inputs, 0).start()

    root = 0.7978845608028654

    def forward(part):
        rows = slice(part * slots, (part + 1) * slots)
        inputs = m.inputs[rows]
        mean = jnp.mean(inputs * inputs, axis=1, keepdims=True)
        normed = (inputs * lax.rsqrt(mean + 1e-06)).astype(BF16)
        pre = matmul(normed, m.w_in[...], ((1,), (0,)))
        tanh = jnp.tanh(root * (pre + 0.044715 * (pre * pre * pre)))
        cdf = 0.5 * (1.0 + tanh)
        act = (pre * cdf).astype(BF16)
        m.act[rows] = act
        m.slope[rows] = cdf + 0.5 * pre * (1.0 - tanh * tanh) * (
            root * (1.0 + (3.0 * 0.044715) * (pre * pre))
        )
        m.base[rows] = inputs + matmul(act, m.w_out[...], ((1,), (0,)))
        source = lax.broadcasted_iota(jnp.int32, (wide, wide // 2), 0)
        column = lax.broadcasted_iota(jnp.int32, (wide, wide // 2), 1)
        block = lax.shift_right_logical(column, 6) * 2 + core
        chosen = jnp.where(
            source == block * 64 + jnp.bitwise_and(column, 63), 1.0, 0.0
        ).astype(BF16)
        m.normed[rows] = matmul(normed, chosen, ((1,), (0,))).astype(BF16)

    def backward(part, count):
        rows = slice(part * slots, (part + 1) * slots)
        err = m.base[rows] - m.targets[rows]
        slot = lax.broadcasted_iota(jnp.int32, (slots, 1), 0).astype(F32)
        valid = (slot < count).astype(F32)
        dout = (2.0 * err * valid / m.total[0:1, 0:1]).astype(BF16)
        m.dout[rows] = dout
        dact = matmul(dout, m.w_out[...], ((1,), (1,)))
        m.dpre[rows] = (dact * m.slope[rows]).astype(BF16)

    for r in range(STEPS // 2):
        par = r % 2
        if r == 0:
            came(range(4), 0, 1)
            came(range(4), 0, 2)
        else:
            came(range(4), par, 0)
        came(range(4, 8), par, 0)
        for side in range(2):
            for e in range(2):
                plane = e + side * (X + 2)
                for t, value in enumerate(face_tiles(m.xrecv, (par, side), e)):
                    A[rows_of(plane, t), :] = value
            for t, value in enumerate(face_tiles(m.yrecv, (par, side), 0)):
                A[rows_over(t, -1 if side == 0 else Y), :] = value
        for t in range(T):
            for i in range(4):
                plane = 1 if i < 2 else X + 2
                at = -1 if i % 2 == 0 else Y
                A[rows_of(plane, t, at, 1), :] = m.crecv[par, i, :, tile_of(t)]
        if r == 0:
            for side, plane, ring_coef in ((0, 1, 0), (1, X + 2, X + 1)):
                olds = face_tiles(m.xrecv, (0, side), 2)
                coefs = face_tiles(m.xrecv, (0, side), 3, True)
                side_olds = face_tiles(m.yrecv, (0, side), 2)
                side_coefs = face_tiles(m.yrecv, (0, side), 3, True)
                for t in range(T):
                    B[rows_of(plane, t), :] = olds[t]
                    C[coef_of(ring_coef, t), :] = coefs[t]
                    D[coef_of(ring_coef, t), :] = 2.0 - 6.0 * coefs[t]
                    m.yold[side, t] = side_olds[t]
                    m.ycoef[side, t] = side_coefs[t]

        for p in (1, 2, X + 1, X + 2):
            first(p)
        for side in range(2):
            at = side * (Y - 1)
            old = whole([m.held_rows[side, t] for t in range(T)])
            value = row_update(A, old, at)
            for t in range(T):
                B[rows_over(t, at), :] = value[:, tile_of(t)]
        for side in range(2):

            def plane_of(ref, *index):
                return whole([ref[(*index, tile)] for tile in range(T)])

            n = whole(face_tiles(m.yrecv, (par, side), 0))
            outer = whole(face_tiles(m.yrecv, (par, side), 1))
            inner = whole([A[rows_over(t, side * (Y - 1)), :] for t in range(T)])
            plus, minus = (inner, outer) if side == 0 else (outer, inner)
            c = plane_of(m.ycoef, side)
            value = side_update(
                n,
                plus,
                minus,
                (m.crecv[par, side], m.crecv[par, 2 + side]),
                plane_of(m.yold, side),
                c,
                2.0 - 6.0 * c,
            )
            for t in range(T):
                m.yold[side, t] = value[:, tile_of(t)]
                B[rows_over(t, -1 if side == 0 else Y), :] = value[:, tile_of(t)]
        if r == 0:
            sent(range(4), 0, 1)
            sent(range(4), 0, 2)
        else:
            sent(range(4), par, 0)
        sent(range(4, 8), par, 0)
        final_round = r == STEPS // 2 - 1

        if final_round:
            lax.fori_loop(2, X + 2, last, 0, unroll=2)
        else:
            for side, rows in ((0, (0, 1)), (1, (Y - 1, Y - 2))):
                values = []
                for at in rows:
                    old = whole([A[rows_over(t, at), :] for t in range(T)])
                    values.append(row_update(B, old, at))
                sources = [lambda t, v=v: v[:, tile_of(t)] for v in values]
                put_face(m.ysend, side, sources, True, True)
                start((2 + side,), 1 - par, 0)
            for p in (2, 3, X, X + 1):
                second(p)
            put_lines()
            start(range(4, 8), 1 - par, 0)
            put_planes(2, True, True)
            start(range(2), 1 - par, 0)
            lax.fori_loop(4, X, second, 0, unroll=2)
            early()
        if r == 0:
            load_in.wait()
            load_out.wait()
            forward(0)
            m.nsend[1] = count_finish(0)
            count_start(1)
        if r == 1:
            swap(m.inputs, 0).wait()
            forward(1)
            m.nsend[2] = count_finish(1)
            count_start(2)
        if r == 2:
            m.total[...] = count_finish(2)

    turn(out_ref)
    lax.fori_loop(0, slots, pick_targets, 0, unroll=16)
    m.targets[0:slots] = in_order(picked_values(), m.order[...], 2)
    swap(m.targets, 1).start()
    backward(0, m.nrecv[0, gx][0:1, 0:1])
    swap(m.targets, 1).wait()
    backward(1, m.nrecv[0, high * 2 + 1 - core][0:1, 0:1])
    half = 512
    places = ((gz, lambda v: device(x=v)), (y, lambda v: device(y=v)))

    def ring(along, piece, relay, fin, send, sems):
        me, to = places[along]
        plus, minus, opposed = [lax.rem(me + d, 4) for d in (1, 3, 2)]
        begin, end = pl.ds(0, 2), pl.ds(2, 2)

        def copy(src, dst, out, into, peer):
            return remote(src, dst, sems.at[out], sems.at[into], to(peer))

        copies = [
            copy(piece(begin, opposed), relay.at[0], 0, 2, plus),
            copy(piece(end, opposed), relay.at[1], 0, 3, minus),
            copy(piece(end, plus), fin.at[0, end], 1, 4, plus),
            copy(piece(begin, minus), fin.at[1, begin], 1, 4, minus),
            copy(send.at[0], fin.at[0, begin], 1, 4, plus),
            copy(send.at[1], fin.at[1, end], 1, 4, minus),
        ]
        relays = copy(relay, relay, 0, 2, plus)
        fins = copy(fin, fin, 1, 4, plus)

        def open_ring():
            for one in copies[:4]:
                one.start()

        def pass_on():
            copies[0].wait_recv()
            send[0] = relay[0] + piece(begin, plus)[...]
            copies[4].start()
            copies[1].wait_recv()
            send[1] = relay[1] + piece(end, minus)[...]
            copies[5].start()

        def close_ring():
            fins.wait_recv()
            total = piece(pl.ds(0, 4), me)[...] + fin[0] + fin[1]
            relays.wait_send()
            fins.wait_send()
            return total

        return open_ring, pass_on, close_ring

    def piece1(batch, colour):
        def piece(part, owner):
            rows = pl.ds(pl.multiple_of(batch * 64 + owner * 16, 8), 16)
            return m.sums.at[part, rows, pl.ds(colour * half, half)]

        return piece

    def piece2(number):
        def piece(part, owner):
            lanes = pl.ds(pl.multiple_of(owner * LANES, LANES), LANES)
            return m.held1.at[number, part, :, lanes]

        return piece

    def rings_of(batch):
        one, two = [], []
        for colour in range(2):
            q = batch * 2 + colour
            one.append(
                ring(
                    colour,
                    piece1(batch, colour),
                    m.relay1.at[q],
                    m.fin1.at[q],
                    m.send1.at[q],
                    m.sems1.at[q],
                )
            )
            two.append(
                ring(
                    1 - colour,
                    piece2(q),
                    m.relay2.at[q],
                    m.fin2.at[q],
                    m.send2.at[q],
                    m.sems2.at[q],
                )
            )
        return one, two

    batches = [rings_of(batch) for batch in range(2)]

    def run(batch, stage, what, held=None):
        for colour, one in enumerate(batches[batch][stage]):
            value = one[what]()
            if held is not None:
                held[batch * 2 + colour] = value

    z_me = high * 2 + low

    def z_piece(batch, h, l):
        rows = pl.ds(pl.multiple_of(l * 8, 8), 8)
        return m.held2.at[pl.ds(batch * 2, 2), h, rows, :]

    z_peers = []
    for h, l in z_steps:
        ph, pw = lax.rem(high + h, 4), lax.rem(low + l, 2)
        z_peers.append((ph, pw, ph * 2 + pw, device(high=ph, low=pw)))

    def z_copy_out(batch, number):
        ph, pw, slot, peer = z_peers[number]
        return remote(
            z_piece(batch, ph, pw),
            m.zgot.at[z_me, batch],
            m.zp_send.at[batch],
            m.zp_recv.at[batch],
            peer,
        )

    def z_start(batch):
        for number in range(7):
            z_copy_out(batch, number).start()
        m.zgot[z_me, batch] = z_piece(batch, high, low)[...]

    def z_all(batch):
        others = m.zgot.at[0:7, batch]
        return remote(
            others, others, m.zp_send.at[batch], m.zp_recv.at[batch], z_peers[0][3]
        )

    grad_in = matmul(m.normed[...], m.dpre[...], ((0,), (0,)))
    for h in range(4):
        m.sums[h, 0:64] = grad_in[h * 64 : (h + 1) * 64]
    run(0, 0, 0)
    dout = m.dout[...]
    for h in range(4):
        block = pl.multiple_of((h * 2 + core) * LANES, LANES)
        grad_out = matmul(m.act[:, pl.ds(block, LANES)], dout, ((0,), (0,)))
        m.sums[h, 64:128, 0:512] = grad_out[0:64]
        m.sums[h, 64:128, 512:1024] = grad_out[64:128]
    run(1, 0, 0)
    run(0, 0, 1)
    run(1, 0, 1)
    run(0, 0, 2, m.held1)
    run(0, 1, 0)
    run(1, 0, 2, m.held1)
    run(1, 1, 0)
    run(0, 1, 1)
    run(1, 1, 1)
    run(0, 1, 2, m.held2)
    z_start(0)
    run(1, 1, 2, m.held2)
    z_start(1)
    g_me = (gz * 4 + y) * 2 + low
    g_peers = []
    for i, j, l in g_steps:
        px, py, pw = lax.rem(gz + i, 4), lax.rem(y + j, 4), lax.rem(low + l, 2)
        g_peers.append(((px * 4 + py) * 2 + pw, device(x=px, y=py, low=pw)))

    def g_copy(batch, number, slot):
        return remote(
            m.gathered.at[slot, batch],
            m.gathered.at[slot, batch],
            m.g_send.at[batch],
            m.g_recv.at[batch],
            g_peers[number][1],
        )

    for batch in range(2):
        z_all(batch).wait_recv()
        total = m.zgot[0, batch]
        for slot in range(1, 8):
            total = total + m.zgot[slot, batch]
        m.gathered[g_me, batch] = total
        for number in range(31):
            g_copy(batch, number, g_me).start()
    def g_all(batch):
        others = m.gathered.at[0:31, batch]
        return remote(
            others, others, m.g_send.at[batch], m.g_recv.at[batch], g_peers[0][1]
        )

    for batch in range(2):
        z_all(batch).wait_send()
    for batch in range(2):
        g_all(batch).wait_recv()
    sum_ref[...] = m.gathered[...]
    for batch in range(2):
        g_all(batch).wait_send()


def step(prev, now, material, table, used, anchors, w_in, w_out, sizes):
    X, Y, Z = now.shape
    W = Z + LANES
    T = W // LANES
    slots = anchors.shape[0]
    wide, hidden = w_in.shape
    vmem = pl.BlockSpec(memory_space=pltpu.VMEM)
    smem = pl.BlockSpec(memory_space=pltpu.SMEM)
    hbm = pl.BlockSpec(memory_space=pltpu.HBM)
    dma = pltpu.SemaphoreType.DMA
    most = max(sizes)

    def f32(*shape):
        return pltpu.VMEM(shape, F32)

    def b16(*shape):
        return pltpu.VMEM(shape, BF16)

    scratch = dict(
        A=f32(2 * PAD + (X + 4) * T * R, LANES),
        B=f32(2 * PAD + (X + 4) * T * R, LANES),
        C=f32((X + 2) * T * Y, LANES),
        D=f32((X + 2) * T * Y, LANES),
        now=f32(X, Y, Z),
        prev=f32(X, Y, Z),
        xsend=f32(2, 9, Y, LANES),
        xrecv=f32(2, 2, 9, Y, LANES),
        ysend=f32(2, 9, X, LANES),
        yrecv=f32(2, 2, 9, X, LANES),
        yold=f32(2, T, X, LANES),
        ycoef=f32(2, T, X, LANES),
        held_rows=f32(2, T, X, LANES),
        csend=f32(4, 1, W),
        crecv=f32(2, 4, 1, W),
        zsend=f32(2, 3, Y, LANES),
        zrecv=f32(2, 3, Y, LANES),
        nsend=f32(3, 8, LANES),
        nrecv=f32(3, most, 8, LANES),
        total=f32(8, LANES),
        rows=f32(Z // LANES, X * Y, LANES),
        turned=f32((X * Y // LANES + 1) * Z, LANES),
        picked=f32(8 * slots, LANES),
        mat=pltpu.VMEM((X, Y, Z), jnp.int32),
        where=pltpu.SMEM((2, slots), jnp.int32),
        order=b16(8 * LANES, wide),
        w_in=b16(wide, hidden),
        w_out=b16(hidden, wide),
        inputs=f32(2 * slots, wide),
        targets=f32(2 * slots, wide),
        base=f32(2 * slots, wide),
        normed=b16(2 * slots, wide // 2),
        act=b16(2 * slots, hidden),
        slope=f32(2 * slots, hidden),
        dout=b16(2 * slots, wide),
        dpre=b16(2 * slots, hidden),
        sums=f32(4, 128, 1024),
        relay1=f32(4, 2, 2, 16, 512),
        fin1=f32(4, 2, 4, 16, 512),
        send1=f32(4, 2, 2, 16, 512),
        held1=f32(4, 4, 16, 512),
        relay2=f32(4, 2, 2, 16, LANES),
        fin2=f32(4, 2, 4, 16, LANES),
        send2=f32(4, 2, 2, 16, LANES),
        held2=f32(4, 4, 16, LANES),
        zgot=f32(8, 2, 2, 8, LANES),
        gathered=f32(32, 2, 2, 8, LANES),
        load=dma((5,)),
        z_sem=dma((2, 2)),
        f_send=dma((12,)),
        f_recv=dma((2, 12)),
        n_send=dma((3,)),
        n_recv=dma((3,)),
        p_send=dma((2,)),
        p_recv=dma((2,)),
        sems1=dma((4, 5)),
        sems2=dma((4, 5)),
        zp_send=dma((2,)),
        zp_recv=dma((2,)),
        g_send=dma((2,)),
        g_recv=dma((2,)),
    )
    return pl.pallas_call(
        functools.partial(step_kernel, tuple(scratch), sizes),
        name="step",
        out_shape=(
            jax.ShapeDtypeStruct((X, Y, Z), F32),
            jax.ShapeDtypeStruct((32, 2, 2, 8, LANES), F32),
        ),
        in_specs=[hbm, hbm, hbm, smem, smem, smem, hbm, hbm],
        out_specs=(vmem, vmem),
        scratch_shapes=list(scratch.values()),
        compiler_params=pltpu.CompilerParams(
            collective_id=0,
            has_side_effects=True,
            vmem_limit_bytes=40 * 1024 * 1024,
        ),
    )(prev, now, material, table, used, anchors, w_in, w_out)


def place_kernel(final_ref, sum_ref, final_out, in_ref, out_ref):
    final_out[...] = final_ref[...]
    for slot in range(32):
        ix, iy, il = slot // 8, slot // 2 % 4, slot % 2
        for colour in range(2):
            one, two = (ix, iy) if colour == 0 else (iy, ix)
            top = one * 16 + il * 8
            at = two * LANES
            left = colour * 512 + at
            low = colour * 64 + top
            in_ref[top : top + 8, left : left + LANES] = sum_ref[slot, 0, colour]
            out_ref[low : low + 8, at : at + LANES] = sum_ref[slot, 1, colour]


def place(final, sums):
    vmem = pl.BlockSpec(memory_space=pltpu.VMEM)
    return pl.pallas_call(
        place_kernel,
        name="place",
        out_shape=(
            jax.ShapeDtypeStruct(final.shape, F32),
            jax.ShapeDtypeStruct((64, 1024), F32),
            jax.ShapeDtypeStruct((128, 512), F32),
        ),
        in_specs=[vmem, vmem],
        out_specs=(vmem, vmem, vmem),
        compiler_params=pltpu.CompilerParams(vmem_limit_bytes=8 * 1024 * 1024),
    )(final, sums)


def body(pressure_prev, pressure_now, material, speed_table, anchors, counts, w_in, w_out):
    sizes = tuple(lax.axis_size(axis) for axis in AXES)
    pressure_prev, pressure_now, material, speed_table, anchors, w_in, w_out = [
        pltpu.with_memory_space_constraint(v, pltpu.HBM)
        for v in (
            pressure_prev,
            pressure_now,
            material,
            speed_table,
            anchors.reshape(-1),
            w_in,
            w_out,
        )
    ]
    final, sums = step(
        pressure_prev,
        pressure_now,
        material,
        speed_table,
        counts.reshape(-1),
        anchors,
        w_in,
        w_out,
        sizes,
    )
    return place(final, sums)


def solution(mesh):
    return jax.shard_map(
        body,
        mesh=mesh,
        in_specs=(
            P("gx", "gy", "gz"),
            P("gx", "gy", "gz"),
            P("gx", "gy", "gz"),
            P(),
            P("gx", "gy", "gz"),
            P("gx", "gy", "gz"),
            P(),
            P(),
        ),
        out_specs=(P("gx", "gy", "gz"), P("gx", None), P("gx", None)),
        check_vma=False,
    )
```

```python
import functools
import types

import jax
import jax.numpy as jnp
from jax import lax
from jax.experimental import pallas as pl
from jax.experimental.pallas import tpu as pltpu
from jax.sharding import PartitionSpec as P

STEPS = 8
PATCH = 8
LANES = 128
R = 32
PAD = 8
AXES = ("gx", "gy", "gz")
F32 = jnp.float32
BF16 = jnp.bfloat16


def remote(src, dst, send_sem, recv_sem, device):
    return pltpu.make_async_remote_copy(
        src_ref=src,
        dst_ref=dst,
        send_sem=send_sem,
        recv_sem=recv_sem,
        device_id=device,
        device_id_type=pl.DeviceIdType.MESH,
    )


def signal(sem, device):
    pl.semaphore_signal(
        sem, inc=1, device_id=device, device_id_type=pl.DeviceIdType.MESH
    )


def matmul(a, b, dims):
    return lax.dot_general(a, b, (dims, ((), ())), preferred_element_type=F32)


def in_order(values, order, parts):
    pieces, rest = [], values
    for part in range(parts):
        pieces.append(rest.astype(BF16))
        rest = rest - pieces[-1].astype(F32)
    terms = matmul(jnp.concatenate(pieces, axis=0), order, ((1,), (0,)))
    rows = values.shape[0]
    total = terms[0:rows]
    for part in range(1, parts):
        total = total + terms[part * rows : (part + 1) * rows]
    return total


def step_kernel(
    names,
    sizes,
    prev_hbm,
    now_hbm,
    mat_hbm,
    tab_ref,
    cnt_ref,
    anchor_ref,
    win_hbm,
    wout_hbm,
    out_ref,
    sum_ref,
    *scratch,
):
    m = types.SimpleNamespace(**dict(zip(names, scratch)))
    nx, ny, nz = sizes
    gx, gy, gz = [lax.axis_index(axis) for axis in AXES]
    here = (gx, gy, gz)
    core, high = lax.rem(gx, 2), gx // 2
    low, y = lax.rem(gy, 2), gy // 2
    X, Y, Z = now_hbm.shape
    W = Z + LANES
    T = W // LANES
    slots = anchor_ref.shape[0]
    wide, hidden = win_hbm.shape
    A, B, C, D = m.A, m.B, m.C, m.D

    def rows_of(p, t, shift=0, count=Y):
        start = p * (T * R) + (PAD + t * R)
        if not isinstance(p, int):
            start = pl.multiple_of(start, 8)
        return pl.ds(start + shift, count)

    def rows_over(t, shift):
        return pl.ds(2 * T * R + PAD + t * R + shift, X, stride=T * R)

    def coef_of(p, t):
        start = p * (T * Y) + t * Y
        if not isinstance(p, int):
            start = pl.multiple_of(start, 8)
        return pl.ds(start, Y)

    def coef_over(t, shift):
        return pl.ds(T * Y + t * Y + shift, X, stride=T * Y)

    def tile_of(t):
        return slice(t * LANES, (t + 1) * LANES)


    def device(core=core, high=high, low=low, y=y, x=gz):
        return (high * 2 + core, y * 2 + low, x)

    def line_peer(axis, step):
        place = list(here)
        place[axis] = lax.rem(here[axis] + step, sizes[axis])
        return tuple(place)

    partner = device(core=1 - core)

    barrier = pltpu.get_barrier_semaphore()
    z_steps = [(h, l) for h in range(4) for l in range(2) if h or l]
    g_steps = [
        (i, j, l) for i in range(4) for j in range(4) for l in range(2) if i or j or l
    ]
    reached = []
    for axis in range(3):
        for step in range(1, sizes[axis]):
            reached.append(line_peer(axis, step))
    for dx in (nx - 1, 1):
        for dy in (ny - 1, 1):
            reached.append((lax.rem(gx + dx, nx), lax.rem(gy + dy, ny), gz))
    for h, l in z_steps:
        if h and l:
            reached.append(
                device(high=lax.rem(high + h, 4), low=lax.rem(low + l, 2))
            )
    for i, j, l in g_steps:
        if i and (j or l):
            reached.append(
                device(
                    x=lax.rem(gz + i, 4), y=lax.rem(y + j, 4), low=lax.rem(low + l, 2)
                )
            )

    loads = [
        pltpu.make_async_copy(mat_hbm, m.mat, m.load.at[2]),
        pltpu.make_async_copy(now_hbm, m.now, m.load.at[3]),
        pltpu.make_async_copy(prev_hbm, m.prev, m.load.at[4]),
    ]
    for one in loads:
        one.start()
    load_in = pltpu.make_async_copy(win_hbm, m.w_in, m.load.at[0])
    load_out = pltpu.make_async_copy(wout_hbm, m.w_out, m.load.at[1])
    load_in.start()
    load_out.start()

    def clear(missing, ref, *index):
        @pl.when(missing)
        def _():
            for par in range(2):
                ref[(par, *index)] = jnp.zeros(ref.shape[1 + len(index) :], F32)

    ends = ((gx == 0, gx == nx - 1), (gy == 0, gy == ny - 1))
    for side in range(2):
        clear(ends[0][side], m.xrecv, side)
        clear(ends[1][side], m.yrecv, side)
        for other in range(2):
            clear(
                jnp.logical_or(ends[0][side], ends[1][other]),
                m.crecv,
                side * 2 + other,
            )

    @pl.when(gz == 0)
    def _():
        m.zrecv[0] = jnp.zeros(m.zrecv.shape[1:], F32)

    @pl.when(gz == nz - 1)
    def _():
        m.zrecv[1] = jnp.zeros(m.zrecv.shape[1:], F32)

    for place in reversed(reached):
        signal(barrier, place)

    lane = lax.broadcasted_iota(jnp.int32, (Y, LANES), 1)
    def pack_edge(values):
        at = lax.broadcasted_iota(jnp.int32, values[0].shape, 1)
        group = lax.shift_right_logical(jnp.bitwise_and(at + 8, LANES - 1), 4)
        packed = values[0]
        for e, value in enumerate(values[1:], 1):
            packed = jnp.where(group == e, pltpu.roll(value, 16 * e, 1), packed)
        return packed

    def open_edge(packed, e, masked=False):
        value = pltpu.roll(packed, LANES - 16 * e, 1) if e else packed
        if masked:
            at = lax.broadcasted_iota(jnp.int32, value.shape, 1)
            value = jnp.where((at < 8) | (at >= LANES - 8), value, 0.0)
        return value

    def face_tiles(ref, index, e, masked=False):
        tiles = [ref[(*index, 1 + 2 * e + t)] for t in range(2)]
        return tiles + [open_edge(ref[(*index, 0)], e, masked)]

    def put_face(ref, side, sources, main, edge):
        if main:
            for e, source in enumerate(sources):
                for t in range(2):
                    ref[side, 1 + 2 * e + t] = source(t)
        if edge:
            ref[side, 0] = pack_edge([source(2) for source in sources])

    def put_rows(entries, main, edge):
        for side, at, second in ((0, 0, 1), (1, Y - 1, Y - 2)):
            sources = [
                lambda t, at=at: A[rows_over(t, at), :],
                lambda t, second=second: A[rows_over(t, second), :],
                lambda t, at=at: B[rows_over(t, at), :],
                lambda t, at=at: C[coef_over(t, at), :],
            ][:entries]
            put_face(m.ysend, side, sources, main, edge)

    def put_planes(entries, main, edge):
        for side, planes in enumerate(((2, 3, 2, 1), (X, X + 1, X + 1, X))):
            sources = [
                lambda t, p=planes[0]: A[rows_of(p, t), :],
                lambda t, p=planes[1]: A[rows_of(p, t), :],
                lambda t, p=planes[2]: B[rows_of(p, t), :],
                lambda t, p=planes[3]: C[coef_of(p, t), :],
            ][:entries]
            put_face(m.xsend, side, sources, main, edge)

    inner_tiles = range(Z // LANES)

    for one in loads:
        one.wait()

    def pack(x, carry):
        material = m.mat[x]
        c = jnp.zeros((Y, Z), F32)
        for number in range(tab_ref.shape[0]):
            c = jnp.where(material == number, tab_ref[number], c)
        n, p = m.now[x], m.prev[x]
        for t in inner_tiles:
            A[rows_of(x + 2, t), :] = n[:, tile_of(t)]
            B[rows_of(x + 2, t), :] = p[:, tile_of(t)]
            C[coef_of(x + 1, t), :] = c[:, tile_of(t)]
            D[coef_of(x + 1, t), :] = 2.0 - 6.0 * c[:, tile_of(t)]
        mine = lax.shift_right_logical(lane, 3) == x
        up, down = [], []
        for field, held_up, held_down in zip((n, p, c), carry[0], carry[1]):
            last = pltpu.roll(field[:, Z - LANES :], lax.rem(x * 8 + 8, LANES), 1)
            first = pltpu.roll(field[:, :LANES], x * 8, 1)
            up.append(jnp.where(mine, last, held_up))
            down.append(jnp.where(mine, first, held_down))
        return tuple(up), tuple(down)

    empty = tuple(jnp.zeros((Y, LANES), F32) for _ in range(3))
    ups, downs = lax.fori_loop(0, X, pack, (empty, empty), unroll=2)
    for i in range(3):
        m.zsend[0, i] = ups[i]
        m.zsend[1, i] = downs[i]

    put_planes(4, True, False)
    put_rows(4, True, False)
    m.nsend[0] = jnp.full((8, LANES), cnt_ref[0].astype(F32))

    pl.semaphore_wait(barrier, len(reached))

    def z_copy(side):
        step = 1 if side == 0 else nz - 1
        return remote(
            m.zsend.at[side],
            m.zrecv.at[side],
            m.z_sem.at[0, side],
            m.z_sem.at[1, side],
            (gx, gy, lax.rem(gz + step, nz)),
        )

    @pl.when(gz < nz - 1)
    def _():
        z_copy(0).start()

    @pl.when(gz > 0)
    def _():
        z_copy(1).start()

    left, right = lax.rem(gx + nx - 1, nx), lax.rem(gx + 1, nx)
    below, above = lax.rem(gy + ny - 1, ny), lax.rem(gy + 1, ny)
    targets_of = (
        (left, gy, gz),
        (right, gy, gz),
        (gx, below, gz),
        (gx, above, gz),
        (left, below, gz),
        (left, above, gz),
        (right, below, gz),
        (right, above, gz),
    )
    sides = (gx > 0, gx < nx - 1, gy > 0, gy < ny - 1)
    has = sides + tuple(
        jnp.logical_and(sides[i], sides[j]) for i in (0, 1) for j in (2, 3)
    )
    opposite = (1, 0, 3, 2, 7, 6, 5, 4)

    def face(d, par, form):
        if d < 4:
            side = d % 2
            send, got = (m.xsend, m.xrecv) if d < 2 else (m.ysend, m.yrecv)
            tiles = (pl.ds(0, 5), pl.ds(1, 8), pl.ds(0, 1))[form]
            src = send.at[side, tiles]
            dst = got.at[par, 1 - side, tiles]
        else:
            src = m.csend.at[d - 4]
            dst = m.crecv.at[par, 7 - d]
        number = d + 8 if form == 2 else d
        arrives = opposite[d] + 8 if form == 2 else opposite[d]
        return remote(
            src, dst, m.f_send.at[number], m.f_recv.at[par, arrives], targets_of[d]
        )

    def each(ds, action):
        for d in ds:

            @pl.when(has[d])
            def _():
                action(d)

    def start(ds, par, form):
        each(ds, lambda d: face(d, par, form).start())

    def sent(ds, par, form):
        each(ds, lambda d: face(d, par, form).wait_send())

    def came(ds, par, form):
        each(ds, lambda d: face(opposite[d], par, form).wait_recv())

    start(range(4), 0, 1)

    def count_copy(axis, step):
        return remote(
            m.nsend.at[axis],
            m.nrecv.at[axis, here[axis]],
            m.n_send.at[axis],
            m.n_recv.at[axis],
            line_peer(axis, step),
        )

    def count_start(axis):
        for step in range(1, sizes[axis]):
            count_copy(axis, step).start()
        m.nrecv[axis, here[axis]] = m.nsend[axis]

    def count_finish(axis):
        size = sizes[axis]
        others = m.nrecv.at[axis, 0 : size - 1]
        all_of_them = remote(
            others, others, m.n_send.at[axis], m.n_recv.at[axis], line_peer(axis, 1)
        )
        all_of_them.wait_send()
        all_of_them.wait_recv()
        total = m.nrecv[axis, 0]
        for i in range(1, size):
            total = total + m.nrecv[axis, i]
        return total

    count_start(0)

    def whole(parts):
        return jnp.concatenate(parts, axis=1)

    def beside_of(field, p):
        def at(plane, shift):
            return whole([field[rows_of(plane, t, shift), :] for t in range(T)])

        n = at(p, 0)
        beside = at(p + 1, 0) + at(p - 1, 0)
        beside = beside + at(p, 1) + at(p, -1)
        return n, beside + pltpu.roll(n, W - 1, 1) + pltpu.roll(n, 1, 1)

    def update(field, other, p):
        n, beside = beside_of(field, p)
        old = whole([other[rows_of(p, t), :] for t in range(T)])
        c = whole([C[coef_of(p - 1, t), :] for t in range(T)])
        d = whole([D[coef_of(p - 1, t), :] for t in range(T)])
        return d * n - old + c * beside

    across = lax.broadcasted_iota(jnp.int32, (X, W), 0)

    def side_update(n, plus, minus, ends, old, c, d):
        beside = jnp.where(across == X - 1, ends[1], pltpu.roll(n, X - 1, 0))
        beside = beside + jnp.where(across == 0, ends[0], pltpu.roll(n, 1, 0))
        beside = beside + plus + minus
        beside = beside + pltpu.roll(n, W - 1, 1) + pltpu.roll(n, 1, 1)
        return d * n - old + c * beside

    def row_update(field, old, at):
        def row(shift):
            return whole([field[rows_over(t, at + shift), :] for t in range(T)])

        ends = [
            whole([field[rows_of(p, t, at, 1), :] for t in range(T)])
            for p in (1, X + 2)
        ]
        c = whole([C[coef_over(t, at), :] for t in range(T)])
        d = whole([D[coef_over(t, at), :] for t in range(T)])
        return side_update(row(0), row(1), row(-1), ends, old, c, d)

    def first(p, carry=0):
        after = update(A, B, p)
        for t in range(T):
            B[rows_of(p, t), :] = after[:, tile_of(t)]
        return carry

    def second(p, carry=0):
        after = update(B, A, p)
        for t in range(T):
            A[rows_of(p, t), :] = after[:, tile_of(t)]
        return carry

    def last(p, carry):
        out_ref[p - 2] = update(B, A, p)[:, 0:Z]
        return carry

    def early():
        for side in range(2):
            for t in range(T):
                m.held_rows[side, t] = B[rows_over(t, side * (Y - 1)), :]
        lax.fori_loop(3, X + 1, first, 0, unroll=2)

    tiles = X * Y // LANES
    narrow = lax.broadcasted_iota(jnp.int32, (8, LANES), 1)

    def turn(field):
        for x in range(X):
            for half in range(Z // LANES):
                m.rows[half, pl.ds(x, Y, stride=X), :] = field[
                    x, :, half * LANES : (half + 1) * LANES
                ]
        for half in range(Z // LANES):
            for tile in range(tiles):
                at = tile * Z + half * LANES
                m.turned[at : at + LANES, :] = m.rows[
                    half, tile * LANES : (tile + 1) * LANES, :
                ].T

    def pick_one(s, first_row, by):
        first = m.turned[pl.ds(first_row, 8), :]
        second = m.turned[pl.ds(first_row + Z, 8), :]
        back = jnp.bitwise_and(LANES - by, LANES - 1)
        m.picked[pl.ds(pl.multiple_of(s * 8, 8), 8), :] = pltpu.roll(
            jnp.where(narrow >= by, first, second), back, 1
        )

    def pick_inputs(s, carry):
        anchor = anchor_ref[s]
        i = anchor // (Y * Z)
        rest = anchor - i * (Y * Z)
        j = rest // Z
        shift = j * X + i
        first_row = (shift // LANES) * Z + (rest - j * Z)
        by = jnp.bitwise_and(shift, LANES - 1)
        m.where[0, s] = first_row
        m.where[1, s] = by
        pick_one(s, first_row, by)
        return carry

    def pick_targets(s, carry):
        pick_one(s, m.where[0, s], m.where[1, s])
        return carry

    def picked_values():
        return jnp.concatenate(
            [m.picked[pl.ds(c, slots, stride=8), :] for c in range(8)], axis=1
        )

    def swap(ref, number):
        return remote(
            ref.at[0:slots],
            ref.at[slots : 2 * slots],
            m.p_send.at[number],
            m.p_recv.at[number],
            partner,
        )

    m.turned[tiles * Z : (tiles + 1) * Z, :] = jnp.zeros((Z, LANES), F32)
    turn(m.now)

    @pl.when(gz < nz - 1)
    def _():
        z_copy(0).wait_send()
        z_copy(1).wait_recv()

    @pl.when(gz > 0)
    def _():
        z_copy(1).wait_send()
        z_copy(0).wait_recv()

    def unpack(x, carry):
        values = []
        for i in range(3):
            before = pltpu.roll(m.zrecv[0, i], lax.rem(120 + LANES - x * 8, LANES), 1)
            after = pltpu.roll(m.zrecv[1, i], lax.rem(LANES - x * 8, LANES), 1)
            values.append(
                jnp.where(lane < 8, after, jnp.where(lane >= 120, before, 0.0))
            )
        A[rows_of(x + 2, T - 1), :] = values[0]
        B[rows_of(x + 2, T - 1), :] = values[1]
        C[coef_of(x + 1, T - 1), :] = values[2]
        D[coef_of(x + 1, T - 1), :] = 2.0 - 6.0 * values[2]
        return carry

    lax.fori_loop(0, X, unpack, 0, unroll=2)

    def put_lines():
        for i in range(4):
            plane = 2 if i < 2 else X + 1
            at = 0 if i % 2 == 0 else Y - 1
            for t in range(T):
                m.csend[i, :, tile_of(t)] = A[rows_of(plane, t, at, 1), :]

    put_planes(4, False, True)
    put_rows(4, False, True)
    put_lines()
    start(range(4, 8), 0, 0)
    start(range(4), 0, 2)
    early()

    lax.fori_loop(0, slots, pick_inputs, 0, unroll=8)
    at = lax.broadcasted_iota(jnp.int32, (8 * LANES, wide), 0)
    feature = lax.broadcasted_iota(jnp.int32, (8 * LANES, wide), 1)
    pa = jnp.bitwise_and(at, X - 1)
    pb = jnp.bitwise_and(lax.shift_right_logical(at, 4), 7)
    pc = lax.shift_right_logical(at, 7)
    m.order[...] = jnp.where(
        (pa < PATCH) & (feature == pa * 64 + pb * 8 + pc), 1.0, 0.0
    ).astype(BF16)
    m.inputs[0:slots] = in_order(picked_values(), m.order[...], 3)
    swap(m.inputs, 0).start()

    root = 0.7978845608028654

    def forward(part):
        rows = slice(part * slots, (part + 1) * slots)
        inputs = m.inputs[rows]
        mean = jnp.mean(inputs * inputs, axis=1, keepdims=True)
        normed = (inputs * lax.rsqrt(mean + 1e-06)).astype(BF16)
        pre = matmul(normed, m.w_in[...], ((1,), (0,)))
        tanh = jnp.tanh(root * (pre + 0.044715 * (pre * pre * pre)))
        cdf = 0.5 * (1.0 + tanh)
        act = (pre * cdf).astype(BF16)
        m.act[rows] = act
        m.slope[rows] = cdf + 0.5 * pre * (1.0 - tanh * tanh) * (
            root * (1.0 + (3.0 * 0.044715) * (pre * pre))
        )
        m.base[rows] = inputs + matmul(act, m.w_out[...], ((1,), (0,)))
        source = lax.broadcasted_iota(jnp.int32, (wide, wide // 2), 0)
        column = lax.broadcasted_iota(jnp.int32, (wide, wide // 2), 1)
        block = lax.shift_right_logical(column, 6) * 2 + core
        chosen = jnp.where(
            source == block * 64 + jnp.bitwise_and(column, 63), 1.0, 0.0
        ).astype(BF16)
        m.normed[rows] = matmul(normed, chosen, ((1,), (0,))).astype(BF16)

    def backward(part, count):
        rows = slice(part * slots, (part + 1) * slots)
        err = m.base[rows] - m.targets[rows]
        slot = lax.broadcasted_iota(jnp.int32, (slots, 1), 0).astype(F32)
        valid = (slot < count).astype(F32)
        dout = (2.0 * err * valid / m.total[0:1, 0:1]).astype(BF16)
        m.dout[rows] = dout
        dact = matmul(dout, m.w_out[...], ((1,), (1,)))
        m.dpre[rows] = (dact * m.slope[rows]).astype(BF16)

    for r in range(STEPS // 2):
        par = r % 2
        if r == 0:
            came(range(4), 0, 1)
            came(range(4), 0, 2)
        else:
            came(range(4), par, 0)
        for side in range(2):
            for e in range(2):
                plane = e + side * (X + 2)
                for t, value in enumerate(face_tiles(m.xrecv, (par, side), e)):
                    A[rows_of(plane, t), :] = value
            for t, value in enumerate(face_tiles(m.yrecv, (par, side), 0)):
                A[rows_over(t, -1 if side == 0 else Y), :] = value
        if r == 0:
            for side, plane, ring_coef in ((0, 1, 0), (1, X + 2, X + 1)):
                olds = face_tiles(m.xrecv, (0, side), 2)
                coefs = face_tiles(m.xrecv, (0, side), 3, True)
                side_olds = face_tiles(m.yrecv, (0, side), 2)
                side_coefs = face_tiles(m.yrecv, (0, side), 3, True)
                for t in range(T):
                    B[rows_of(plane, t), :] = olds[t]
                    C[coef_of(ring_coef, t), :] = coefs[t]
                    D[coef_of(ring_coef, t), :] = 2.0 - 6.0 * coefs[t]
                    m.yold[side, t] = side_olds[t]
                    m.ycoef[side, t] = side_coefs[t]

        first(2)
        first(X + 1)
        for side in range(2):
            at = side * (Y - 1)
            old = whole([m.held_rows[side, t] for t in range(T)])
            value = row_update(A, old, at)
            for t in range(T):
                B[rows_over(t, at), :] = value[:, tile_of(t)]
        came(range(4, 8), par, 0)
        for t in range(T):
            for i in range(4):
                plane = 1 if i < 2 else X + 2
                at = -1 if i % 2 == 0 else Y
                A[rows_of(plane, t, at, 1), :] = m.crecv[par, i, :, tile_of(t)]
        first(1)
        first(X + 2)
        for side in range(2):

            def plane_of(ref, *index):
                return whole([ref[(*index, tile)] for tile in range(T)])

            n = whole(face_tiles(m.yrecv, (par, side), 0))
            outer = whole(face_tiles(m.yrecv, (par, side), 1))
            inner = whole([A[rows_over(t, side * (Y - 1)), :] for t in range(T)])
            plus, minus = (inner, outer) if side == 0 else (outer, inner)
            c = plane_of(m.ycoef, side)
            value = side_update(
                n,
                plus,
                minus,
                (m.crecv[par, side], m.crecv[par, 2 + side]),
                plane_of(m.yold, side),
                c,
                2.0 - 6.0 * c,
            )
            for t in range(T):
                m.yold[side, t] = value[:, tile_of(t)]
                B[rows_over(t, -1 if side == 0 else Y), :] = value[:, tile_of(t)]
        if r == 0:
            sent(range(4), 0, 1)
            sent(range(4), 0, 2)
        else:
            sent(range(4), par, 0)
        sent(range(4, 8), par, 0)
        final_round = r == STEPS // 2 - 1

        if final_round:
            lax.fori_loop(2, X + 2, last, 0, unroll=2)
        else:
            for side, rows in ((0, (0, 1)), (1, (Y - 1, Y - 2))):
                values = []
                for at in rows:
                    old = whole([A[rows_over(t, at), :] for t in range(T)])
                    values.append(row_update(B, old, at))
                m.csend[side] = values[0][0:1]
                m.csend[2 + side] = values[0][X - 1 : X]
                start((4 + side, 6 + side), 1 - par, 0)
                sources = [lambda t, v=v: v[:, tile_of(t)] for v in values]
                put_face(m.ysend, side, sources, True, True)
                start((2 + side,), 1 - par, 0)
            for p in (2, 3, X, X + 1):
                second(p)
            put_planes(2, True, True)
            start(range(2), 1 - par, 0)
            lax.fori_loop(4, X, second, 0, unroll=2)
            early()
        if r == 0:
            load_in.wait()
            load_out.wait()
            forward(0)
            m.nsend[1] = count_finish(0)
            count_start(1)
        if r == 1:
            swap(m.inputs, 0).wait()
            forward(1)
            m.nsend[2] = count_finish(1)
            count_start(2)
        if r == 2:
            m.total[...] = count_finish(2)

    turn(out_ref)
    lax.fori_loop(0, slots, pick_targets, 0, unroll=16)
    m.targets[0:slots] = in_order(picked_values(), m.order[...], 2)
    swap(m.targets, 1).start()
    backward(0, m.nrecv[0, gx][0:1, 0:1])
    swap(m.targets, 1).wait()
    backward(1, m.nrecv[0, high * 2 + 1 - core][0:1, 0:1])
    half = 512
    places = ((gz, lambda v: device(x=v)), (y, lambda v: device(y=v)))

    def ring(along, piece, relay, fin, send, sems):
        me, to = places[along]
        plus, minus, opposed = [lax.rem(me + d, 4) for d in (1, 3, 2)]
        begin, end = pl.ds(0, 2), pl.ds(2, 2)

        def copy(src, dst, out, into, peer):
            return remote(src, dst, sems.at[out], sems.at[into], to(peer))

        copies = [
            copy(piece(begin, opposed), relay.at[0], 0, 2, plus),
            copy(piece(end, opposed), relay.at[1], 0, 3, minus),
            copy(piece(end, plus), fin.at[0, end], 1, 4, plus),
            copy(piece(begin, minus), fin.at[1, begin], 1, 4, minus),
            copy(send.at[0], fin.at[0, begin], 1, 4, plus),
            copy(send.at[1], fin.at[1, end], 1, 4, minus),
        ]
        relays = copy(relay, relay, 0, 2, plus)
        fins = copy(fin, fin, 1, 4, plus)

        def open_ring():
            for one in copies[:4]:
                one.start()

        def pass_on():
            copies[0].wait_recv()
            send[0] = relay[0] + piece(begin, plus)[...]
            copies[4].start()
            copies[1].wait_recv()
            send[1] = relay[1] + piece(end, minus)[...]
            copies[5].start()

        def close_ring():
            fins.wait_recv()
            total = piece(pl.ds(0, 4), me)[...] + fin[0] + fin[1]
            relays.wait_send()
            fins.wait_send()
            return total

        return open_ring, pass_on, close_ring

    def piece1(batch, colour):
        def piece(part, owner):
            rows = pl.ds(pl.multiple_of(batch * 64 + owner * 16, 8), 16)
            return m.sums.at[part, rows, pl.ds(colour * half, half)]

        return piece

    def piece2(number):
        def piece(part, owner):
            lanes = pl.ds(pl.multiple_of(owner * LANES, LANES), LANES)
            return m.held1.at[number, part, :, lanes]

        return piece

    def rings_of(batch):
        one, two = [], []
        for colour in range(2):
            q = batch * 2 + colour
            one.append(
                ring(
                    colour,
                    piece1(batch, colour),
                    m.relay1.at[q],
                    m.fin1.at[q],
                    m.send1.at[q],
                    m.sems1.at[q],
                )
            )
            two.append(
                ring(
                    1 - colour,
                    piece2(q),
                    m.relay2.at[q],
                    m.fin2.at[q],
                    m.send2.at[q],
                    m.sems2.at[q],
                )
            )
        return one, two

    batches = [rings_of(batch) for batch in range(2)]

    def run(batch, stage, what, held=None):
        for colour, one in enumerate(batches[batch][stage]):
            value = one[what]()
            if held is not None:
                held[batch * 2 + colour] = value

    z_me = high * 2 + low

    def z_piece(batch, h, l):
        rows = pl.ds(pl.multiple_of(l * 8, 8), 8)
        return m.held2.at[pl.ds(batch * 2, 2), h, rows, :]

    z_peers = []
    for h, l in z_steps:
        ph, pw = lax.rem(high + h, 4), lax.rem(low + l, 2)
        z_peers.append((ph, pw, ph * 2 + pw, device(high=ph, low=pw)))

    def z_copy_out(batch, number):
        ph, pw, slot, peer = z_peers[number]
        return remote(
            z_piece(batch, ph, pw),
            m.zgot.at[z_me, batch],
            m.zp_send.at[batch],
            m.zp_recv.at[batch],
            peer,
        )

    def z_start(batch):
        for number in range(7):
            z_copy_out(batch, number).start()
        m.zgot[z_me, batch] = z_piece(batch, high, low)[...]

    def z_all(batch):
        others = m.zgot.at[0:7, batch]
        return remote(
            others, others, m.zp_send.at[batch], m.zp_recv.at[batch], z_peers[0][3]
        )

    grad_in = matmul(m.normed[...], m.dpre[...], ((0,), (0,)))
    for h in range(4):
        m.sums[h, 0:64] = grad_in[h * 64 : (h + 1) * 64]
    run(0, 0, 0)
    dout = m.dout[...]
    for h in range(4):
        block = pl.multiple_of((h * 2 + core) * LANES, LANES)
        grad_out = matmul(m.act[:, pl.ds(block, LANES)], dout, ((0,), (0,)))
        m.sums[h, 64:128, 0:512] = grad_out[0:64]
        m.sums[h, 64:128, 512:1024] = grad_out[64:128]
    run(1, 0, 0)
    run(0, 0, 1)
    run(1, 0, 1)
    run(0, 0, 2, m.held1)
    run(0, 1, 0)
    run(1, 0, 2, m.held1)
    run(1, 1, 0)
    run(0, 1, 1)
    run(1, 1, 1)
    run(0, 1, 2, m.held2)
    z_start(0)
    run(1, 1, 2, m.held2)
    z_start(1)
    g_me = (gz * 4 + y) * 2 + low
    g_peers = []
    for i, j, l in g_steps:
        px, py, pw = lax.rem(gz + i, 4), lax.rem(y + j, 4), lax.rem(low + l, 2)
        g_peers.append(((px * 4 + py) * 2 + pw, device(x=px, y=py, low=pw)))

    def g_copy(batch, number, slot):
        return remote(
            m.gathered.at[slot, batch],
            m.gathered.at[slot, batch],
            m.g_send.at[batch],
            m.g_recv.at[batch],
            g_peers[number][1],
        )

    for batch in range(2):
        z_all(batch).wait_recv()
        total = m.zgot[0, batch]
        for slot in range(1, 8):
            total = total + m.zgot[slot, batch]
        m.gathered[g_me, batch] = total
        for number in range(31):
            g_copy(batch, number, g_me).start()
    def g_all(batch):
        others = m.gathered.at[0:31, batch]
        return remote(
            others, others, m.g_send.at[batch], m.g_recv.at[batch], g_peers[0][1]
        )

    for batch in range(2):
        z_all(batch).wait_send()
    for batch in range(2):
        g_all(batch).wait_recv()
    sum_ref[...] = m.gathered[...]
    for batch in range(2):
        g_all(batch).wait_send()


def step(prev, now, material, table, used, anchors, w_in, w_out, sizes):
    X, Y, Z = now.shape
    W = Z + LANES
    T = W // LANES
    slots = anchors.shape[0]
    wide, hidden = w_in.shape
    vmem = pl.BlockSpec(memory_space=pltpu.VMEM)
    smem = pl.BlockSpec(memory_space=pltpu.SMEM)
    hbm = pl.BlockSpec(memory_space=pltpu.HBM)
    dma = pltpu.SemaphoreType.DMA
    most = max(sizes)

    def f32(*shape):
        return pltpu.VMEM(shape, F32)

    def b16(*shape):
        return pltpu.VMEM(shape, BF16)

    scratch = dict(
        A=f32(2 * PAD + (X + 4) * T * R, LANES),
        B=f32(2 * PAD + (X + 4) * T * R, LANES),
        C=f32((X + 2) * T * Y, LANES),
        D=f32((X + 2) * T * Y, LANES),
        now=f32(X, Y, Z),
        prev=f32(X, Y, Z),
        xsend=f32(2, 9, Y, LANES),
        xrecv=f32(2, 2, 9, Y, LANES),
        ysend=f32(2, 9, X, LANES),
        yrecv=f32(2, 2, 9, X, LANES),
        yold=f32(2, T, X, LANES),
        ycoef=f32(2, T, X, LANES),
        held_rows=f32(2, T, X, LANES),
        csend=f32(4, 1, W),
        crecv=f32(2, 4, 1, W),
        zsend=f32(2, 3, Y, LANES),
        zrecv=f32(2, 3, Y, LANES),
        nsend=f32(3, 8, LANES),
        nrecv=f32(3, most, 8, LANES),
        total=f32(8, LANES),
        rows=f32(Z // LANES, X * Y, LANES),
        turned=f32((X * Y // LANES + 1) * Z, LANES),
        picked=f32(8 * slots, LANES),
        mat=pltpu.VMEM((X, Y, Z), jnp.int32),
        where=pltpu.SMEM((2, slots), jnp.int32),
        order=b16(8 * LANES, wide),
        w_in=b16(wide, hidden),
        w_out=b16(hidden, wide),
        inputs=f32(2 * slots, wide),
        targets=f32(2 * slots, wide),
        base=f32(2 * slots, wide),
        normed=b16(2 * slots, wide // 2),
        act=b16(2 * slots, hidden),
        slope=f32(2 * slots, hidden),
        dout=b16(2 * slots, wide),
        dpre=b16(2 * slots, hidden),
        sums=f32(4, 128, 1024),
        relay1=f32(4, 2, 2, 16, 512),
        fin1=f32(4, 2, 4, 16, 512),
        send1=f32(4, 2, 2, 16, 512),
        held1=f32(4, 4, 16, 512),
        relay2=f32(4, 2, 2, 16, LANES),
        fin2=f32(4, 2, 4, 16, LANES),
        send2=f32(4, 2, 2, 16, LANES),
        held2=f32(4, 4, 16, LANES),
        zgot=f32(8, 2, 2, 8, LANES),
        gathered=f32(32, 2, 2, 8, LANES),
        load=dma((5,)),
        z_sem=dma((2, 2)),
        f_send=dma((12,)),
        f_recv=dma((2, 12)),
        n_send=dma((3,)),
        n_recv=dma((3,)),
        p_send=dma((2,)),
        p_recv=dma((2,)),
        sems1=dma((4, 5)),
        sems2=dma((4, 5)),
        zp_send=dma((2,)),
        zp_recv=dma((2,)),
        g_send=dma((2,)),
        g_recv=dma((2,)),
    )
    return pl.pallas_call(
        functools.partial(step_kernel, tuple(scratch), sizes),
        name="step",
        out_shape=(
            jax.ShapeDtypeStruct((X, Y, Z), F32),
            jax.ShapeDtypeStruct((32, 2, 2, 8, LANES), F32),
        ),
        in_specs=[hbm, hbm, hbm, smem, smem, smem, hbm, hbm],
        out_specs=(vmem, vmem),
        scratch_shapes=list(scratch.values()),
        compiler_params=pltpu.CompilerParams(
            collective_id=0,
            has_side_effects=True,
            vmem_limit_bytes=40 * 1024 * 1024,
        ),
    )(prev, now, material, table, used, anchors, w_in, w_out)


def place_kernel(final_ref, sum_ref, final_out, in_ref, out_ref):
    final_out[...] = final_ref[...]
    for slot in range(32):
        ix, iy, il = slot // 8, slot // 2 % 4, slot % 2
        for colour in range(2):
            one, two = (ix, iy) if colour == 0 else (iy, ix)
            top = one * 16 + il * 8
            at = two * LANES
            left = colour * 512 + at
            low = colour * 64 + top
            in_ref[top : top + 8, left : left + LANES] = sum_ref[slot, 0, colour]
            out_ref[low : low + 8, at : at + LANES] = sum_ref[slot, 1, colour]


def place(final, sums):
    vmem = pl.BlockSpec(memory_space=pltpu.VMEM)
    return pl.pallas_call(
        place_kernel,
        name="place",
        out_shape=(
            jax.ShapeDtypeStruct(final.shape, F32),
            jax.ShapeDtypeStruct((64, 1024), F32),
            jax.ShapeDtypeStruct((128, 512), F32),
        ),
        in_specs=[vmem, vmem],
        out_specs=(vmem, vmem, vmem),
        compiler_params=pltpu.CompilerParams(vmem_limit_bytes=8 * 1024 * 1024),
    )(final, sums)


def body(pressure_prev, pressure_now, material, speed_table, anchors, counts, w_in, w_out):
    sizes = tuple(lax.axis_size(axis) for axis in AXES)
    pressure_prev, pressure_now, material, speed_table, anchors, w_in, w_out = [
        pltpu.with_memory_space_constraint(v, pltpu.HBM)
        for v in (
            pressure_prev,
            pressure_now,
            material,
            speed_table,
            anchors.reshape(-1),
            w_in,
            w_out,
        )
    ]
    final, sums = step(
        pressure_prev,
        pressure_now,
        material,
        speed_table,
        counts.reshape(-1),
        anchors,
        w_in,
        w_out,
        sizes,
    )
    return place(final, sums)


def solution(mesh):
    return jax.shard_map(
        body,
        mesh=mesh,
        in_specs=(
            P("gx", "gy", "gz"),
            P("gx", "gy", "gz"),
            P("gx", "gy", "gz"),
            P(),
            P("gx", "gy", "gz"),
            P("gx", "gy", "gz"),
            P(),
            P(),
        ),
        out_specs=(P("gx", "gy", "gz"), P("gx", None), P("gx", None)),
        check_vma=False,
    )
```

```python
import functools
import types

import jax
import jax.numpy as jnp
from jax import lax
from jax.experimental import pallas as pl
from jax.experimental.pallas import tpu as pltpu
from jax.sharding import PartitionSpec as P

STEPS = 8
PATCH = 8
LANES = 128
R = 32
PAD = 8
AXES = ("gx", "gy", "gz")
F32 = jnp.float32
BF16 = jnp.bfloat16


def remote(src, dst, send_sem, recv_sem, device):
    return pltpu.make_async_remote_copy(
        src_ref=src,
        dst_ref=dst,
        send_sem=send_sem,
        recv_sem=recv_sem,
        device_id=device,
        device_id_type=pl.DeviceIdType.MESH,
    )


def signal(sem, device):
    pl.semaphore_signal(
        sem, inc=1, device_id=device, device_id_type=pl.DeviceIdType.MESH
    )


def matmul(a, b, dims):
    return lax.dot_general(a, b, (dims, ((), ())), preferred_element_type=F32)


def in_order(values, order, parts):
    pieces, rest = [], values
    for part in range(parts):
        pieces.append(rest.astype(BF16))
        rest = rest - pieces[-1].astype(F32)
    terms = matmul(jnp.concatenate(pieces, axis=0), order, ((1,), (0,)))
    rows = values.shape[0]
    total = terms[0:rows]
    for part in range(1, parts):
        total = total + terms[part * rows : (part + 1) * rows]
    return total


def step_kernel(
    names,
    sizes,
    prev_hbm,
    now_hbm,
    mat_hbm,
    tab_ref,
    cnt_ref,
    anchor_ref,
    win_hbm,
    wout_hbm,
    out_ref,
    sum_ref,
    *scratch,
):
    m = types.SimpleNamespace(**dict(zip(names, scratch)))
    nx, ny, nz = sizes
    gx, gy, gz = [lax.axis_index(axis) for axis in AXES]
    here = (gx, gy, gz)
    core, high = lax.rem(gx, 2), gx // 2
    low, y = lax.rem(gy, 2), gy // 2
    X, Y, Z = now_hbm.shape
    W = Z + LANES
    T = W // LANES
    slots = anchor_ref.shape[0]
    wide, hidden = win_hbm.shape
    A, B, C, D = m.A, m.B, m.C, m.D

    def rows_of(p, t, shift=0, count=Y):
        start = p * (T * R) + (PAD + t * R)
        if not isinstance(p, int):
            start = pl.multiple_of(start, 8)
        return pl.ds(start + shift, count)

    def rows_over(t, shift):
        return pl.ds(2 * T * R + PAD + t * R + shift, X, stride=T * R)

    def coef_of(p, t):
        start = p * (T * Y) + t * Y
        if not isinstance(p, int):
            start = pl.multiple_of(start, 8)
        return pl.ds(start, Y)

    def coef_over(t, shift):
        return pl.ds(T * Y + t * Y + shift, X, stride=T * Y)

    def tile_of(t):
        return slice(t * LANES, (t + 1) * LANES)


    def device(core=core, high=high, low=low, y=y, x=gz):
        return (high * 2 + core, y * 2 + low, x)

    def line_peer(axis, step):
        place = list(here)
        place[axis] = lax.rem(here[axis] + step, sizes[axis])
        return tuple(place)

    partner = device(core=1 - core)

    barrier = pltpu.get_barrier_semaphore()
    z_steps = [(h, l) for h in range(4) for l in range(2) if h or l]
    g_steps = [
        (i, j, l) for i in range(4) for j in range(4) for l in range(2) if i or j or l
    ]
    z_steps.sort(key=lambda p: -(2 * min(p[0], 4 - p[0]) + p[1]))
    g_steps.sort(key=lambda p: -(min(p[0], 4 - p[0]) + min(p[1], 4 - p[1]) + p[2]))
    reached = []
    for axis in range(3):
        for step in range(1, sizes[axis]):
            reached.append(line_peer(axis, step))
    for dx in (nx - 1, 1):
        for dy in (ny - 1, 1):
            reached.append((lax.rem(gx + dx, nx), lax.rem(gy + dy, ny), gz))
    for h, l in z_steps:
        if h and l:
            reached.append(
                device(high=lax.rem(high + h, 4), low=lax.rem(low + l, 2))
            )
    for i, j, l in g_steps:
        if i and (j or l):
            reached.append(
                device(
                    x=lax.rem(gz + i, 4), y=lax.rem(y + j, 4), low=lax.rem(low + l, 2)
                )
            )

    loads = [
        pltpu.make_async_copy(mat_hbm, m.mat, m.load.at[2]),
        pltpu.make_async_copy(now_hbm, m.now, m.load.at[3]),
        pltpu.make_async_copy(prev_hbm, m.prev, m.load.at[4]),
    ]
    for one in loads:
        one.start()
    load_in = pltpu.make_async_copy(win_hbm, m.w_in, m.load.at[0])
    load_out = pltpu.make_async_copy(wout_hbm, m.w_out, m.load.at[1])
    load_in.start()
    load_out.start()

    def clear(missing, ref, *index):
        @pl.when(missing)
        def _():
            for par in range(2):
                ref[(par, *index)] = jnp.zeros(ref.shape[1 + len(index) :], F32)

    ends = ((gx == 0, gx == nx - 1), (gy == 0, gy == ny - 1))
    for side in range(2):
        clear(ends[0][side], m.xrecv, side)
        clear(ends[1][side], m.yrecv, side)
        for other in range(2):
            clear(
                jnp.logical_or(ends[0][side], ends[1][other]),
                m.crecv,
                side * 2 + other,
            )

    @pl.when(gz == 0)
    def _():
        m.zrecv[0] = jnp.zeros(m.zrecv.shape[1:], F32)

    @pl.when(gz == nz - 1)
    def _():
        m.zrecv[1] = jnp.zeros(m.zrecv.shape[1:], F32)

    for place in reversed(reached):
        signal(barrier, place)

    lane = lax.broadcasted_iota(jnp.int32, (Y, LANES), 1)
    def pack_edge(values):
        at = lax.broadcasted_iota(jnp.int32, values[0].shape, 1)
        group = lax.shift_right_logical(jnp.bitwise_and(at + 8, LANES - 1), 4)
        packed = values[0]
        for e, value in enumerate(values[1:], 1):
            packed = jnp.where(group == e, pltpu.roll(value, 16 * e, 1), packed)
        return packed

    def open_edge(packed, e, masked=False):
        value = pltpu.roll(packed, LANES - 16 * e, 1) if e else packed
        if masked:
            at = lax.broadcasted_iota(jnp.int32, value.shape, 1)
            value = jnp.where((at < 8) | (at >= LANES - 8), value, 0.0)
        return value

    def face_tiles(ref, index, e, masked=False):
        tiles = [ref[(*index, 1 + 2 * e + t)] for t in range(2)]
        return tiles + [open_edge(ref[(*index, 0)], e, masked)]

    def put_face(ref, side, sources, main, edge):
        if main:
            for e, source in enumerate(sources):
                for t in range(2):
                    ref[side, 1 + 2 * e + t] = source(t)
        if edge:
            ref[side, 0] = pack_edge([source(2) for source in sources])

    def put_rows(entries, main, edge):
        for side, at, second in ((0, 0, 1), (1, Y - 1, Y - 2)):
            sources = [
                lambda t, at=at: A[rows_over(t, at), :],
                lambda t, second=second: A[rows_over(t, second), :],
                lambda t, at=at: B[rows_over(t, at), :],
                lambda t, at=at: C[coef_over(t, at), :],
            ][:entries]
            put_face(m.ysend, side, sources, main, edge)

    def put_planes(entries, main, edge):
        for side, planes in enumerate(((2, 3, 2, 1), (X, X + 1, X + 1, X))):
            sources = [
                lambda t, p=planes[0]: A[rows_of(p, t), :],
                lambda t, p=planes[1]: A[rows_of(p, t), :],
                lambda t, p=planes[2]: B[rows_of(p, t), :],
                lambda t, p=planes[3]: C[coef_of(p, t), :],
            ][:entries]
            put_face(m.xsend, side, sources, main, edge)

    inner_tiles = range(Z // LANES)

    for one in loads:
        one.wait()

    def pack(x, carry):
        material = m.mat[x]
        c = jnp.zeros((Y, Z), F32)
        for number in range(tab_ref.shape[0]):
            c = jnp.where(material == number, tab_ref[number], c)
        n, p = m.now[x], m.prev[x]
        for t in inner_tiles:
            A[rows_of(x + 2, t), :] = n[:, tile_of(t)]
            B[rows_of(x + 2, t), :] = p[:, tile_of(t)]
            C[coef_of(x + 1, t), :] = c[:, tile_of(t)]
            D[coef_of(x + 1, t), :] = 2.0 - 6.0 * c[:, tile_of(t)]
        mine = lax.shift_right_logical(lane, 3) == x
        up, down = [], []
        for field, held_up, held_down in zip((n, p, c), carry[0], carry[1]):
            last = pltpu.roll(field[:, Z - LANES :], lax.rem(x * 8 + 8, LANES), 1)
            first = pltpu.roll(field[:, :LANES], x * 8, 1)
            up.append(jnp.where(mine, last, held_up))
            down.append(jnp.where(mine, first, held_down))
        return tuple(up), tuple(down)

    empty = tuple(jnp.zeros((Y, LANES), F32) for _ in range(3))
    ups, downs = lax.fori_loop(0, X, pack, (empty, empty), unroll=2)
    for i in range(3):
        m.zsend[0, i] = ups[i]
        m.zsend[1, i] = downs[i]

    put_planes(4, True, False)
    put_rows(4, True, False)
    m.nsend[0] = jnp.full((8, LANES), cnt_ref[0].astype(F32))

    pl.semaphore_wait(barrier, len(reached))

    def z_copy(side):
        step = 1 if side == 0 else nz - 1
        return remote(
            m.zsend.at[side],
            m.zrecv.at[side],
            m.z_sem.at[0, side],
            m.z_sem.at[1, side],
            (gx, gy, lax.rem(gz + step, nz)),
        )

    @pl.when(gz < nz - 1)
    def _():
        z_copy(0).start()

    @pl.when(gz > 0)
    def _():
        z_copy(1).start()

    left, right = lax.rem(gx + nx - 1, nx), lax.rem(gx + 1, nx)
    below, above = lax.rem(gy + ny - 1, ny), lax.rem(gy + 1, ny)
    targets_of = (
        (left, gy, gz),
        (right, gy, gz),
        (gx, below, gz),
        (gx, above, gz),
        (left, below, gz),
        (left, above, gz),
        (right, below, gz),
        (right, above, gz),
    )
    sides = (gx > 0, gx < nx - 1, gy > 0, gy < ny - 1)
    has = sides + tuple(
        jnp.logical_and(sides[i], sides[j]) for i in (0, 1) for j in (2, 3)
    )
    opposite = (1, 0, 3, 2, 7, 6, 5, 4)

    def face(d, par, form):
        if d < 4:
            side = d % 2
            send, got = (m.xsend, m.xrecv) if d < 2 else (m.ysend, m.yrecv)
            tiles = (pl.ds(0, 5), pl.ds(1, 8), pl.ds(0, 1))[form]
            src = send.at[side, tiles]
            dst = got.at[par, 1 - side, tiles]
        else:
            src = m.csend.at[d - 4]
            dst = m.crecv.at[par, 7 - d]
        number = d + 8 if form == 2 else d
        arrives = opposite[d] + 8 if form == 2 else opposite[d]
        return remote(
            src, dst, m.f_send.at[number], m.f_recv.at[par, arrives], targets_of[d]
        )

    def each(ds, action):
        for d in ds:

            @pl.when(has[d])
            def _():
                action(d)

    def start(ds, par, form):
        each(ds, lambda d: face(d, par, form).start())

    def sent(ds, par, form):
        each(ds, lambda d: face(d, par, form).wait_send())

    def came(ds, par, form):
        each(ds, lambda d: face(opposite[d], par, form).wait_recv())

    start(range(4), 0, 1)

    def count_copy(axis, step):
        return remote(
            m.nsend.at[axis],
            m.nrecv.at[axis, here[axis]],
            m.n_send.at[axis],
            m.n_recv.at[axis],
            line_peer(axis, step),
        )

    def count_start(axis):
        for step in range(1, sizes[axis]):
            count_copy(axis, step).start()
        m.nrecv[axis, here[axis]] = m.nsend[axis]

    def count_finish(axis):
        size = sizes[axis]
        others = m.nrecv.at[axis, 0 : size - 1]
        all_of_them = remote(
            others, others, m.n_send.at[axis], m.n_recv.at[axis], line_peer(axis, 1)
        )
        all_of_them.wait_send()
        all_of_them.wait_recv()
        total = m.nrecv[axis, 0]
        for i in range(1, size):
            total = total + m.nrecv[axis, i]
        return total

    count_start(0)

    def whole(parts):
        return jnp.concatenate(parts, axis=1)

    def beside_of(field, p):
        def at(plane, shift):
            return whole([field[rows_of(plane, t, shift), :] for t in range(T)])

        n = at(p, 0)
        beside = at(p + 1, 0) + at(p - 1, 0)
        beside = beside + at(p, 1) + at(p, -1)
        return n, beside + pltpu.roll(n, W - 1, 1) + pltpu.roll(n, 1, 1)

    def update(field, other, p):
        n, beside = beside_of(field, p)
        old = whole([other[rows_of(p, t), :] for t in range(T)])
        c = whole([C[coef_of(p - 1, t), :] for t in range(T)])
        d = whole([D[coef_of(p - 1, t), :] for t in range(T)])
        return d * n - old + c * beside

    across = lax.broadcasted_iota(jnp.int32, (X, W), 0)

    def side_update(n, plus, minus, ends, old, c, d):
        beside = jnp.where(across == X - 1, ends[1], pltpu.roll(n, X - 1, 0))
        beside = beside + jnp.where(across == 0, ends[0], pltpu.roll(n, 1, 0))
        beside = beside + plus + minus
        beside = beside + pltpu.roll(n, W - 1, 1) + pltpu.roll(n, 1, 1)
        return d * n - old + c * beside

    def row_update(field, old, at):
        def row(shift):
            return whole([field[rows_over(t, at + shift), :] for t in range(T)])

        ends = [
            whole([field[rows_of(p, t, at, 1), :] for t in range(T)])
            for p in (1, X + 2)
        ]
        c = whole([C[coef_over(t, at), :] for t in range(T)])
        d = whole([D[coef_over(t, at), :] for t in range(T)])
        return side_update(row(0), row(1), row(-1), ends, old, c, d)

    def first(p, carry=0):
        after = update(A, B, p)
        for t in range(T):
            B[rows_of(p, t), :] = after[:, tile_of(t)]
        return carry

    def second(p, carry=0):
        after = update(B, A, p)
        for t in range(T):
            A[rows_of(p, t), :] = after[:, tile_of(t)]
        return carry

    def last(p, carry):
        out_ref[p - 2] = update(B, A, p)[:, 0:Z]
        return carry

    def early():
        for side in range(2):
            for t in range(T):
                m.held_rows[side, t] = B[rows_over(t, side * (Y - 1)), :]
        lax.fori_loop(3, X + 1, first, 0, unroll=2)

    tiles = X * Y // LANES
    narrow = lax.broadcasted_iota(jnp.int32, (8, LANES), 1)

    def turn(field):
        for x in range(X):
            for half in range(Z // LANES):
                m.rows[half, pl.ds(x, Y, stride=X), :] = field[
                    x, :, half * LANES : (half + 1) * LANES
                ]
        for half in range(Z // LANES):
            for tile in range(tiles):
                at = tile * Z + half * LANES
                m.turned[at : at + LANES, :] = m.rows[
                    half, tile * LANES : (tile + 1) * LANES, :
                ].T

    def pick_one(s, first_row, by):
        first = m.turned[pl.ds(first_row, 8), :]
        second = m.turned[pl.ds(first_row + Z, 8), :]
        back = jnp.bitwise_and(LANES - by, LANES - 1)
        m.picked[pl.ds(pl.multiple_of(s * 8, 8), 8), :] = pltpu.roll(
            jnp.where(narrow >= by, first, second), back, 1
        )

    def pick_inputs(s, carry):
        anchor = anchor_ref[s]
        i = anchor // (Y * Z)
        rest = anchor - i * (Y * Z)
        j = rest // Z
        shift = j * X + i
        first_row = (shift // LANES) * Z + (rest - j * Z)
        by = jnp.bitwise_and(shift, LANES - 1)
        m.where[0, s] = first_row
        m.where[1, s] = by
        pick_one(s, first_row, by)
        return carry

    def pick_targets(s, carry):
        pick_one(s, m.where[0, s], m.where[1, s])
        return carry

    def picked_values():
        return jnp.concatenate(
            [m.picked[pl.ds(c, slots, stride=8), :] for c in range(8)], axis=1
        )

    def swap(ref, number):
        return remote(
            ref.at[0:slots],
            ref.at[slots : 2 * slots],
            m.p_send.at[number],
            m.p_recv.at[number],
            partner,
        )

    m.turned[tiles * Z : (tiles + 1) * Z, :] = jnp.zeros((Z, LANES), F32)
    turn(m.now)

    @pl.when(gz < nz - 1)
    def _():
        z_copy(0).wait_send()
        z_copy(1).wait_recv()

    @pl.when(gz > 0)
    def _():
        z_copy(1).wait_send()
        z_copy(0).wait_recv()

    def unpack(x, carry):
        values = []
        for i in range(3):
            before = pltpu.roll(m.zrecv[0, i], lax.rem(120 + LANES - x * 8, LANES), 1)
            after = pltpu.roll(m.zrecv[1, i], lax.rem(LANES - x * 8, LANES), 1)
            values.append(
                jnp.where(lane < 8, after, jnp.where(lane >= 120, before, 0.0))
            )
        A[rows_of(x + 2, T - 1), :] = values[0]
        B[rows_of(x + 2, T - 1), :] = values[1]
        C[coef_of(x + 1, T - 1), :] = values[2]
        D[coef_of(x + 1, T - 1), :] = 2.0 - 6.0 * values[2]
        return carry

    lax.fori_loop(0, X, unpack, 0, unroll=2)

    def put_lines():
        for i in range(4):
            plane = 2 if i < 2 else X + 1
            at = 0 if i % 2 == 0 else Y - 1
            for t in range(T):
                m.csend[i, :, tile_of(t)] = A[rows_of(plane, t, at, 1), :]

    put_planes(4, False, True)
    put_rows(4, False, True)
    put_lines()
    start(range(4, 8), 0, 0)
    start(range(4), 0, 2)
    early()

    lax.fori_loop(0, slots, pick_inputs, 0, unroll=8)
    at = lax.broadcasted_iota(jnp.int32, (8 * LANES, wide), 0)
    feature = lax.broadcasted_iota(jnp.int32, (8 * LANES, wide), 1)
    pa = jnp.bitwise_and(at, X - 1)
    pb = jnp.bitwise_and(lax.shift_right_logical(at, 4), 7)
    pc = lax.shift_right_logical(at, 7)
    m.order[...] = jnp.where(
        (pa < PATCH) & (feature == pa * 64 + pb * 8 + pc), 1.0, 0.0
    ).astype(BF16)
    m.inputs[0:slots] = in_order(picked_values(), m.order[...], 3)
    swap(m.inputs, 0).start()

    root = 0.7978845608028654

    def forward(part):
        rows = slice(part * slots, (part + 1) * slots)
        inputs = m.inputs[rows]
        mean = jnp.mean(inputs * inputs, axis=1, keepdims=True)
        normed = (inputs * lax.rsqrt(mean + 1e-06)).astype(BF16)
        pre = matmul(normed, m.w_in[...], ((1,), (0,)))
        tanh = jnp.tanh(root * (pre + 0.044715 * (pre * pre * pre)))
        cdf = 0.5 * (1.0 + tanh)
        act = (pre * cdf).astype(BF16)
        m.act[rows] = act
        m.slope[rows] = cdf + 0.5 * pre * (1.0 - tanh * tanh) * (
            root * (1.0 + (3.0 * 0.044715) * (pre * pre))
        )
        m.base[rows] = inputs + matmul(act, m.w_out[...], ((1,), (0,)))
        source = lax.broadcasted_iota(jnp.int32, (wide, wide // 2), 0)
        column = lax.broadcasted_iota(jnp.int32, (wide, wide // 2), 1)
        block = lax.shift_right_logical(column, 6) * 2 + core
        chosen = jnp.where(
            source == block * 64 + jnp.bitwise_and(column, 63), 1.0, 0.0
        ).astype(BF16)
        m.normed[rows] = matmul(normed, chosen, ((1,), (0,))).astype(BF16)

    def backward(part, count):
        rows = slice(part * slots, (part + 1) * slots)
        err = m.base[rows] - m.targets[rows]
        slot = lax.broadcasted_iota(jnp.int32, (slots, 1), 0).astype(F32)
        valid = (slot < count).astype(F32)
        dout = (2.0 * err * valid / m.total[0:1, 0:1]).astype(BF16)
        m.dout[rows] = dout
        dact = matmul(dout, m.w_out[...], ((1,), (1,)))
        m.dpre[rows] = (dact * m.slope[rows]).astype(BF16)

    for r in range(STEPS // 2):
        par = r % 2
        if r == 0:
            came(range(4), 0, 1)
            came(range(4), 0, 2)
        else:
            came(range(4), par, 0)
        for side in range(2):
            for e in range(2):
                plane = e + side * (X + 2)
                for t, value in enumerate(face_tiles(m.xrecv, (par, side), e)):
                    A[rows_of(plane, t), :] = value
            for t, value in enumerate(face_tiles(m.yrecv, (par, side), 0)):
                A[rows_over(t, -1 if side == 0 else Y), :] = value
        if r == 0:
            for side, plane, ring_coef in ((0, 1, 0), (1, X + 2, X + 1)):
                olds = face_tiles(m.xrecv, (0, side), 2)
                coefs = face_tiles(m.xrecv, (0, side), 3, True)
                side_olds = face_tiles(m.yrecv, (0, side), 2)
                side_coefs = face_tiles(m.yrecv, (0, side), 3, True)
                for t in range(T):
                    B[rows_of(plane, t), :] = olds[t]
                    C[coef_of(ring_coef, t), :] = coefs[t]
                    D[coef_of(ring_coef, t), :] = 2.0 - 6.0 * coefs[t]
                    m.yold[side, t] = side_olds[t]
                    m.ycoef[side, t] = side_coefs[t]

        first(2)
        first(X + 1)
        for side in range(2):
            at = side * (Y - 1)
            old = whole([m.held_rows[side, t] for t in range(T)])
            value = row_update(A, old, at)
            for t in range(T):
                B[rows_over(t, at), :] = value[:, tile_of(t)]
        came(range(4, 8), par, 0)
        for t in range(T):
            for i in range(4):
                plane = 1 if i < 2 else X + 2
                at = -1 if i % 2 == 0 else Y
                A[rows_of(plane, t, at, 1), :] = m.crecv[par, i, :, tile_of(t)]
        first(1)
        first(X + 2)
        for side in range(2):

            def plane_of(ref, *index):
                return whole([ref[(*index, tile)] for tile in range(T)])

            n = whole(face_tiles(m.yrecv, (par, side), 0))
            outer = whole(face_tiles(m.yrecv, (par, side), 1))
            inner = whole([A[rows_over(t, side * (Y - 1)), :] for t in range(T)])
            plus, minus = (inner, outer) if side == 0 else (outer, inner)
            c = plane_of(m.ycoef, side)
            value = side_update(
                n,
                plus,
                minus,
                (m.crecv[par, side], m.crecv[par, 2 + side]),
                plane_of(m.yold, side),
                c,
                2.0 - 6.0 * c,
            )
            for t in range(T):
                m.yold[side, t] = value[:, tile_of(t)]
                B[rows_over(t, -1 if side == 0 else Y), :] = value[:, tile_of(t)]
        if r == 0:
            sent(range(4), 0, 1)
            sent(range(4), 0, 2)
        else:
            sent(range(4), par, 0)
        sent(range(4, 8), par, 0)
        final_round = r == STEPS // 2 - 1

        if final_round:
            lax.fori_loop(2, X + 2, last, 0, unroll=2)
        else:
            for side, rows in ((0, (0, 1)), (1, (Y - 1, Y - 2))):
                values = []
                for at in rows:
                    old = whole([A[rows_over(t, at), :] for t in range(T)])
                    values.append(row_update(B, old, at))
                m.csend[side] = values[0][0:1]
                m.csend[2 + side] = values[0][X - 1 : X]
                start((4 + side, 6 + side), 1 - par, 0)
                sources = [lambda t, v=v: v[:, tile_of(t)] for v in values]
                put_face(m.ysend, side, sources, True, True)
                start((2 + side,), 1 - par, 0)
            for p in (2, 3, X, X + 1):
                second(p)
            put_planes(2, True, True)
            start(range(2), 1 - par, 0)
            lax.fori_loop(4, X, second, 0, unroll=2)
            early()
        if r == 0:
            load_in.wait()
            load_out.wait()
            forward(0)
            m.nsend[1] = count_finish(0)
            count_start(1)
        if r == 1:
            swap(m.inputs, 0).wait()
            forward(1)
            m.nsend[2] = count_finish(1)
            count_start(2)
        if r == 2:
            m.total[...] = count_finish(2)

    turn(out_ref)
    lax.fori_loop(0, slots, pick_targets, 0, unroll=16)
    m.targets[0:slots] = in_order(picked_values(), m.order[...], 2)
    swap(m.targets, 1).start()
    backward(0, m.nrecv[0, gx][0:1, 0:1])
    swap(m.targets, 1).wait()
    backward(1, m.nrecv[0, high * 2 + 1 - core][0:1, 0:1])
    half = 512
    places = ((gz, lambda v: device(x=v)), (y, lambda v: device(y=v)))

    def ring(along, piece, relay, fin, send, sems):
        me, to = places[along]
        plus, minus, opposed = [lax.rem(me + d, 4) for d in (1, 3, 2)]
        begin, end = pl.ds(0, 2), pl.ds(2, 2)

        def copy(src, dst, out, into, peer):
            return remote(src, dst, sems.at[out], sems.at[into], to(peer))

        copies = [
            copy(piece(begin, opposed), relay.at[0], 0, 2, plus),
            copy(piece(end, opposed), relay.at[1], 0, 3, minus),
            copy(piece(end, plus), fin.at[0, end], 1, 4, plus),
            copy(piece(begin, minus), fin.at[1, begin], 1, 4, minus),
            copy(send.at[0], fin.at[0, begin], 1, 4, plus),
            copy(send.at[1], fin.at[1, end], 1, 4, minus),
        ]
        relays = copy(relay, relay, 0, 2, plus)
        fins = copy(fin, fin, 1, 4, plus)

        def open_ring():
            for one in copies[:4]:
                one.start()

        def pass_on():
            copies[0].wait_recv()
            send[0] = relay[0] + piece(begin, plus)[...]
            copies[4].start()
            copies[1].wait_recv()
            send[1] = relay[1] + piece(end, minus)[...]
            copies[5].start()

        def close_ring():
            fins.wait_recv()
            total = piece(pl.ds(0, 4), me)[...] + fin[0] + fin[1]
            relays.wait_send()
            fins.wait_send()
            return total

        return open_ring, pass_on, close_ring

    def piece1(batch, colour):
        def piece(part, owner):
            rows = pl.ds(pl.multiple_of(batch * 64 + owner * 16, 8), 16)
            return m.sums.at[part, rows, pl.ds(colour * half, half)]

        return piece

    def piece2(number):
        def piece(part, owner):
            lanes = pl.ds(pl.multiple_of(owner * LANES, LANES), LANES)
            return m.held1.at[number, part, :, lanes]

        return piece

    def rings_of(batch):
        one, two = [], []
        for colour in range(2):
            q = batch * 2 + colour
            one.append(
                ring(
                    colour,
                    piece1(batch, colour),
                    m.relay1.at[q],
                    m.fin1.at[q],
                    m.send1.at[q],
                    m.sems1.at[q],
                )
            )
            two.append(
                ring(
                    1 - colour,
                    piece2(q),
                    m.relay2.at[q],
                    m.fin2.at[q],
                    m.send2.at[q],
                    m.sems2.at[q],
                )
            )
        return one, two

    batches = [rings_of(batch) for batch in range(2)]

    def run(batch, stage, what, held=None):
        for colour, one in enumerate(batches[batch][stage]):
            value = one[what]()
            if held is not None:
                held[batch * 2 + colour] = value

    z_me = high * 2 + low

    def z_piece(batch, h, l):
        rows = pl.ds(pl.multiple_of(l * 8, 8), 8)
        return m.held2.at[pl.ds(batch * 2, 2), h, rows, :]

    z_peers = []
    for h, l in z_steps:
        ph, pw = lax.rem(high + h, 4), lax.rem(low + l, 2)
        z_peers.append((ph, pw, ph * 2 + pw, device(high=ph, low=pw)))

    def z_copy_out(batch, number):
        ph, pw, slot, peer = z_peers[number]
        return remote(
            z_piece(batch, ph, pw),
            m.zgot.at[z_me, batch],
            m.zp_send.at[batch],
            m.zp_recv.at[batch],
            peer,
        )

    def z_start(batch):
        for number in range(7):
            z_copy_out(batch, number).start()
        m.zgot[z_me, batch] = z_piece(batch, high, low)[...]

    def z_all(batch):
        others = m.zgot.at[0:7, batch]
        return remote(
            others, others, m.zp_send.at[batch], m.zp_recv.at[batch], z_peers[0][3]
        )

    grad_in = matmul(m.normed[...], m.dpre[...], ((0,), (0,)))
    for h in range(4):
        m.sums[h, 0:64] = grad_in[h * 64 : (h + 1) * 64]
    run(0, 0, 0)
    dout = m.dout[...]
    for h in range(4):
        block = pl.multiple_of((h * 2 + core) * LANES, LANES)
        grad_out = matmul(m.act[:, pl.ds(block, LANES)], dout, ((0,), (0,)))
        m.sums[h, 64:128, 0:512] = grad_out[0:64]
        m.sums[h, 64:128, 512:1024] = grad_out[64:128]
    run(1, 0, 0)
    run(0, 0, 1)
    run(1, 0, 1)
    run(0, 0, 2, m.held1)
    run(0, 1, 0)
    run(1, 0, 2, m.held1)
    run(1, 1, 0)
    run(0, 1, 1)
    run(1, 1, 1)
    run(0, 1, 2, m.held2)
    z_start(0)
    run(1, 1, 2, m.held2)
    z_start(1)
    g_me = (gz * 4 + y) * 2 + low
    g_peers = []
    for i, j, l in g_steps:
        px, py, pw = lax.rem(gz + i, 4), lax.rem(y + j, 4), lax.rem(low + l, 2)
        g_peers.append(((px * 4 + py) * 2 + pw, device(x=px, y=py, low=pw)))

    def g_copy(batch, number, slot):
        return remote(
            m.gathered.at[slot, batch],
            m.gathered.at[slot, batch],
            m.g_send.at[batch],
            m.g_recv.at[batch],
            g_peers[number][1],
        )

    for batch in range(2):
        z_all(batch).wait_recv()
        total = m.zgot[0, batch]
        for slot in range(1, 8):
            total = total + m.zgot[slot, batch]
        m.gathered[g_me, batch] = total
        for number in range(31):
            g_copy(batch, number, g_me).start()
    def g_all(batch):
        others = m.gathered.at[0:31, batch]
        return remote(
            others, others, m.g_send.at[batch], m.g_recv.at[batch], g_peers[0][1]
        )

    for batch in range(2):
        z_all(batch).wait_send()
    for batch in range(2):
        g_all(batch).wait_recv()
        sum_ref[:, batch] = m.gathered[:, batch]
    for batch in range(2):
        g_all(batch).wait_send()


def step(prev, now, material, table, used, anchors, w_in, w_out, sizes):
    X, Y, Z = now.shape
    W = Z + LANES
    T = W // LANES
    slots = anchors.shape[0]
    wide, hidden = w_in.shape
    vmem = pl.BlockSpec(memory_space=pltpu.VMEM)
    smem = pl.BlockSpec(memory_space=pltpu.SMEM)
    hbm = pl.BlockSpec(memory_space=pltpu.HBM)
    dma = pltpu.SemaphoreType.DMA
    most = max(sizes)

    def f32(*shape):
        return pltpu.VMEM(shape, F32)

    def b16(*shape):
        return pltpu.VMEM(shape, BF16)

    scratch = dict(
        A=f32(2 * PAD + (X + 4) * T * R, LANES),
        B=f32(2 * PAD + (X + 4) * T * R, LANES),
        C=f32((X + 2) * T * Y, LANES),
        D=f32((X + 2) * T * Y, LANES),
        now=f32(X, Y, Z),
        prev=f32(X, Y, Z),
        xsend=f32(2, 9, Y, LANES),
        xrecv=f32(2, 2, 9, Y, LANES),
        ysend=f32(2, 9, X, LANES),
        yrecv=f32(2, 2, 9, X, LANES),
        yold=f32(2, T, X, LANES),
        ycoef=f32(2, T, X, LANES),
        held_rows=f32(2, T, X, LANES),
        csend=f32(4, 1, W),
        crecv=f32(2, 4, 1, W),
        zsend=f32(2, 3, Y, LANES),
        zrecv=f32(2, 3, Y, LANES),
        nsend=f32(3, 8, LANES),
        nrecv=f32(3, most, 8, LANES),
        total=f32(8, LANES),
        rows=f32(Z // LANES, X * Y, LANES),
        turned=f32((X * Y // LANES + 1) * Z, LANES),
        picked=f32(8 * slots, LANES),
        mat=pltpu.VMEM((X, Y, Z), jnp.int32),
        where=pltpu.SMEM((2, slots), jnp.int32),
        order=b16(8 * LANES, wide),
        w_in=b16(wide, hidden),
        w_out=b16(hidden, wide),
        inputs=f32(2 * slots, wide),
        targets=f32(2 * slots, wide),
        base=f32(2 * slots, wide),
        normed=b16(2 * slots, wide // 2),
        act=b16(2 * slots, hidden),
        slope=f32(2 * slots, hidden),
        dout=b16(2 * slots, wide),
        dpre=b16(2 * slots, hidden),
        sums=f32(4, 128, 1024),
        relay1=f32(4, 2, 2, 16, 512),
        fin1=f32(4, 2, 4, 16, 512),
        send1=f32(4, 2, 2, 16, 512),
        held1=f32(4, 4, 16, 512),
        relay2=f32(4, 2, 2, 16, LANES),
        fin2=f32(4, 2, 4, 16, LANES),
        send2=f32(4, 2, 2, 16, LANES),
        held2=f32(4, 4, 16, LANES),
        zgot=f32(8, 2, 2, 8, LANES),
        gathered=f32(32, 2, 2, 8, LANES),
        load=dma((5,)),
        z_sem=dma((2, 2)),
        f_send=dma((12,)),
        f_recv=dma((2, 12)),
        n_send=dma((3,)),
        n_recv=dma((3,)),
        p_send=dma((2,)),
        p_recv=dma((2,)),
        sems1=dma((4, 5)),
        sems2=dma((4, 5)),
        zp_send=dma((2,)),
        zp_recv=dma((2,)),
        g_send=dma((2,)),
        g_recv=dma((2,)),
    )
    return pl.pallas_call(
        functools.partial(step_kernel, tuple(scratch), sizes),
        name="step",
        out_shape=(
            jax.ShapeDtypeStruct((X, Y, Z), F32),
            jax.ShapeDtypeStruct((32, 2, 2, 8, LANES), F32),
        ),
        in_specs=[hbm, hbm, hbm, smem, smem, smem, hbm, hbm],
        out_specs=(vmem, vmem),
        scratch_shapes=list(scratch.values()),
        compiler_params=pltpu.CompilerParams(
            collective_id=0,
            has_side_effects=True,
            vmem_limit_bytes=40 * 1024 * 1024,
        ),
    )(prev, now, material, table, used, anchors, w_in, w_out)


def place_kernel(final_ref, sum_ref, final_out, in_ref, out_ref):
    final_out[...] = final_ref[...]
    for slot in range(32):
        ix, iy, il = slot // 8, slot // 2 % 4, slot % 2
        for colour in range(2):
            one, two = (ix, iy) if colour == 0 else (iy, ix)
            top = one * 16 + il * 8
            at = two * LANES
            left = colour * 512 + at
            low = colour * 64 + top
            in_ref[top : top + 8, left : left + LANES] = sum_ref[slot, 0, colour]
            out_ref[low : low + 8, at : at + LANES] = sum_ref[slot, 1, colour]


def place(final, sums):
    vmem = pl.BlockSpec(memory_space=pltpu.VMEM)
    return pl.pallas_call(
        place_kernel,
        name="place",
        out_shape=(
            jax.ShapeDtypeStruct(final.shape, F32),
            jax.ShapeDtypeStruct((64, 1024), F32),
            jax.ShapeDtypeStruct((128, 512), F32),
        ),
        in_specs=[vmem, vmem],
        out_specs=(vmem, vmem, vmem),
        compiler_params=pltpu.CompilerParams(vmem_limit_bytes=8 * 1024 * 1024),
    )(final, sums)


def body(pressure_prev, pressure_now, material, speed_table, anchors, counts, w_in, w_out):
    sizes = tuple(lax.axis_size(axis) for axis in AXES)
    pressure_prev, pressure_now, material, speed_table, anchors, w_in, w_out = [
        pltpu.with_memory_space_constraint(v, pltpu.HBM)
        for v in (
            pressure_prev,
            pressure_now,
            material,
            speed_table,
            anchors.reshape(-1),
            w_in,
            w_out,
        )
    ]
    final, sums = step(
        pressure_prev,
        pressure_now,
        material,
        speed_table,
        counts.reshape(-1),
        anchors,
        w_in,
        w_out,
        sizes,
    )
    return place(final, sums)


def solution(mesh):
    return jax.shard_map(
        body,
        mesh=mesh,
        in_specs=(
            P("gx", "gy", "gz"),
            P("gx", "gy", "gz"),
            P("gx", "gy", "gz"),
            P(),
            P("gx", "gy", "gz"),
            P("gx", "gy", "gz"),
            P(),
            P(),
        ),
        out_specs=(P("gx", "gy", "gz"), P("gx", None), P("gx", None)),
        check_vma=False,
    )
```
